32 devices in a mesh: dp: 8 (over y, x, core), shard: 4 (over z).
Axes of the slice: x: 2, y: 2, z: 4, core: 2. Of those that a mesh axis runs over, the one named last changes fastest.
Arguments:
- tokens: bfloat16 [8192, 2048], P(('dp', 'shard')), may hold values from -6 to 6
- doc_lengths: int32 [32, 4], P(('dp', 'shard')), may hold values from 1 to 128, 256 in all within a row
- weights: float32 [2048, 192, 128], P(('dp', 'shard')), may hold values from -2 to 2
- momentum: float32 [2048, 192, 128], P(('dp', 'shard')), may hold values from -8192 to 8192
- vectors: float32 [2048, 12], P(('dp', 'shard')), may hold values from -2 to 2
- vector_moment: float32 [2048, 12], P(('dp', 'shard')), may hold values from -8192 to 8192
- vector_second: float32 [2048, 12], P(('dp', 'shard')), may hold values from 0 to 8192, as said below
- cotangent: bfloat16 [8192, 2048], P(('dp', 'shard')), may hold values from -6 to 6
Outputs:
- layer_output: bfloat16 [8192, 2048], P(('dp', 'shard'))
- input_gradient: float32 [8192, 2048], P(('dp', 'shard'))
- weight_gradient: float32 [2048, 192, 128], P(('dp', 'shard'))
- new_weights: float32 [2048, 192, 128], P(('dp', 'shard'))
- new_momentum: float32 [2048, 192, 128], P(('dp', 'shard'))
- next_moment: float32 [2048, 12], P(('dp', 'shard'))
- next_second: float32 [2048, 12], P(('dp', 'shard'))
- next_vectors: float32 [2048, 12], P(('dp', 'shard'))
The draws below stay inside these ranges and needn't reach their ends.
Inputs may be any that keep to these rules, and one draw needn't show every extreme that they name: `doc_lengths`: in each row the first 3 entries are sequence lengths and the last is the padding at the row's end; a row sums to 256 and its largest entry is exactly 128. `vector_second`: positive.
All inputs are finite; a program needn't handle non-finite values.
Results may differ from the reference program's by a relative error of at most 0.019.
Values may be sent and summed in bfloat16 or wider, within the bound.
A program may use at most 832 MiB of HBM per device.

```python
import math
from functools import partial
import jax
import jax.numpy as jnp
import numpy as np
from jax import lax

D = 2048
HEADS = 16
HEAD = 128
FF = 8192
T_DEV = 256
DOCS = 4
NS_ITERS = 5
STEP = 10
NB = 192
VROWS = 12
TOKENS = 8192
DEVICES = 32


def block_scale():
    number = jnp.arange(NB)
    unit_scale = D ** (-0.5)
    return jnp.where(number < 3 * HEADS, unit_scale, jnp.where(number < 4 * HEADS, 5.0 * unit_scale, jnp.where(number < 4 * HEADS + FF // HEAD, unit_scale, 2.0 * FF ** (-0.5))))


def draw_weights(key, part):
    drawn = jnp.clip(jax.random.normal(jax.random.fold_in(key, 11), (D, NB, HEAD), jnp.float32), -3.5, 3.5)
    return drawn * block_scale()[None, :, None]


def draw_momentum(key, part):
    drawn = jnp.clip(jax.random.normal(jax.random.fold_in(key, 21), (D, NB, HEAD), jnp.float32), -6.0, 6.0)
    return drawn * 0.3 * math.sqrt(TOKENS)


def draw_vectors(key, part):
    column = jnp.arange(VROWS)
    gain_values = 1.0 + jax.random.uniform(jax.random.fold_in(key, 31), (D, VROWS), jnp.float32, -0.3, 0.3)
    bias_values = 0.2 * jnp.clip(jax.random.normal(jax.random.fold_in(key, 32), (D, VROWS), jnp.float32), -6.0, 6.0)
    gain_column = (column == 0) | (column == 2)
    return jnp.where(gain_column[None, :], gain_values, bias_values)


def draw_vector_moment(key, part):
    drawn = jnp.clip(jax.random.normal(jax.random.fold_in(key, 41), (D, VROWS), jnp.float32), -6.0, 6.0)
    return drawn * 0.11 * math.sqrt(TOKENS)


def draw_vector_second(key, part):
    factor = jnp.exp(jax.random.uniform(jax.random.fold_in(key, 51), (D, VROWS), jnp.float32) * math.log(4.0))
    return factor * (0.05 / 0.95) * TOKENS


def strengthened(result, stream_key, source, target, parts, factor):
    owner, partner = [(jnp.arange(result.shape[position]) // (result.shape[position] // parts)).reshape([-1 if axis == position else 1 for axis in range(result.ndim)]) for position in (source, target)]
    chosen = jax.random.permutation(stream_key, parts)[partner]
    strong = (owner == chosen) | (owner == (partner + parts // 2) % parts)
    return jnp.where(strong, factor * result, result)


def level_of(own_key, shape, pieces, least, high):
    gain = 1.0
    for axis_at, parts in pieces:
        steps = jax.random.uniform(jax.random.fold_in(jax.random.fold_in(own_key, 6), axis_at), (parts,), jnp.float32, least / len(pieces), high / len(pieces))
        gain = gain * jnp.repeat(jnp.exp(steps), shape[axis_at] // parts).reshape((-1,) + (1,) * (len(shape) - 1 - axis_at))
    return gain


def length_profile(count, total, most, skew):
    loads = [(1 << 20) // math.isqrt(rank ** skew) + 1 for rank in range(2, count + 1)]
    surplus, counts = total - most - (count - 1), [1] * (count - 1)
    while surplus > 0:
        movable = [i for i in range(count - 1) if counts[i] < most]
        whole, remaining = sum([loads[i] for i in movable]), surplus
        for i in movable:
            addition = min(most - counts[i], max(1, remaining * loads[i] // whole), surplus)
            counts[i] = counts[i] + addition
            surplus = surplus - addition
    return np.array([most] + counts)


def uneven_parts(rng, number_of, total, most, lean):
    if number_of == 2:
        one = jax.random.randint(rng, (), max(1, total - most), min(most, total - 1) + 1)
        return jnp.stack([one, total - one])
    sizes = jnp.asarray(length_profile(number_of, total, most, lean), jnp.int32)
    couples = (number_of - 1) // 2
    source_of, sink = sizes[1:1 + 2 * couples:2], sizes[2:2 + 2 * couples:2]
    room = jnp.minimum(source_of - 1, most - sink)
    moved = jax.random.randint(jax.random.fold_in(rng, 1), (couples,), 0, 1 << 20) % (room + 1)
    sizes = sizes.at[1:1 + 2 * couples:2].set(source_of - moved).at[2:2 + 2 * couples:2].set(sink + moved)
    return sizes[jax.random.permutation(jax.random.fold_in(rng, 2), number_of)]


def gaussian(stream_key, shape, deviation, reach, cuts=(), held_as=jnp.bfloat16):
    values = deviation * jax.random.normal(stream_key, shape, jnp.float32)
    if cuts:
        values = values * level_of(stream_key, shape, cuts, -0.22, 0.18)
    return jnp.clip(values, -reach, reach).astype(held_as)


def gaussian_with(rng, shape, deviation, reach, split, heavy, kind=jnp.bfloat16):
    result = deviation * jax.random.normal(rng, shape, jnp.float32)
    if split:
        result = result * level_of(rng, shape, split, -0.22, 0.18)
    return jnp.clip(strengthened(result, jax.random.fold_in(rng, 3), *heavy), -reach, reach).astype(kind)


def setup_inputs(seed: int = 0) -> dict:
    arg_keys = jax.random.split(jax.random.key(seed), 9)
    tokens = gaussian(arg_keys[0], (TOKENS, D), 1.0, 6.0, ((0, 32),))
    doc_lengths = jax.vmap(lambda own: uneven_parts(own, DOCS, T_DEV, T_DEV // 2, 0))(jax.random.split(arg_keys[1], DEVICES)).reshape((DEVICES, DOCS)).astype(jnp.int32)
    weights = draw_weights(jax.random.fold_in(arg_keys[8], 71), 0)
    momentum = draw_momentum(jax.random.fold_in(arg_keys[8], 71), 0)
    vectors = draw_vectors(jax.random.fold_in(arg_keys[8], 71), 0)
    vector_moment = draw_vector_moment(jax.random.fold_in(arg_keys[8], 71), 0)
    vector_second = draw_vector_second(jax.random.fold_in(arg_keys[8], 71), 0)
    cotangent = gaussian_with(arg_keys[7], (TOKENS, D), 1.0, 6.0, ((0, 32),), (0, 1, 32, 2.75))
    return {"tokens": tokens, "doc_lengths": doc_lengths, "weights": weights, "momentum": momentum, "vectors": vectors, "vector_moment": vector_moment, "vector_second": vector_second, "cotangent": cotangent}


HIGHEST = lax.Precision.HIGHEST
COEF_A = 3.4445
COEF_B = -4.775
COEF_C = 2.0315

@jax.custom_vjp
def low(v):
    return lax.optimization_barrier(v.astype(jnp.bfloat16)).astype(jnp.float32)

@jax.custom_vjp
def low_back(v):
    return v

def low_keep(v):
    return (low(v), None)

def low_pass(kept, grad):
    return (grad,)

def back_keep(v):
    return (v, None)

def back_low(kept, grad):
    return (low(grad),)
low.defvjp(low_keep, low_pass)
low_back.defvjp(back_keep, back_low)

def layer_norm(values, gain_row, shift_row):
    average = lax.optimization_barrier(jnp.mean(values, axis=-1, keepdims=True))
    centered = values - average
    variance = lax.optimization_barrier(jnp.mean(centered * centered, axis=-1, keepdims=True))
    return centered * lax.rsqrt(variance + 1e-05) * gain_row + shift_row

def allowed_mask(length_rows, row_length):
    boundary = jnp.cumsum(length_rows, axis=-1)
    places = jnp.arange(row_length, dtype=jnp.int32)
    segment = lax.optimization_barrier(jnp.sum((places[None, :, None] >= boundary[:, None, :]).astype(jnp.int32), axis=-1))
    same_span = segment[:, :, None] == segment[:, None, :]
    causal = places[:, None] >= places[None, :]
    padded = segment[:, :, None] == length_rows.shape[-1] - 1
    diagonal = places[:, None] == places[None, :]
    return same_span & causal[None] & (jnp.logical_not(padded) | diagonal[None])

def layer_group(weight_low, vector_low, token_rows, allowed):
    inner_count = FF // HEAD
    bias_query = vector_low[:, 4].reshape(HEADS, HEAD)
    bias_value = vector_low[:, 5].reshape(HEADS, HEAD)
    bias_up = vector_low[:, 8:].T.reshape(inner_count, HEAD)
    normed_one = low(layer_norm(token_rows, vector_low[:, 0], vector_low[:, 1]))
    joined = jnp.einsum('rtd,dhc->rthc', normed_one, weight_low[:, :3 * HEADS], precision=HIGHEST)
    queries = low(low_back(joined[:, :, :HEADS] + bias_query))
    key_rows = low(low_back(joined[:, :, HEADS:2 * HEADS]))
    value_rows = low(low_back(joined[:, :, 2 * HEADS:] + bias_value))
    scores = jnp.einsum('rqhc,rkhc->rhqk', queries, key_rows, precision=HIGHEST) * HEAD ** (-0.5)
    scores = low_back(scores)
    scores = jnp.where(allowed[:, None], scores, -1e+30)
    row_peak = lax.optimization_barrier(jnp.max(scores, axis=-1, keepdims=True))
    exponent = jnp.exp(scores - row_peak)
    probability = low(exponent / lax.optimization_barrier(jnp.sum(exponent, axis=-1, keepdims=True)))
    attended = jnp.einsum('rhqk,rkhc->rqhc', probability, value_rows, precision=HIGHEST)
    attended = low(low_back(attended))
    branch = jnp.einsum('rthc,dhc->rtd', attended, weight_low[:, 3 * HEADS:4 * HEADS], precision=HIGHEST) + vector_low[:, 6]
    branch = low_back(branch)
    middle = token_rows + branch
    normed_two = low(layer_norm(middle, vector_low[:, 2], vector_low[:, 3]))
    before = jnp.einsum('rtd,djc->rtjc', normed_two, weight_low[:, 4 * HEADS:4 * HEADS + inner_count], precision=HIGHEST) + bias_up
    before = low_back(before)
    activated = low(jax.nn.gelu(before, approximate=True))
    branch_two = jnp.einsum('rtjc,djc->rtd', activated, weight_low[:, 4 * HEADS + inner_count:], precision=HIGHEST) + vector_low[:, 7]
    branch_two = low_back(branch_two)
    return middle + branch_two

def reference(tokens, doc_lengths, weights, momentum, vectors, vector_moment, vector_second, cotangent):
    count_rows = doc_lengths.shape[0]
    allowed = allowed_mask(doc_lengths, T_DEV)
    group_rows = 1
    while group_rows * 2 <= max(1, 4096 // T_DEV) and count_rows % (group_rows * 2) == 0:
        group_rows = group_rows * 2
    stacked_masks = allowed.reshape(count_rows // group_rows, group_rows, T_DEV, T_DEV)

    def forward(token_values, weight_values, vector_values):
        weight_low = low(weight_values)
        vector_low = low(vector_values)
        checked = jax.checkpoint(partial(layer_group, weight_low, vector_low))

        def scan_step(state_carry, inputs_pair):
            return (state_carry, checked(inputs_pair[0], inputs_pair[1]))
        stacked = token_values.reshape(count_rows // group_rows, group_rows, T_DEV, D)
        unused, results = lax.scan(scan_step, None, (stacked, stacked_masks))
        return results.reshape(count_rows * T_DEV, D)
    outputs, pullback = jax.vjp(forward, tokens.astype(jnp.float32), weights, vectors)
    grad_tokens, grad_weights, grad_vectors = pullback(cotangent.astype(jnp.float32))
    moment_new = 0.95 * momentum + grad_weights
    squares = lax.optimization_barrier(jnp.sum(moment_new * moment_new, axis=(0, 2)))
    current = moment_new / (jnp.sqrt(squares) + 1e-07)[None, :, None]
    for number in range(NS_ITERS):
        gram_matrix = jnp.einsum('rkc,rke->kce', current, current, precision=HIGHEST)
        square = jnp.einsum('kce,kef->kcf', gram_matrix, gram_matrix, precision=HIGHEST)
        polynomial = COEF_B * gram_matrix + COEF_C * square
        current = COEF_A * current + jnp.einsum('rkc,kce->rke', current, polynomial, precision=HIGHEST)
    new_weights = weights * (1.0 - 0.15 * 0.1) - 0.15 * 0.2 * math.sqrt(D) * current
    first_moment = 0.9 * vector_moment + 0.1 * grad_vectors
    second = 0.95 * vector_second + 0.05 * grad_vectors * grad_vectors
    corrected = first_moment / (1.0 - 0.9 ** STEP)
    normal_second = second / (1.0 - 0.95 ** STEP)
    next_vectors = vectors - 0.5 * corrected / (jnp.sqrt(normal_second) + 1e-08)
    return (outputs.astype(jnp.bfloat16), grad_tokens, grad_weights, new_weights, moment_new, first_moment, second, next_vectors)
```

```python
from functools import partial
import math

import jax
import jax.numpy as jnp
from jax import lax
from jax.sharding import Mesh, PartitionSpec as P

HEADS = 16
HEAD = 128
NS_ITERS = 5
STEP = 10

COEF_A = 3.4445
COEF_B = -4.775
COEF_C = 2.0315
BF = jnp.bfloat16
F32 = jnp.float32
ALL = ("hi", "tp", "shard")
FS = ("hi", "shard")


def dot(spec, a, b, **kw):
    return jnp.einsum(spec, a, b, preferred_element_type=F32, **kw)


def layer_norm(values, gain_row, shift_row):
    average = jnp.mean(values, axis=-1, keepdims=True)
    centered = values - average
    variance = jnp.mean(centered * centered, axis=-1, keepdims=True)
    return centered * lax.rsqrt(variance + 1e-05) * gain_row + shift_row


def allowed_mask(length_rows, row_length):
    ends = [length_rows[:, 0]]
    for span in range(1, length_rows.shape[-1]):
        ends.append(ends[-1] + length_rows[:, span])
    boundary = jnp.stack(ends, axis=-1)
    places = jnp.arange(row_length, dtype=jnp.int32)
    segment = jnp.sum((places[None, :, None] >= boundary[:, None, :]).astype(jnp.int32), axis=-1)
    same_span = segment[:, :, None] == segment[:, None, :]
    causal = places[:, None] >= places[None, :]
    padded = segment[:, :, None] == length_rows.shape[-1] - 1
    diagonal = places[:, None] == places[None, :]
    return same_span & causal[None] & (jnp.logical_not(padded) | diagonal[None])


def newton_schulz(current):
    def ein(spec, a, b):
        return jnp.einsum(spec, a, b, precision=lax.Precision.HIGH, preferred_element_type=F32)
    total = jnp.sum(current * current, axis=(0, 2))
    current = current * (1.0 / (jnp.sqrt(total) + 1e-07))[None, :, None]
    for number in range(NS_ITERS):
        gram = ein("rkc,rke->kce", current, current)
        square = ein("kce,kef->kcf", gram, gram)
        polynomial = COEF_B * gram + COEF_C * square
        current = COEF_A * current + ein("rkc,kce->rke", current, polynomial)
    return current


def local(tokens, doc_lengths, weights, momentum, vectors, vector_moment, vector_second, cotangent):
    hi, tp, sh = (lax.axis_size(a) for a in ALL)
    groups, world = hi * sh, hi * tp * sh
    rows, blocks, head = weights.shape
    row_tokens, d = tokens.shape
    heads = HEADS // tp
    inner_all = (blocks - 4 * HEADS) // 2
    inner = inner_all // tp
    attn_blocks = 4 * heads
    me = lax.axis_index("tp")
    t_all = tp * row_tokens

    low = weights.astype(BF)
    attn_send = low[:, : 4 * HEADS].reshape(rows, 4, tp, heads, head).transpose(2, 0, 1, 3, 4).reshape(tp, rows, attn_blocks * head)
    mlp_send = low[:, 4 * HEADS :].reshape(rows, 2, tp, inner, head).transpose(2, 0, 1, 3, 4).reshape(tp, rows, 2 * inner * head)

    def rows_in_order(gathered):
        n = gathered.shape[-1]
        return gathered.reshape(hi, sh, tp, rows, n).transpose(0, 2, 1, 3, 4).reshape(d, n)

    def spread(array):
        swapped = lax.all_to_all(array, "tp", split_axis=0, concat_axis=0, tiled=True)
        return rows_in_order(lax.all_gather(swapped, FS, axis=0, tiled=False))

    w_attn = spread(attn_send)
    w_mlp = spread(mlp_send)
    vec = lax.all_gather(vectors.astype(BF), "tp", axis=0, tiled=False)
    vec = lax.all_gather(vec, FS, axis=0, tiled=False)
    vec = vec.reshape(hi, sh, tp, rows, -1).transpose(0, 2, 1, 3, 4).reshape(d, -1).astype(F32)

    tok_all = lax.all_gather(tokens, "tp", axis=0, tiled=True)
    cot_all = lax.all_gather(cotangent, "tp", axis=0, tiled=True)
    lengths = lax.all_gather(doc_lengths, "tp", axis=0, tiled=True)
    allowed = allowed_mask(lengths, row_tokens)

    def per_of(count):
        return -(-count // groups)

    def to_owners(part, count):
        per = per_of(count)
        part = jnp.pad(part, ((0, 0), (0, 0), (0, per * groups - count), (0, 0)))
        part = part.reshape(rows, tp, hi, sh, per * head)
        return part.transpose(2, 1, 3, 0, 4)

    def split(array):
        attn = array[:, : 4 * HEADS].reshape(rows, 4, tp, heads, head).transpose(0, 2, 1, 3, 4).reshape(rows, tp, attn_blocks, head)
        mlp = array[:, 4 * HEADS :].reshape(rows, 2, tp, inner, head)
        return ((attn, attn_blocks), (mlp[:, 0], inner), (mlp[:, 1], inner))

    mom_send = jnp.concatenate([to_owners(p, c) for p, c in split(momentum.astype(BF))], axis=-1)
    width = mom_send.shape[-1]
    mom_mine = lax.all_to_all(mom_send.reshape(world, rows, width), ALL, split_axis=0, concat_axis=0, tiled=True)
    mom_mine = mom_mine.reshape(d, width)

    bias_q = lax.dynamic_slice(vec[:, 4], (me * heads * head,), (heads * head,))
    bias_v = lax.dynamic_slice(vec[:, 5], (me * heads * head,), (heads * head,))
    bias_up = lax.dynamic_slice(vec[:, 8:].T.reshape(-1), (me * inner * head,), (inner * head,))
    hc = heads * head
    w_qkv, w_out = w_attn[:, : 3 * hc], w_attn[:, 3 * hc :]
    w_up, w_down = w_mlp[:, : inner * head], w_mlp[:, inner * head :]

    normed_one = layer_norm(tok_all.astype(F32), vec[:, 0], vec[:, 1]).astype(BF)
    joined = dot("td,dn->tn", normed_one, w_qkv)

    def per_head(values):
        return values.reshape(tp, row_tokens, heads, head)

    queries = per_head((joined[:, :hc] + bias_q).astype(BF))
    key_rows = per_head(joined[:, hc : 2 * hc].astype(BF))
    value_rows = per_head((joined[:, 2 * hc :] + bias_v).astype(BF))
    scores = dot("rqhc,rkhc->rhqk", queries, key_rows) * head ** (-0.5)
    scores = jnp.where(allowed[:, None], scores, -1e30)
    row_peak = jnp.max(scores, axis=-1, keepdims=True)
    exponent = jnp.exp(scores - row_peak)
    probability = exponent / jnp.sum(exponent, axis=-1, keepdims=True)
    probability_low = probability.astype(BF)
    attended = dot("rhqk,rkhc->rqhc", probability_low, value_rows).astype(BF).reshape(t_all, hc)

    def own_sum(partial_rows):
        return lax.psum_scatter(partial_rows.astype(BF), "tp", scatter_dimension=0, tiled=True).astype(F32)

    branch = own_sum(dot("tc,dc->td", attended, w_out)) + vec[:, 6]
    token_values = tokens.astype(F32)
    middle = token_values + branch
    normed_two_own = layer_norm(middle, vec[:, 2], vec[:, 3]).astype(BF)
    normed_two = lax.all_gather(normed_two_own, "tp", axis=0, tiled=True)
    before = dot("td,dn->tn", normed_two, w_up) + bias_up
    grad_activated = dot("td,dn->tn", cot_all, w_down)
    gelu_value, gelu_back = jax.vjp(partial(jax.nn.gelu, approximate=True), before)
    activated = gelu_value.astype(BF)
    grad_before = gelu_back(grad_activated)[0].astype(BF)

    grad_normed_two = own_sum(dot("tn,dn->td", grad_before, w_up))
    _, norm_back_two = jax.vjp(layer_norm, middle, vec[:, 2], vec[:, 3])
    grad_middle_part, grad_gain_two, grad_shift_two = norm_back_two(grad_normed_two)
    grad_middle = cotangent.astype(F32) + grad_middle_part
    grad_branch_own = grad_middle.astype(BF)
    grad_branch = lax.all_gather(grad_branch_own, "tp", axis=0, tiled=True)
    output = middle + own_sum(dot("tn,dn->td", activated, w_down)) + vec[:, 7]
    grad_attended = dot("td,dc->tc", grad_branch, w_out).astype(BF)
    grad_att = per_head(grad_attended)
    grad_prob = dot("rqhc,rkhc->rhqk", grad_att, value_rows)
    row_total = jnp.sum(probability * grad_prob, axis=-1, keepdims=True)
    grad_scores = (probability * (grad_prob - row_total)).astype(BF)
    scale = head ** (-0.5)
    grad_q = (dot("rhqk,rkhc->rqhc", grad_scores, key_rows) * scale).astype(BF).reshape(t_all, hc)
    grad_k = (dot("rhqk,rqhc->rkhc", grad_scores, queries) * scale).astype(BF).reshape(t_all, hc)
    grad_v = dot("rhqk,rqhc->rkhc", probability_low, grad_att).astype(BF).reshape(t_all, hc)
    grad_joined = jnp.concatenate([grad_q, grad_k, grad_v], axis=1)
    grad_normed_one = own_sum(dot("tn,dn->td", grad_joined, w_qkv))
    _, norm_back_one = jax.vjp(layer_norm, token_values, vec[:, 0], vec[:, 1])
    grad_tokens_part, grad_gain_one, grad_shift_one = norm_back_one(grad_normed_one)
    grad_tokens = grad_middle + grad_tokens_part

    def to_block_owners(left_right, count):
        per = per_of(count)
        parts = [dot("td,tn->dn", a, b).astype(BF) for a, b in left_right]
        joined_part = parts[0] if len(parts) == 1 else jnp.concatenate(parts, axis=1)
        joined_part = jnp.pad(joined_part, ((0, 0), (0, (per * groups - count) * head)))
        stacked = joined_part.reshape(d, groups, per * head).transpose(1, 0, 2)
        return lax.psum_scatter(stacked, FS, scatter_dimension=0, tiled=False)

    g_down = to_block_owners([(cot_all, activated)], inner)
    g_up = to_block_owners([(normed_two, grad_before)], inner)
    g_attn = to_block_owners([(normed_one, grad_joined), (grad_branch, attended)], attn_blocks)
    g_mine = jnp.concatenate([g_attn, g_up, g_down], axis=1)

    def to_row_owners(mine):
        back = lax.all_to_all(mine.astype(BF).reshape(world, rows, width), ALL, split_axis=0, concat_axis=0, tiled=True)
        back = back.reshape(hi, tp, sh, rows, width)
        pieces, at = [], 0
        for number, count in enumerate((attn_blocks, inner, inner)):
            per = per_of(count)
            piece = back[..., at : at + per * head].reshape(hi, tp, sh, rows, per, head)
            at += per * head
            piece = piece.transpose(3, 1, 0, 2, 4, 5).reshape(rows, tp, groups * per, head)[:, :, :count]
            if number == 0:
                piece = piece.reshape(rows, tp, 4, heads, head).transpose(0, 2, 1, 3, 4)
            pieces.append(piece.reshape(rows, -1, head))
        return jnp.concatenate(pieces, axis=1)

    weight_grad = to_row_owners(g_mine).astype(F32)
    moment_new = 0.95 * momentum + weight_grad

    moment_mine = 0.95 * mom_mine.astype(F32) + g_mine.astype(F32)
    orthogonal = newton_schulz(moment_mine.reshape(d, width // head, head)).reshape(d, width)
    orthogonal_rows = to_row_owners(orthogonal).astype(F32)
    new_weights = weights * (1.0 - 0.15 * 0.1) - 0.15 * 0.2 * math.sqrt(d) * orthogonal_rows

    plain = jnp.stack(
        [
            grad_gain_one,
            grad_shift_one,
            grad_gain_two,
            grad_shift_two,
            jnp.zeros((d,), F32),
            jnp.zeros((d,), F32),
            jnp.sum(grad_branch_own, axis=0, dtype=F32),
            jnp.sum(cotangent, axis=0, dtype=F32),
        ],
        axis=0,
    )
    plain = lax.dynamic_update_slice(plain, jnp.sum(grad_q, axis=0, dtype=F32)[None], (4, me * hc))
    plain = lax.dynamic_update_slice(plain, jnp.sum(grad_v, axis=0, dtype=F32)[None], (5, me * hc))
    hidden = jnp.zeros((inner_all * head,), F32)
    hidden = lax.dynamic_update_slice(hidden, jnp.sum(grad_before, axis=0, dtype=F32), (me * inner * head,))
    terms = jnp.concatenate([plain, hidden.reshape(-1, d)], axis=0)
    terms = terms.reshape(-1, world, rows).transpose(1, 0, 2).reshape(world, -1)
    vector_grad = jnp.sum(lax.all_to_all(terms, ALL, split_axis=0, concat_axis=0, tiled=True), axis=0)
    vector_grad = vector_grad.reshape(-1, rows).T
    first_moment = 0.9 * vector_moment + 0.1 * vector_grad
    second = 0.95 * vector_second + 0.05 * vector_grad * vector_grad
    corrected = first_moment / (1.0 - 0.9**STEP)
    normal_second = second / (1.0 - 0.95**STEP)
    next_vectors = vectors - 0.5 * corrected / (jnp.sqrt(normal_second) + 1e-08)
    return (
        output.astype(BF),
        grad_tokens,
        weight_grad,
        new_weights,
        moment_new,
        first_moment,
        second,
        next_vectors,
    )


def solution(mesh):
    dp, sh = mesh.shape["dp"], mesh.shape["shard"]
    tp = math.gcd(dp, 8)
    fine = Mesh(mesh.devices.reshape(dp // tp, tp, sh), ALL)
    two, three = P(ALL, None), P(ALL, None, None)
    return jax.shard_map(
        local,
        mesh=fine,
        in_specs=(two, two, three, three, two, two, two, two),
        out_specs=(two, two, three, three, three, two, two, two),
        check_vma=False,
    )
```

```python
from functools import partial
import math

import jax
import jax.numpy as jnp
from jax import lax
from jax.experimental import pallas as pl
from jax.experimental.pallas import tpu as pltpu
from jax.sharding import Mesh, PartitionSpec as P

HEADS = 16
HEAD = 128
NS_ITERS = 5
STEP = 10

COEF_A = 3.4445
COEF_B = -4.775
COEF_C = 2.0315
BF = jnp.bfloat16
F32 = jnp.float32
ALL = ("hi", "tp", "shard")
FS = ("hi", "shard")


MESH = pl.DeviceIdType.MESH
WIDE = 256


def rem(a, b):
    return lax.rem(a, jnp.int32(b))


def div(a, b):
    return lax.div(a, jnp.int32(b))


def spots():
    me = lax.axis_index("tp")
    c, x, y = rem(me, 2), rem(div(me, 2), 2), div(me, 4)
    return me, c, x, y, me + 1 - 2 * c, me + 2 - 4 * x, me + 4 - 8 * y


def meet(peers):
    barrier = pltpu.get_barrier_semaphore()
    for peer in peers:
        pl.semaphore_signal(barrier, inc=1, device_id={"tp": peer}, device_id_type=MESH)
    pl.semaphore_wait(barrier, len(peers))


def remote(src, dst, send, recv, peer):
    return pltpu.make_async_remote_copy(
        src_ref=src, dst_ref=dst, send_sem=send, recv_sem=recv, device_id={"tp": peer}, device_id_type=MESH
    )


def sum_scratch(rows, width):
    count = width // WIDE
    return [
        pltpu.VMEM((count, 2, 2, 2, rows, WIDE), BF),
        pltpu.VMEM((count, 2, 2, rows, WIDE), BF),
        pltpu.VMEM((count, 2, rows, WIDE), BF),
        pltpu.VMEM((count, rows, WIDE), BF),
        pltpu.SemaphoreType.DMA((3, count)),
        pltpu.SemaphoreType.DMA((3, count)),
    ]


class Summing:
    def __init__(self, left, right, total, scratch):
        self.left, self.right, self.total = left, right, total
        self.part, self.from_c, self.from_1, self.from_2, self.send, self.recv = scratch
        self.count = self.part.shape[0]
        self.rows = self.part.shape[4]
        self.copies = {}

    def fill(self, k):
        right = self.right[k * WIDE : (k + 1) * WIDE, :]

        def one(dest, carry):
            rows = self.left[pl.ds(pl.multiple_of(dest * self.rows, self.rows), self.rows), :]
            made = lax.dot_general(rows, right, (((1,), (1,)), ((), ())), preferred_element_type=F32)
            self.part[k, div(dest, 4), rem(div(dest, 2), 2), rem(dest, 2)] = made.astype(BF)
            return carry

        lax.fori_loop(0, 8, one, 0)

    def begin(self, stage, k, src, dst, peer):
        copy = remote(src, dst, self.send.at[stage, k], self.recv.at[stage, k], peer)
        copy.start()
        self.copies[stage, k] = copy

    def run(self):
        me, c, x, y, pc, px, py = spots()
        oc, ox, oy = 1 - c, 1 - x, 1 - y
        part = self.part

        def core_stage(k):
            self.copies[0, k].wait_recv()
            for i in range(4):
                a, b = i // 2, i % 2
                part[k, a, b, c] = (part[k, a, b, c].astype(F32) + self.from_c[k, a, b].astype(F32)).astype(BF)
            if k % 2 == 0:
                self.begin(1, k, part.at[k, :, ox, c], self.from_1.at[k], px)
            else:
                self.begin(1, k, part.at[k, oy, :, c], self.from_1.at[k], py)

        for k in range(self.count):
            self.fill(k)
            self.begin(0, k, part.at[k, :, :, oc], self.from_c.at[k], pc)
            if k:
                core_stage(k - 1)
        core_stage(self.count - 1)
        for k in range(self.count):
            self.copies[1, k].wait_recv()
            for i in range(2):
                if k % 2 == 0:
                    part[k, i, x, c] = (part[k, i, x, c].astype(F32) + self.from_1[k, i].astype(F32)).astype(BF)
                else:
                    part[k, y, i, c] = (part[k, y, i, c].astype(F32) + self.from_1[k, i].astype(F32)).astype(BF)
            if k % 2 == 0:
                self.begin(2, k, part.at[k, oy, x, c], self.from_2.at[k], py)
            else:
                self.begin(2, k, part.at[k, y, ox, c], self.from_2.at[k], px)
        for k in range(self.count):
            self.copies[2, k].wait_recv()
            self.total[:, k * WIDE : (k + 1) * WIDE] = part[k, y, x, c].astype(F32) + self.from_2[k].astype(F32)

    def end(self):
        for copy in self.copies.values():
            copy.wait_send()


class Gathering:
    def __init__(self, own, out, send, recv, local):
        self.own, self.out, self.send, self.recv, self.local = own, out, send, recv, local
        self.copies = []

    def begin(self, src, dst, peer):
        n = len(self.copies)
        copy = remote(src, dst, self.send.at[n], self.recv.at[n], peer)
        copy.start()
        self.copies.append(copy)
        return copy

    def start(self):
        me, c, x, y, pc, px, py = spots()
        self.spots = me, px, py, pc
        own, out = self.own, self.out
        half = own.shape[-1] // 2
        self.low, self.high = pl.ds(0, half), pl.ds(half, half)
        low, high = self.low, self.high
        self.px_high = self.begin(own.at[:, high], out.at[me, :, high], px)
        self.py_low = self.begin(own.at[:, low], out.at[me, :, low], py)
        self.begin(own, out.at[me], pc)
        self.px_low = self.begin(own.at[:, low], out.at[me, :, low], px)
        self.py_high = self.begin(own.at[:, high], out.at[me, :, high], py)
        self.kept = pltpu.make_async_copy(own, out.at[me], self.local)
        self.kept.start()

    def forward(self):
        me, px, py, pc = self.spots
        out, low, high = self.out, self.low, self.high
        across = px + py - me
        self.px_high.wait_recv()
        a = self.begin(out.at[px, :, high], out.at[px, :, high], py)
        self.begin(out.at[px, :, high], out.at[px, :, high], pc)
        self.py_low.wait_recv()
        b = self.begin(out.at[py, :, low], out.at[py, :, low], px)
        self.begin(out.at[py, :, low], out.at[py, :, low], pc)
        self.px_low.wait_recv()
        self.begin(out.at[px, :, low], out.at[px, :, low], pc)
        self.py_high.wait_recv()
        self.begin(out.at[py, :, high], out.at[py, :, high], pc)
        a.wait_recv()
        self.begin(out.at[across, :, high], out.at[across, :, high], pc)
        b.wait_recv()
        self.begin(out.at[across, :, low], out.at[across, :, low], pc)
        self.seen = (0, 1, 3, 4, 5, 7)

    def end(self):
        for n, copy in enumerate(self.copies):
            if n not in self.seen:
                copy.wait_recv()
            copy.wait_send()
        self.kept.wait()


def gather_scratch():
    return [pltpu.SemaphoreType.DMA((13,)), pltpu.SemaphoreType.DMA((13,)), pltpu.SemaphoreType.DMA]


def row_loop(rows, body):
    def one(i, carry):
        body(pl.ds(pl.multiple_of(i * 16, 16), 16))
        return carry

    lax.fori_loop(0, rows // 16, one, 0)


def normalized(values):
    average = jnp.mean(values, axis=-1, keepdims=True)
    centered = values - average
    variance = jnp.mean(centered * centered, axis=-1, keepdims=True)
    scale = lax.rsqrt(variance + 1e-05)
    return centered * scale, scale


def norm_back(values, grad, gain):
    unit, scale = normalized(values)
    weighted = grad * gain
    mean_one = jnp.mean(weighted, axis=-1, keepdims=True)
    mean_two = jnp.mean(weighted * unit, axis=-1, keepdims=True)
    return scale * (weighted - mean_one - unit * mean_two), grad * unit


def gather_kernel(one_ref, two_ref, one_out, two_out, *sems):
    me, c, x, y, pc, px, py = spots()
    meet((pc, px, py))
    one = Gathering(one_ref, one_out, *sems[:3])
    two = Gathering(two_ref, two_out, *sems[3:])
    one.start()
    one.forward()
    two.start()
    two.forward()
    one.end()
    two.end()


def middle_kernel(att, w_out, tok, vec, middle, normed_all, total, own, *scratch):
    me, c, x, y, pc, px, py = spots()
    meet((pc, px, py))
    sums = Summing(att, w_out, total, scratch[:6])
    sums.run()

    def body(at):
        values = tok[at, :].astype(F32) + total[at, :] + vec[6:7, :]
        middle[at, :] = values
        unit, _ = normalized(values)
        own[at, :] = (unit * vec[2:3, :] + vec[3:4, :]).astype(BF)

    row_loop(own.shape[0], body)
    spread = Gathering(own, normed_all, *scratch[6:])
    spread.start()
    spread.forward()
    sums.end()
    spread.end()


def branch_kernel(grad_before, w_up, middle, cot, vec, grad_middle, sums_out, branch_all, total, own, *scratch):
    me, c, x, y, pc, px, py = spots()
    meet((pc, px, py))
    sums = Summing(grad_before, w_up, total, scratch[:6])
    sums.run()
    sums_out[...] = jnp.zeros_like(sums_out)

    def body(at):
        grad = total[at, :]
        part, for_gain = norm_back(middle[at, :], grad, vec[2:3, :])
        back = cot[at, :].astype(F32)
        whole = back + part
        grad_middle[at, :] = whole
        low = whole.astype(BF)
        own[at, :] = low
        low = low.astype(F32)
        for n, values in enumerate((for_gain, grad, low, back)):
            sums_out[n] += values[:8] + values[8:]

    row_loop(own.shape[0], body)
    spread = Gathering(own, branch_all, *scratch[6:])
    spread.start()
    spread.forward()
    sums.end()
    spread.end()


def last_kernel(grad_joined, w_qkv, activated, w_down, tok, middle, grad_middle, vec, grad_tokens, sums_out, output, total, *scratch):
    me, c, x, y, pc, px, py = spots()
    meet((pc, px, py))
    sums = Summing(grad_joined, w_qkv, total, scratch[:6])
    sums.run()
    sums_out[...] = jnp.zeros_like(sums_out)

    def body(at):
        grad = total[at, :]
        part, for_gain = norm_back(tok[at, :].astype(F32), grad, vec[0:1, :])
        grad_tokens[at, :] = grad_middle[at, :] + part
        for n, values in enumerate((for_gain, grad)):
            sums_out[n] += values[:8] + values[8:]

    row_loop(total.shape[0], body)
    more = Summing(activated, w_down, total, scratch[6:])
    more.run()

    def body_two(at):
        output[at, :] = (middle[at, :] + total[at, :] + vec[7:8, :]).astype(BF)

    row_loop(total.shape[0], body_two)
    sums.end()
    more.end()


def call(body, ins, outs, scratch, number, microseconds, name):
    spec = {True: pl.BlockSpec(memory_space=pl.ANY), False: pl.BlockSpec(memory_space=pltpu.VMEM)}
    return pl.pallas_call(
        body,
        out_shape=[s for s, _ in outs],
        in_specs=[spec[stays] for _, stays in ins],
        out_specs=[spec[stays] for _, stays in outs],
        scratch_shapes=scratch,
        compiler_params=pltpu.CompilerParams(
            collective_id=number, has_side_effects=True, vmem_limit_bytes=60 * 2**20
        ),
        cost_estimate=pl.CostEstimate(flops=0, transcendentals=0, bytes_accessed=int(microseconds * 3.0e6)),
        name=name,
    )(*[a for a, _ in ins])


def dot(spec, a, b, **kw):
    return jnp.einsum(spec, a, b, preferred_element_type=F32, **kw)


def layer_norm(values, gain_row, shift_row):
    average = jnp.mean(values, axis=-1, keepdims=True)
    centered = values - average
    variance = jnp.mean(centered * centered, axis=-1, keepdims=True)
    return centered * lax.rsqrt(variance + 1e-05) * gain_row + shift_row


def allowed_mask(length_rows, row_length):
    ends = [length_rows[:, 0]]
    for span in range(1, length_rows.shape[-1]):
        ends.append(ends[-1] + length_rows[:, span])
    boundary = jnp.stack(ends, axis=-1)
    places = jnp.arange(row_length, dtype=jnp.int32)
    segment = jnp.sum((places[None, :, None] >= boundary[:, None, :]).astype(jnp.int32), axis=-1)
    same_span = segment[:, :, None] == segment[:, None, :]
    causal = places[:, None] >= places[None, :]
    padded = segment[:, :, None] == length_rows.shape[-1] - 1
    diagonal = places[:, None] == places[None, :]
    return same_span & causal[None] & (jnp.logical_not(padded) | diagonal[None])


def newton_schulz(current):
    def ein(spec, a, b):
        return jnp.einsum(spec, a, b, precision=lax.Precision.HIGH, preferred_element_type=F32)
    total = jnp.sum(current * current, axis=(0, 2))
    current = current * (1.0 / (jnp.sqrt(total) + 1e-07))[None, :, None]
    for number in range(NS_ITERS):
        gram = ein("rkc,rke->kce", current, current)
        square = ein("kce,kef->kcf", gram, gram)
        polynomial = COEF_B * gram + COEF_C * square
        current = COEF_A * current + ein("rkc,kce->rke", current, polynomial)
    return current


def local(tokens, doc_lengths, weights, momentum, vectors, vector_moment, vector_second, cotangent):
    hi, tp, sh = (lax.axis_size(a) for a in ALL)
    groups, world = hi * sh, hi * tp * sh
    rows, blocks, head = weights.shape
    row_tokens, d = tokens.shape
    heads = HEADS // tp
    inner_all = (blocks - 4 * HEADS) // 2
    inner = inner_all // tp
    attn_blocks = 4 * heads
    me = lax.axis_index("tp")
    t_all = tp * row_tokens

    low = weights.astype(BF)
    attn_send = low[:, : 4 * HEADS].reshape(rows, 4, tp, heads, head).transpose(2, 0, 1, 3, 4).reshape(tp, rows, attn_blocks * head)
    mlp_send = low[:, 4 * HEADS :].reshape(rows, 2, tp, inner, head).transpose(2, 0, 1, 3, 4).reshape(tp, rows, 2 * inner * head)

    def rows_in_order(gathered):
        n = gathered.shape[-1]
        return gathered.reshape(hi, sh, tp, rows, n).transpose(0, 2, 1, 3, 4).reshape(d, n)

    def spread(array):
        swapped = lax.all_to_all(array, "tp", split_axis=0, concat_axis=0, tiled=True)
        return rows_in_order(lax.all_gather(swapped, FS, axis=0, tiled=False))

    w_attn = spread(attn_send)
    w_mlp = spread(mlp_send)
    vec = lax.all_gather(vectors.astype(BF), "tp", axis=0, tiled=False)
    vec = lax.all_gather(vec, FS, axis=0, tiled=False)
    vec = vec.reshape(hi, sh, tp, rows, -1).transpose(0, 2, 1, 3, 4).reshape(d, -1).astype(F32)

    gathered = jax.ShapeDtypeStruct((tp, row_tokens, d), BF)
    tok_all, cot_all = call(
        gather_kernel, [(tokens, True), (cotangent, True)], [(gathered, True)] * 2, gather_scratch() * 2, 1, 75, "gather_rows"
    )
    tok_all, cot_all = tok_all.reshape(t_all, d), cot_all.reshape(t_all, d)
    lengths = lax.all_gather(doc_lengths, "tp", axis=0, tiled=True)
    allowed = allowed_mask(lengths, row_tokens)

    def per_of(count):
        return -(-count // groups)

    def to_owners(part, count):
        per = per_of(count)
        part = jnp.pad(part, ((0, 0), (0, 0), (0, per * groups - count), (0, 0)))
        part = part.reshape(rows, tp, hi, sh, per * head)
        return part.transpose(2, 1, 3, 0, 4)

    def split(array):
        attn = array[:, : 4 * HEADS].reshape(rows, 4, tp, heads, head).transpose(0, 2, 1, 3, 4).reshape(rows, tp, attn_blocks, head)
        mlp = array[:, 4 * HEADS :].reshape(rows, 2, tp, inner, head)
        return ((attn, attn_blocks), (mlp[:, 0], inner), (mlp[:, 1], inner))

    mom_send = jnp.concatenate([to_owners(p, c) for p, c in split(momentum.astype(BF))], axis=-1)
    width = mom_send.shape[-1]
    mom_mine = lax.all_to_all(mom_send.reshape(world, rows, width), ALL, split_axis=0, concat_axis=0, tiled=True)
    mom_mine = mom_mine.reshape(d, width)

    bias_q = lax.dynamic_slice(vec[:, 4], (me * heads * head,), (heads * head,))
    bias_v = lax.dynamic_slice(vec[:, 5], (me * heads * head,), (heads * head,))
    bias_up = lax.dynamic_slice(vec[:, 8:].T.reshape(-1), (me * inner * head,), (inner * head,))
    hc = heads * head
    w_qkv, w_out = w_attn[:, : 3 * hc], w_attn[:, 3 * hc :]
    w_up, w_down = w_mlp[:, : inner * head], w_mlp[:, inner * head :]

    normed_one = layer_norm(tok_all.astype(F32), vec[:, 0], vec[:, 1]).astype(BF)
    joined = dot("td,dn->tn", normed_one, w_qkv)

    def per_head(values):
        return values.reshape(tp, row_tokens, heads, head)

    queries = per_head((joined[:, :hc] + bias_q).astype(BF))
    key_rows = per_head(joined[:, hc : 2 * hc].astype(BF))
    value_rows = per_head((joined[:, 2 * hc :] + bias_v).astype(BF))
    scores = dot("rqhc,rkhc->rhqk", queries, key_rows) * head ** (-0.5)
    scores = jnp.where(allowed[:, None], scores, -1e30)
    row_peak = jnp.max(scores, axis=-1, keepdims=True)
    exponent = jnp.exp(scores - row_peak)
    probability = exponent / jnp.sum(exponent, axis=-1, keepdims=True)
    probability_low = probability.astype(BF)
    attended = dot("rhqk,rkhc->rqhc", probability_low, value_rows).astype(BF).reshape(t_all, hc)

    vec_rows = jnp.pad(vec.T, ((0, 4), (0, 0)))
    own_f32 = jax.ShapeDtypeStruct((row_tokens, d), F32)
    own_scratch = [pltpu.VMEM((row_tokens, d), F32), pltpu.VMEM((row_tokens, d), BF)]
    middle, normed_two = call(
        middle_kernel,
        [(attended, False), (w_out, False), (tokens, False), (vec_rows, False)],
        [(own_f32, False), (gathered, True)],
        own_scratch + sum_scratch(row_tokens, d) + gather_scratch(),
        2,
        95,
        "attention_output",
    )
    normed_two = normed_two.reshape(t_all, d)
    before = dot("td,dn->tn", normed_two, w_up) + bias_up
    grad_activated = dot("td,dn->tn", cot_all, w_down)
    gelu_value, gelu_back = jax.vjp(partial(jax.nn.gelu, approximate=True), before)
    activated = gelu_value.astype(BF)
    grad_before = gelu_back(grad_activated)[0].astype(BF)

    grad_middle, sums_two, grad_branch = call(
        branch_kernel,
        [(grad_before, False), (w_up, False), (middle, False), (cotangent, False), (vec_rows, False)],
        [(own_f32, False), (jax.ShapeDtypeStruct((4, 8, d), F32), False), (gathered, True)],
        own_scratch + sum_scratch(row_tokens, d) + gather_scratch(),
        3,
        95,
        "second_norm_backward",
    )
    grad_branch = grad_branch.reshape(t_all, d)
    grad_attended = dot("td,dc->tc", grad_branch, w_out).astype(BF)
    grad_att = per_head(grad_attended)
    grad_prob = dot("rqhc,rkhc->rhqk", grad_att, value_rows)
    row_total = jnp.sum(probability * grad_prob, axis=-1, keepdims=True)
    grad_scores = (probability * (grad_prob - row_total)).astype(BF)
    scale = head ** (-0.5)
    grad_q = (dot("rhqk,rkhc->rqhc", grad_scores, key_rows) * scale).astype(BF).reshape(t_all, hc)
    grad_k = (dot("rhqk,rqhc->rkhc", grad_scores, queries) * scale).astype(BF).reshape(t_all, hc)
    grad_v = dot("rhqk,rqhc->rkhc", probability_low, grad_att).astype(BF).reshape(t_all, hc)
    grad_joined = jnp.concatenate([grad_q, grad_k, grad_v], axis=1)
    grad_tokens, sums_one, output = call(
        last_kernel,
        [(grad_joined, False), (w_qkv, False), (activated, False), (w_down, False)]
        + [(tokens, False), (middle, False), (grad_middle, False), (vec_rows, False)],
        [(own_f32, False), (jax.ShapeDtypeStruct((2, 8, d), F32), False), (jax.ShapeDtypeStruct((row_tokens, d), BF), False)],
        own_scratch[:1] + sum_scratch(row_tokens, d) * 2,
        4,
        85,
        "first_norm_backward",
    )

    def to_block_owners(left_right, count):
        per = per_of(count)
        parts = [dot("td,tn->dn", a, b).astype(BF) for a, b in left_right]
        joined_part = parts[0] if len(parts) == 1 else jnp.concatenate(parts, axis=1)
        joined_part = jnp.pad(joined_part, ((0, 0), (0, (per * groups - count) * head)))
        stacked = joined_part.reshape(d, groups, per * head).transpose(1, 0, 2)
        return lax.psum_scatter(stacked, FS, scatter_dimension=0, tiled=False)

    g_down = to_block_owners([(cot_all, activated)], inner)
    g_up = to_block_owners([(normed_two, grad_before)], inner)
    g_attn = to_block_owners([(normed_one, grad_joined), (grad_branch, attended)], attn_blocks)
    g_mine = jnp.concatenate([g_attn, g_up, g_down], axis=1)

    def to_row_owners(mine):
        back = lax.all_to_all(mine.astype(BF).reshape(world, rows, width), ALL, split_axis=0, concat_axis=0, tiled=True)
        back = back.reshape(hi, tp, sh, rows, width)
        pieces, at = [], 0
        for number, count in enumerate((attn_blocks, inner, inner)):
            per = per_of(count)
            piece = back[..., at : at + per * head].reshape(hi, tp, sh, rows, per, head)
            at += per * head
            piece = piece.transpose(3, 1, 0, 2, 4, 5).reshape(rows, tp, groups * per, head)[:, :, :count]
            if number == 0:
                piece = piece.reshape(rows, tp, 4, heads, head).transpose(0, 2, 1, 3, 4)
            pieces.append(piece.reshape(rows, -1, head))
        return jnp.concatenate(pieces, axis=1)

    weight_grad = to_row_owners(g_mine).astype(F32)
    moment_new = 0.95 * momentum + weight_grad

    moment_mine = 0.95 * mom_mine.astype(F32) + g_mine.astype(F32)
    orthogonal = newton_schulz(moment_mine.reshape(d, width // head, head)).reshape(d, width)
    orthogonal_rows = to_row_owners(orthogonal).astype(F32)
    new_weights = weights * (1.0 - 0.15 * 0.1) - 0.15 * 0.2 * math.sqrt(d) * orthogonal_rows

    sums_one, sums_two = jnp.sum(sums_one, axis=1), jnp.sum(sums_two, axis=1)
    plain = jnp.stack(
        [
            sums_one[0],
            sums_one[1],
            sums_two[0],
            sums_two[1],
            jnp.zeros((d,), F32),
            jnp.zeros((d,), F32),
            sums_two[2],
            sums_two[3],
        ],
        axis=0,
    )
    plain = lax.dynamic_update_slice(plain, jnp.sum(grad_q, axis=0, dtype=F32)[None], (4, me * hc))
    plain = lax.dynamic_update_slice(plain, jnp.sum(grad_v, axis=0, dtype=F32)[None], (5, me * hc))
    hidden = jnp.zeros((inner_all * head,), F32)
    hidden = lax.dynamic_update_slice(hidden, jnp.sum(grad_before, axis=0, dtype=F32), (me * inner * head,))
    terms = jnp.concatenate([plain, hidden.reshape(-1, d)], axis=0)
    terms = terms.reshape(-1, world, rows).transpose(1, 0, 2).reshape(world, -1)
    vector_grad = jnp.sum(lax.all_to_all(terms, ALL, split_axis=0, concat_axis=0, tiled=True), axis=0)
    vector_grad = vector_grad.reshape(-1, rows).T
    first_moment = 0.9 * vector_moment + 0.1 * vector_grad
    second = 0.95 * vector_second + 0.05 * vector_grad * vector_grad
    corrected = first_moment / (1.0 - 0.9**STEP)
    normal_second = second / (1.0 - 0.95**STEP)
    next_vectors = vectors - 0.5 * corrected / (jnp.sqrt(normal_second) + 1e-08)
    return (
        output,
        grad_tokens,
        weight_grad,
        new_weights,
        moment_new,
        first_moment,
        second,
        next_vectors,
    )


def solution(mesh):
    dp, sh = mesh.shape["dp"], mesh.shape["shard"]
    tp = math.gcd(dp, 8)
    fine = Mesh(mesh.devices.reshape(dp // tp, tp, sh), ALL)
    two, three = P(ALL, None), P(ALL, None, None)
    return jax.shard_map(
        local,
        mesh=fine,
        in_specs=(two, two, three, three, two, two, two, two),
        out_specs=(two, two, three, three, three, two, two, two),
        check_vma=False,
    )
```

```python
from functools import partial
import math

import jax
import jax.numpy as jnp
from jax import lax
from jax.experimental import pallas as pl
from jax.experimental.pallas import tpu as pltpu
from jax.sharding import Mesh, PartitionSpec as P

HEADS = 16
HEAD = 128
NS_ITERS = 5
STEP = 10

COEF_A = 3.4445
COEF_B = -4.775
COEF_C = 2.0315
BF = jnp.bfloat16
F32 = jnp.float32
ALL = ("hi", "tp", "shard")
FS = ("hi", "shard")


MESH = pl.DeviceIdType.MESH
WIDE = 256


def rem(a, b):
    return lax.rem(a, jnp.int32(b))


def div(a, b):
    return lax.div(a, jnp.int32(b))


def spots():
    me = lax.axis_index("tp")
    c, x, y = rem(me, 2), rem(div(me, 2), 2), div(me, 4)
    return me, c, x, y, me + 1 - 2 * c, me + 2 - 4 * x, me + 4 - 8 * y


def meet(peers):
    barrier = pltpu.get_barrier_semaphore()
    for peer in peers:
        pl.semaphore_signal(barrier, inc=1, device_id={"tp": peer}, device_id_type=MESH)
    pl.semaphore_wait(barrier, len(peers))


def remote(src, dst, send, recv, peer):
    return pltpu.make_async_remote_copy(
        src_ref=src, dst_ref=dst, send_sem=send, recv_sem=recv, device_id={"tp": peer}, device_id_type=MESH
    )


def sum_scratch(rows, width):
    count = width // WIDE
    return [
        pltpu.VMEM((count, 2, 2, 2, rows, WIDE), BF),
        pltpu.VMEM((count, 2, 2, rows, WIDE), BF),
        pltpu.VMEM((count, 2, rows, WIDE), BF),
        pltpu.VMEM((count, rows, WIDE), BF),
        pltpu.SemaphoreType.DMA((3, count)),
        pltpu.SemaphoreType.DMA((3, count)),
    ]


class Summing:
    def __init__(self, left, right, total, scratch):
        self.left, self.right, self.total = left, right, total
        self.part, self.from_c, self.from_1, self.from_2, self.send, self.recv = scratch
        self.count = self.part.shape[0]
        self.rows = self.part.shape[4]
        self.copies = {}

    def fill(self, k):
        right = self.right[k * WIDE : (k + 1) * WIDE, :]

        def one(dest, carry):
            rows = self.left[pl.ds(pl.multiple_of(dest * self.rows, self.rows), self.rows), :]
            made = lax.dot_general(rows, right, (((1,), (1,)), ((), ())), preferred_element_type=F32)
            self.part[k, div(dest, 4), rem(div(dest, 2), 2), rem(dest, 2)] = made.astype(BF)
            return carry

        lax.fori_loop(0, 8, one, 0)

    def begin(self, stage, k, src, dst, peer):
        copy = remote(src, dst, self.send.at[stage, k], self.recv.at[stage, k], peer)
        copy.start()
        self.copies[stage, k] = copy

    def run(self):
        me, c, x, y, pc, px, py = spots()
        oc, ox, oy = 1 - c, 1 - x, 1 - y
        part = self.part

        def core_stage(k):
            self.copies[0, k].wait_recv()
            for i in range(4):
                a, b = i // 2, i % 2
                part[k, a, b, c] = (part[k, a, b, c].astype(F32) + self.from_c[k, a, b].astype(F32)).astype(BF)
            if k % 2 == 0:
                self.begin(1, k, part.at[k, :, ox, c], self.from_1.at[k], px)
            else:
                self.begin(1, k, part.at[k, oy, :, c], self.from_1.at[k], py)

        for k in range(self.count):
            self.fill(k)
            self.begin(0, k, part.at[k, :, :, oc], self.from_c.at[k], pc)
            if k:
                core_stage(k - 1)
        core_stage(self.count - 1)
        for k in range(self.count):
            self.copies[1, k].wait_recv()
            for i in range(2):
                if k % 2 == 0:
                    part[k, i, x, c] = (part[k, i, x, c].astype(F32) + self.from_1[k, i].astype(F32)).astype(BF)
                else:
                    part[k, y, i, c] = (part[k, y, i, c].astype(F32) + self.from_1[k, i].astype(F32)).astype(BF)
            if k % 2 == 0:
                self.begin(2, k, part.at[k, oy, x, c], self.from_2.at[k], py)
            else:
                self.begin(2, k, part.at[k, y, ox, c], self.from_2.at[k], px)
        for k in range(self.count):
            self.copies[2, k].wait_recv()
            self.total[:, k * WIDE : (k + 1) * WIDE] = part[k, y, x, c].astype(F32) + self.from_2[k].astype(F32)

    def end(self):
        for copy in self.copies.values():
            copy.wait_send()


class Gathering:
    def __init__(self, own, out, send, recv, local):
        self.own, self.out, self.send, self.recv, self.local = own, out, send, recv, local
        self.copies = []

    def begin(self, src, dst, peer):
        n = len(self.copies)
        copy = remote(src, dst, self.send.at[n], self.recv.at[n], peer)
        copy.start()
        self.copies.append(copy)
        return copy

    def start(self):
        me, c, x, y, pc, px, py = spots()
        self.spots = me, px, py, pc
        own, out = self.own, self.out
        half = own.shape[-1] // 2
        self.low, self.high = pl.ds(0, half), pl.ds(half, half)
        low, high = self.low, self.high
        self.px_high = self.begin(own.at[:, high], out.at[me, :, high], px)
        self.py_low = self.begin(own.at[:, low], out.at[me, :, low], py)
        self.begin(own, out.at[me], pc)
        self.px_low = self.begin(own.at[:, low], out.at[me, :, low], px)
        self.py_high = self.begin(own.at[:, high], out.at[me, :, high], py)
        self.kept = pltpu.make_async_copy(own, out.at[me], self.local)
        self.kept.start()

    def forward(self):
        me, px, py, pc = self.spots
        out, low, high = self.out, self.low, self.high
        across = px + py - me
        self.px_high.wait_recv()
        a = self.begin(out.at[px, :, high], out.at[px, :, high], py)
        self.begin(out.at[px, :, high], out.at[px, :, high], pc)
        self.py_low.wait_recv()
        b = self.begin(out.at[py, :, low], out.at[py, :, low], px)
        self.begin(out.at[py, :, low], out.at[py, :, low], pc)
        self.px_low.wait_recv()
        self.begin(out.at[px, :, low], out.at[px, :, low], pc)
        self.py_high.wait_recv()
        self.begin(out.at[py, :, high], out.at[py, :, high], pc)
        a.wait_recv()
        self.begin(out.at[across, :, high], out.at[across, :, high], pc)
        b.wait_recv()
        self.begin(out.at[across, :, low], out.at[across, :, low], pc)
        self.seen = (0, 1, 3, 4, 5, 7)

    def end(self):
        for n, copy in enumerate(self.copies):
            if n not in self.seen:
                copy.wait_recv()
            copy.wait_send()
        self.kept.wait()


def gather_scratch():
    return [pltpu.SemaphoreType.DMA((13,)), pltpu.SemaphoreType.DMA((13,)), pltpu.SemaphoreType.DMA]


def row_loop(rows, body):
    def one(i, carry):
        body(pl.ds(pl.multiple_of(i * 16, 16), 16))
        return carry

    lax.fori_loop(0, rows // 16, one, 0)


def normalized(values):
    average = jnp.mean(values, axis=-1, keepdims=True)
    centered = values - average
    variance = jnp.mean(centered * centered, axis=-1, keepdims=True)
    scale = lax.rsqrt(variance + 1e-05)
    return centered * scale, scale


def norm_back(values, grad, gain):
    unit, scale = normalized(values)
    weighted = grad * gain
    mean_one = jnp.mean(weighted, axis=-1, keepdims=True)
    mean_two = jnp.mean(weighted * unit, axis=-1, keepdims=True)
    return scale * (weighted - mean_one - unit * mean_two), grad * unit


def fetch_rows(w, first, held, sem, hi, sh):
    rows, width = w.shape[2], held.shape[1]

    def one(f, carry):
        s, t, h = rem(f, sh), rem(div(f, sh), 8), div(f, 8 * sh)
        pltpu.make_async_copy(
            w.at[h * sh + s, t, :, pl.ds(first, width)], held.at[pl.ds(pl.multiple_of(f * rows, rows), rows)], sem
        ).start()
        return carry

    lax.fori_loop(0, 8 * hi * sh, one, 0)


def fetched(held, sem):
    pltpu.make_async_copy(held, held, sem).wait()


def first_kernel(hi, sh, tok, piece, cot, normed_all, vec, lengths, own, pieces, send_p, recv_p, send_q, recv_q, *sems):
    me, c, x, y, pc, px, py = spots()
    groups = hi * sh
    mine = lax.axis_index("hi") * sh + lax.axis_index("shard")
    barrier = pltpu.get_barrier_semaphore()
    across, around = [], []
    for i in range(1, groups):
        there = rem(mine + i, groups)
        across.append({"hi": div(there, sh), "shard": rem(there, sh)})
    for i in range(1, 8):
        around.append({"tp": rem(me + i, 8)})
    for peer in across + around:
        pl.semaphore_signal(barrier, inc=1, device_id=peer, device_id_type=MESH)
    pl.semaphore_wait(barrier, groups + 6)

    pieces[mine, me] = piece[...]
    spot = pieces.at[mine, me]
    first = [
        pltpu.make_async_remote_copy(
            src_ref=spot, dst_ref=spot, send_sem=send_p.at[i], recv_sem=recv_p.at[i], device_id=peer, device_id_type=MESH
        )
        for i, peer in enumerate(across)
    ]
    for copy in first:
        copy.start()
    for copy in first:
        copy.wait_recv()
    column = pieces.at[:, me]
    second = [
        pltpu.make_async_remote_copy(
            src_ref=column, dst_ref=column, send_sem=send_q.at[i], recv_sem=recv_q.at[i], device_id=peer, device_id_type=MESH
        )
        for i, peer in enumerate(around)
    ]
    for copy in second:
        copy.start()
    for copy in second:
        copy.wait_recv()
    width = tok.shape[1]
    parts = 8 * groups * 128 // width
    for q in range(width // 128):
        found = None
        for f in range(q * parts, (q + 1) * parts):
            value = pieces[f // (8 * sh) * sh + f % sh, f // sh % 8].astype(F32)
            found = value if found is None else found + value
        vec[:, q * 128 : (q + 1) * 128] = found
    for t in range(8):
        lengths[t : t + 1, :] = pieces[mine, t].astype(F32)[12:13, :]

    def body(at):
        unit, _ = normalized(tok[at, :].astype(F32))
        own[at, :] = (unit * vec[0:1, :] + vec[1:2, :]).astype(BF)

    row_loop(own.shape[0], body)
    spread = Gathering(own, normed_all, *sems)
    spread.start()
    spread.forward()
    spread.end()
    for copy in first + second:
        copy.wait_send()


def allowed_of(lengths, row, size):
    line = lengths[pl.ds(row, 1), :]
    ends = [line[:, 0:1]]
    for n in range(1, 3):
        ends.append(ends[-1] + line[:, n : n + 1])
    down = lax.broadcasted_iota(jnp.int32, (size, 1), 0)
    along = lax.broadcasted_iota(jnp.int32, (1, size), 1)

    def span(places):
        places = places.astype(F32)
        return sum(jnp.where(places >= end, 1.0, 0.0) for end in ends)

    span_down, span_along = span(down), span(along)
    tail = jnp.where(span_down == 3.0, down, 0)
    return (span_down == span_along) & (along <= down) & (along >= tail)


def probabilities(query, key, allowed):
    scores = lax.dot_general(query, key, (((1,), (1,)), ((), ())), preferred_element_type=F32) * HEAD ** (-0.5)
    scores = jnp.where(allowed, scores, -1e30)
    exponent = jnp.exp(scores - jnp.max(scores, axis=-1, keepdims=True))
    return exponent / jnp.sum(exponent, axis=-1, keepdims=True)


def attention_kernel(
    hi, sh, normed, w_any, lengths, vec, tok, cot, middle, normed_all, cot_all, qkv, att, total, own, w, w_sem, *scratch
):
    me, c, x, y, pc, px, py = spots()
    fetch_rows(w_any, 0, w, w_sem, hi, sh)
    meet((pc, px, py))
    spread_cot = Gathering(cot, cot_all, *scratch[9:])
    spread_cot.start()
    size = own.shape[0]
    hc = att.shape[1]
    fetched(w, w_sem)

    def one_row(r, carry):
        joined = jnp.dot(normed[r], w[:, : 3 * hc], preferred_element_type=F32)
        here = pl.ds(pl.multiple_of(me * hc, 128), hc)
        queries = (joined[:, :hc] + vec[4:5, here]).astype(BF)
        keys = joined[:, hc : 2 * hc].astype(BF)
        values = (joined[:, 2 * hc :] + vec[5:6, here]).astype(BF)
        qkv[r, :, :hc] = queries
        qkv[r, :, hc : 2 * hc] = keys
        qkv[r, :, 2 * hc :] = values
        allowed = allowed_of(lengths, r, size)
        rows = pl.ds(pl.multiple_of(r * size, size), size)
        for h in range(hc // HEAD):
            at = slice(h * HEAD, (h + 1) * HEAD)
            low = probabilities(queries[:, at], keys[:, at], allowed).astype(BF)
            att[rows, at] = jnp.dot(low, values[:, at], preferred_element_type=F32).astype(BF)
        return carry

    lax.fori_loop(0, 8, one_row, 0)
    sums = Summing(att, w.at[:, 3 * hc :], total, scratch[:6])
    spread_cot.forward()
    sums.run()

    def body(at):
        values = tok[at, :].astype(F32) + total[at, :] + vec[6:7, :]
        middle[at, :] = values
        unit, _ = normalized(values)
        own[at, :] = (unit * vec[2:3, :] + vec[3:4, :]).astype(BF)

    row_loop(own.shape[0], body)
    spread = Gathering(own, normed_all, *scratch[6:9])
    spread.start()
    spread.forward()
    sums.end()
    spread_cot.end()
    spread.end()


GELU_A = math.sqrt(2.0 / math.pi)


def mlp_kernel(hi, sh, normed, cot, w_any, vec, activated, grad_before, w_up, w_down, sems):
    width = w_up.shape[1]

    @pl.when(pl.program_id(0) == 0)
    def _():
        fetch_rows(w_any, 0, w_up, sems.at[0], hi, sh)
        fetch_rows(w_any, width, w_down, sems.at[1], hi, sh)
        fetched(w_up, sems.at[0])
        fetched(w_down, sems.at[1])

    me = lax.axis_index("tp")
    each = vec.shape[1] // width
    for j in range(width // 256):
        at = slice(j * 256, (j + 1) * 256)
        bias = vec[pl.ds(8 + div(me, each), 1), pl.ds(pl.multiple_of(rem(me, each) * width + j * 256, 256), 256)]
        before = jnp.dot(normed[0], w_up[:, at], preferred_element_type=F32) + bias
        grad = jnp.dot(cot[0], w_down[:, at], preferred_element_type=F32)
        square = before * before
        slope = jnp.tanh(before * (GELU_A + GELU_A * 0.044715 * square))
        half = 0.5 * (1.0 + slope)
        activated[:, at] = (before * half).astype(BF)
        inner = GELU_A + 3.0 * GELU_A * 0.044715 * square
        grad_before[:, at] = (grad * (half + 0.5 * before * (1.0 - slope * slope) * inner)).astype(BF)


def attention_back_kernel(hi, sh, branch, w_any, qkv, lengths, grad_joined, w, sem):
    hc = w.shape[1]
    size = branch.shape[1]
    r = pl.program_id(0)

    @pl.when(r == 0)
    def _():
        fetch_rows(w_any, 3 * hc, w, sem, hi, sh)
        fetched(w, sem)

    grad_att = jnp.dot(branch[0], w[...], preferred_element_type=F32).astype(BF)
    allowed = allowed_of(lengths, r, size)
    scale = HEAD ** (-0.5)
    for h in range(hc // HEAD):
        at = slice(h * HEAD, (h + 1) * HEAD)
        query, key, value = (qkv[0, :, n * hc + h * HEAD : n * hc + (h + 1) * HEAD] for n in range(3))
        probability = probabilities(query, key, allowed)
        low = probability.astype(BF)
        grad = grad_att[:, at]
        grad_prob = lax.dot_general(grad, value, (((1,), (1,)), ((), ())), preferred_element_type=F32)
        row_total = jnp.sum(probability * grad_prob, axis=-1, keepdims=True)
        grad_scores = (probability * (grad_prob - row_total)).astype(BF)
        made = (
            jnp.dot(grad_scores, key, preferred_element_type=F32) * scale,
            lax.dot_general(grad_scores, query, (((0,), (0,)), ((), ())), preferred_element_type=F32) * scale,
            lax.dot_general(low, grad, (((0,), (0,)), ((), ())), preferred_element_type=F32),
        )
        for n in range(3):
            grad_joined[:, n * hc + h * HEAD : n * hc + (h + 1) * HEAD] = made[n].astype(BF)


def branch_kernel(
    hi, sh, grad_before, w_any, middle, cot, vec, grad_middle, sums_out, branch_all, total, own, w_up, w_sem, *scratch
):
    me, c, x, y, pc, px, py = spots()
    fetch_rows(w_any, 0, w_up, w_sem, hi, sh)
    meet((pc, px, py))
    fetched(w_up, w_sem)
    sums = Summing(grad_before, w_up, total, scratch[:6])
    sums.run()
    sums_out[...] = jnp.zeros_like(sums_out)

    def body(at):
        grad = total[at, :]
        part, for_gain = norm_back(middle[at, :], grad, vec[2:3, :])
        back = cot[at, :].astype(F32)
        whole = back + part
        grad_middle[at, :] = whole
        low = whole.astype(BF)
        own[at, :] = low
        low = low.astype(F32)
        for n, values in enumerate((for_gain, grad, low, back)):
            sums_out[n] += values[:8] + values[8:]

    row_loop(own.shape[0], body)
    spread = Gathering(own, branch_all, *scratch[6:])
    spread.start()
    spread.forward()
    sums.end()
    spread.end()


def last_kernel(
    hi, sh, grad_joined, w_attn, activated, w_mlp, tok, middle, grad_middle, vec, grad_tokens, sums_out, output, total,
    w_qkv, w_down, w_sems, *scratch
):
    me, c, x, y, pc, px, py = spots()
    fetch_rows(w_attn, 0, w_qkv, w_sems.at[0], hi, sh)
    fetch_rows(w_mlp, w_down.shape[1], w_down, w_sems.at[1], hi, sh)
    meet((pc, px, py))
    fetched(w_qkv, w_sems.at[0])
    fetched(w_down, w_sems.at[1])
    sums = Summing(grad_joined, w_qkv, total, scratch[:6])
    sums.run()
    sums_out[...] = jnp.zeros_like(sums_out)

    def body(at):
        grad = total[at, :]
        part, for_gain = norm_back(tok[at, :].astype(F32), grad, vec[0:1, :])
        grad_tokens[at, :] = grad_middle[at, :] + part
        for n, values in enumerate((for_gain, grad)):
            sums_out[n] += values[:8] + values[8:]

    row_loop(total.shape[0], body)
    more = Summing(activated, w_down, total, scratch[6:])
    more.run()

    def body_two(at):
        output[at, :] = (middle[at, :] + total[at, :] + vec[7:8, :]).astype(BF)

    row_loop(total.shape[0], body_two)
    sums.end()
    more.end()


def call(body, ins, outs, scratch, number, microseconds, name, grid=None):
    def spec(how):
        if how is True:
            return pl.BlockSpec(memory_space=pl.ANY)
        return pl.BlockSpec(memory_space=pltpu.VMEM) if how is False else pl.BlockSpec(*how)

    remote_params = {} if number is None else {"collective_id": number, "has_side_effects": True}
    return pl.pallas_call(
        body,
        out_shape=[s for s, _ in outs],
        in_specs=[spec(how) for _, how in ins],
        out_specs=[spec(how) for _, how in outs],
        scratch_shapes=scratch,
        compiler_params=pltpu.CompilerParams(vmem_limit_bytes=60 * 2**20, **remote_params),
        cost_estimate=pl.CostEstimate(flops=0, transcendentals=0, bytes_accessed=int(microseconds * 3.0e6)),
        name=name,
        **({} if grid is None else {"grid": grid}),
    )(*[a for a, _ in ins])


PAIR = 2 * HEAD


def ortho_kernel(hi, sh, mom, grad, out, gram, arrived, power, send_a, recv_a, send_b, recv_b):
    groups = hi * sh
    mine = lax.axis_index("hi") * sh + lax.axis_index("shard")
    count = out.shape[1] // PAIR
    per = gram.shape[0] // groups

    def peer(i):
        there = rem(mine + i, groups)
        return there, {"hi": div(there, sh), "shard": rem(there, sh)}

    barrier = pltpu.get_barrier_semaphore()
    for i in range(1, groups):
        pl.semaphore_signal(barrier, inc=1, device_id=peer(i)[1], device_id_type=MESH)
    pl.semaphore_wait(barrier, groups - 1)

    rows = lax.broadcasted_iota(jnp.int32, (PAIR, PAIR), 0)
    columns = lax.broadcasted_iota(jnp.int32, (PAIR, PAIR), 1)
    unit = jnp.where(rows == columns, 1.0, 0.0)
    one, two = slice(0, HEAD), slice(HEAD, PAIR)

    def block(k):
        at = pl.ds(pl.multiple_of(k * PAIR, PAIR), PAIR)
        return (0.95 * mom[:, at].astype(F32) + grad[:, at].astype(F32)).astype(BF), at

    def one_gram(k, carry):
        values, _ = block(k)
        made = lax.dot_general(values, values, (((0,), (0,)), ((), ())), preferred_element_type=F32)
        gram[k, 0] = made[one, one].astype(BF)
        gram[k, 1] = made[two, two].astype(BF)
        return carry

    lax.fori_loop(0, count, one_gram, 0)
    for k in range(count, gram.shape[0]):
        gram[k] = jnp.zeros((2, HEAD, HEAD), BF)

    def copies(i, src, dst, send, recv):
        return pltpu.make_async_remote_copy(
            src_ref=src, dst_ref=dst, send_sem=send.at[i - 1], recv_sem=recv.at[i - 1],
            device_id=peer(i)[1], device_id_type=MESH,
        )

    first = [copies(i, gram.at[pl.ds(peer(i)[0] * per, per)], arrived.at[i - 1], send_a, recv_a) for i in range(1, groups)]
    for copy in first:
        copy.start()
    for copy in first:
        copy.wait_recv()

    def product(a, b):
        a_high, b_high = a.astype(BF), b.astype(BF)
        a_low, b_low = (a - a_high.astype(F32)).astype(BF), (b - b_high.astype(F32)).astype(BF)
        made = jnp.dot(a_high, b_low, preferred_element_type=F32) + jnp.dot(a_low, b_high, preferred_element_type=F32)
        return made + jnp.dot(a_high, b_high, preferred_element_type=F32)

    upper = (rows < HEAD) & (rows == columns)
    lower = (rows >= HEAD) & (rows == columns)
    grams, wholes = [], []
    for j in range(per):
        halves = []
        for n in range(2):
            half = gram[mine * per + j, n].astype(F32)
            for i in range(groups - 1):
                half = half + arrived[i, j, n].astype(F32)
            halves.append(half)
        empty = jnp.zeros((HEAD, HEAD), F32)
        total = jnp.concatenate(
            [jnp.concatenate([halves[0], empty], axis=1), jnp.concatenate([empty, halves[1]], axis=1)], axis=0
        )

        def scaling_of(chosen):
            trace = jnp.sum(jnp.sum(jnp.where(chosen, total, 0.0), axis=1, keepdims=True), axis=0, keepdims=True)
            return 1.0 / (jnp.sqrt(trace) + 1e-07)

        scaling = jnp.where(rows < HEAD, scaling_of(upper), scaling_of(lower))
        grams.append(total * (scaling * scaling))
        wholes.append(scaling)
    for number in range(NS_ITERS):
        squares = [product(a, a) for a in grams]
        steps = [COEF_A * unit + COEF_B * a + COEF_C * s for a, s in zip(grams, squares)]
        wholes = [product(w, p) for w, p in zip(wholes, steps)] if number else [w * p for w, p in zip(wholes, steps)]
        if number < NS_ITERS - 1:
            grams = [product(product(a, p), p) for a, p in zip(grams, steps)]
    for j in range(per):
        power[mine * per + j, 0] = wholes[j][one, one].astype(BF)
        power[mine * per + j, 1] = wholes[j][two, two].astype(BF)
    own = power.at[pl.ds(mine * per, per)]
    second = [copies(i, own, own, send_b, recv_b) for i in range(1, groups)]
    for copy in second:
        copy.start()
    for copy in second:
        copy.wait_recv()

    def finish(k, carry):
        values, at = block(k)
        made = [jnp.dot(values[:, side], power[k, n], preferred_element_type=F32) for n, side in enumerate((one, two))]
        out[:, at] = jnp.concatenate(made, axis=1).astype(BF)
        return carry

    lax.fori_loop(0, count, finish, 0)
    for copy in first + second:
        copy.wait_send()


def orthogonalize(mom, grad, hi, sh, number, name):
    groups = hi * sh
    count = mom.shape[1] // PAIR
    per = -(-count // groups)
    return call(
        partial(ortho_kernel, hi, sh),
        [(mom, False), (grad, False)],
        [(jax.ShapeDtypeStruct(mom.shape, BF), False)],
        [
            pltpu.VMEM((groups * per, 2, HEAD, HEAD), BF),
            pltpu.VMEM((groups - 1, per, 2, HEAD, HEAD), BF),
            pltpu.VMEM((groups * per, 2, HEAD, HEAD), BF),
        ]
        + [pltpu.SemaphoreType.DMA((groups - 1,))] * 4,
        number,
        25,
        name,
    )[0]


def dot(spec, a, b, **kw):
    return jnp.einsum(spec, a, b, preferred_element_type=F32, **kw)


def local(tokens, doc_lengths, weights, momentum, vectors, vector_moment, vector_second, cotangent):
    hi, tp, sh = (lax.axis_size(a) for a in ALL)
    groups, world = hi * sh, hi * tp * sh
    rows, blocks, head = weights.shape
    row_tokens, d = tokens.shape
    heads = HEADS // tp
    inner_all = (blocks - 4 * HEADS) // 2
    inner = inner_all // tp
    attn_blocks = 4 * heads
    me = lax.axis_index("tp")
    t_all = tp * row_tokens

    def arrange(array):
        attn = array[:, : 4 * HEADS].reshape(rows, 4, tp, heads, head).transpose(2, 0, 1, 3, 4).reshape(tp, rows, attn_blocks * head)
        mlp = array[:, 4 * HEADS :].reshape(rows, 2, tp, inner, head).transpose(2, 0, 1, 3, 4).reshape(tp, rows, 2 * inner * head)
        return attn, mlp

    def restore(attn, mlp):
        attn = attn.reshape(tp, rows, 4, heads, head).transpose(1, 2, 0, 3, 4).reshape(rows, 4 * HEADS, head)
        mlp = mlp.reshape(tp, rows, 2, inner, head).transpose(1, 2, 0, 3, 4).reshape(rows, 2 * inner_all, head)
        return jnp.concatenate([attn, mlp], axis=1)

    def swap(array):
        return lax.all_to_all(array, "tp", split_axis=0, concat_axis=0, tiled=True)

    attn_send, mlp_send = arrange(weights.astype(BF))

    def spread(array):
        return lax.all_gather(array, FS, axis=0, tiled=False)

    w_attn = spread(swap(attn_send))
    mlp_swapped, tokens = lax.optimization_barrier((swap(mlp_send), tokens))
    w_mlp = spread(mlp_swapped)

    flat = (lax.axis_index("hi") * tp + me) * sh + lax.axis_index("shard")
    lanes = 128 // rows
    spot = lax.broadcasted_iota(jnp.int32, (1, 128), 1) // rows == flat % lanes
    piece = jnp.where(spot, jnp.tile(vectors.T, (1, lanes)), 0.0)
    count = vectors.shape[1]
    spans = jnp.pad(doc_lengths.astype(F32), ((0, 15 - count), (0, 128 - doc_lengths.shape[1])))
    piece = jnp.concatenate([piece, spans], axis=0).astype(BF)

    gathered = jax.ShapeDtypeStruct((tp, row_tokens, d), BF)
    own_f32 = jax.ShapeDtypeStruct((row_tokens, d), F32)
    own_bf = jax.ShapeDtypeStruct((row_tokens, d), BF)
    own_scratch = [pltpu.VMEM(own_f32.shape, F32), pltpu.VMEM(own_f32.shape, BF)]
    small = [pltpu.SemaphoreType.DMA((groups,))] * 2 + [pltpu.SemaphoreType.DMA((8,))] * 2
    normed_one, vec_rows, lengths = call(
        partial(first_kernel, hi, sh),
        [(tokens, False), (piece, False), (cotangent, True)],
        [
            (gathered, True),
            (jax.ShapeDtypeStruct((16, d), F32), False),
            (jax.ShapeDtypeStruct((8, 128), F32), False),
        ],
        [own_scratch[1], pltpu.VMEM((groups, 8, 16, 128), BF)] + small + gather_scratch(),
        1,
        50,
        "first_norm",
    )

    hc = heads * head
    units = inner * head
    middle, normed_two, cot_all, qkv, attended = call(
        partial(attention_kernel, hi, sh),
        [(normed_one, False), (w_attn, True), (lengths, False), (vec_rows, False), (tokens, False), (cotangent, True)],
        [
            (own_f32, False),
            (gathered, True),
            (gathered, True),
            (jax.ShapeDtypeStruct((tp, row_tokens, 3 * hc), BF), False),
            (jax.ShapeDtypeStruct((t_all, hc), BF), False),
        ],
        own_scratch
        + [pltpu.VMEM((d, 4 * hc), BF), pltpu.SemaphoreType.DMA]
        + sum_scratch(row_tokens, d)
        + gather_scratch() * 2,
        2,
        110,
        "attention",
    )

    mom_attn, mom_mlp = [swap(part).reshape(tp * rows, -1) for part in arrange(momentum.astype(BF))]
    normed_two, mom_attn, mom_mlp = lax.optimization_barrier((normed_two, mom_attn, mom_mlp))

    def rows_of(width):
        return (row_tokens, width), lambda r: (r, 0)

    def row_of(width):
        return (1, row_tokens, width), lambda r: (r, 0, 0)

    def fixed(array):
        return array.shape, lambda r: (0,) * array.ndim

    activated, grad_before = call(
        partial(mlp_kernel, hi, sh),
        [(normed_two, row_of(d)), (cot_all, row_of(d)), (w_mlp, True), (vec_rows, fixed(vec_rows))],
        [(jax.ShapeDtypeStruct((t_all, units), BF), rows_of(units))] * 2,
        [pltpu.VMEM((d, units), BF)] * 2 + [pltpu.SemaphoreType.DMA((2,))],
        None,
        30,
        "hidden_units",
        grid=(tp,),
    )
    flat_one, flat_two, flat_cot = (a.reshape(t_all, d) for a in (normed_one, normed_two, cot_all))

    def summed(left_right):
        parts = [dot("td,tn->dn", a, b).astype(BF) for a, b in left_right]
        part = parts[0] if len(parts) == 1 else jnp.concatenate(parts, axis=1)
        stacked = part.reshape(hi, tp, sh, rows, -1).transpose(0, 2, 1, 3, 4).reshape(groups, tp * rows, -1)
        return stacked

    def sent(stacked):
        return lax.psum_scatter(stacked, FS, scatter_dimension=0, tiled=False)

    s_down = summed([(flat_cot, activated)])
    s_up = summed([(flat_two, grad_before)])
    grad_before, s_down, s_up = lax.optimization_barrier((grad_before, s_down, s_up))
    g_down, g_up = sent(s_down), sent(s_up)

    grad_middle, sums_two, grad_branch = call(
        partial(branch_kernel, hi, sh),
        [(grad_before, False), (w_mlp, True), (middle, False), (cotangent, False), (vec_rows, False)],
        [(own_f32, False), (jax.ShapeDtypeStruct((4, 8, d), F32), False), (gathered, True)],
        own_scratch
        + [pltpu.VMEM((d, units), BF), pltpu.SemaphoreType.DMA]
        + sum_scratch(row_tokens, d)
        + gather_scratch(),
        3,
        95,
        "second_norm_backward",
    )
    grad_branch, g_down = lax.optimization_barrier((grad_branch, g_down))
    (grad_joined,) = call(
        partial(attention_back_kernel, hi, sh),
        [(grad_branch, row_of(d)), (w_attn, True), (qkv, row_of(3 * hc)), (lengths, fixed(lengths))],
        [(jax.ShapeDtypeStruct((t_all, 3 * hc), BF), rows_of(3 * hc))],
        [pltpu.VMEM((d, hc), BF), pltpu.SemaphoreType.DMA],
        None,
        25,
        "attention_backward",
        grid=(tp,),
    )
    grad_branch = grad_branch.reshape(t_all, d)
    s_attn = summed([(flat_one, grad_joined), (grad_branch, attended)])
    grad_joined, s_attn = lax.optimization_barrier((grad_joined, s_attn))
    g_attn = sent(s_attn)
    g_mlp = jnp.concatenate([g_up, g_down], axis=1)
    ortho_mlp = orthogonalize(mom_mlp, g_mlp, hi, sh, 5, "orthogonalize_mlp")
    grad_joined, ortho_mlp = lax.optimization_barrier((grad_joined, ortho_mlp))
    grad_tokens, sums_one, output = call(
        partial(last_kernel, hi, sh),
        [(grad_joined, False), (w_attn, True), (activated, False), (w_mlp, True)]
        + [(tokens, False), (middle, False), (grad_middle, False), (vec_rows, False)],
        [(own_f32, False), (jax.ShapeDtypeStruct((2, 8, d), F32), False), (own_bf, False)],
        own_scratch[:1]
        + [pltpu.VMEM((d, 3 * hc), BF), pltpu.VMEM((d, units), BF), pltpu.SemaphoreType.DMA((2,))]
        + sum_scratch(row_tokens, d) * 2,
        4,
        85,
        "first_norm_backward",
    )
    grad_tokens, output, g_attn = lax.optimization_barrier((grad_tokens, output, g_attn))

    def back(part):
        return swap(part.reshape(tp, rows, -1))

    weight_grad = restore(back(g_attn), back(g_mlp)).astype(F32)
    moment_new = 0.95 * momentum + weight_grad
    ortho_attn = orthogonalize(mom_attn, g_attn, hi, sh, 6, "orthogonalize_attention")
    orthogonal_rows = restore(back(ortho_attn), back(ortho_mlp)).astype(F32)
    new_weights = weights * (1.0 - 0.15 * 0.1) - 0.15 * 0.2 * math.sqrt(d) * orthogonal_rows

    sums_one, sums_two = jnp.sum(sums_one, axis=1), jnp.sum(sums_two, axis=1)
    plain = jnp.stack(
        [
            sums_one[0],
            sums_one[1],
            sums_two[0],
            sums_two[1],
            jnp.zeros((d,), F32),
            jnp.zeros((d,), F32),
            sums_two[2],
            sums_two[3],
        ],
        axis=0,
    )
    plain = lax.dynamic_update_slice(plain, jnp.sum(grad_joined[:, :hc], axis=0, dtype=F32)[None], (4, me * hc))
    plain = lax.dynamic_update_slice(plain, jnp.sum(grad_joined[:, 2 * hc :], axis=0, dtype=F32)[None], (5, me * hc))
    hidden = jnp.zeros((inner_all * head,), F32)
    hidden = lax.dynamic_update_slice(hidden, jnp.sum(grad_before, axis=0, dtype=F32), (me * inner * head,))
    terms = jnp.concatenate([plain, hidden.reshape(-1, d)], axis=0)
    terms = terms.reshape(-1, world, rows).transpose(1, 0, 2).reshape(world, -1)
    vector_grad = jnp.sum(lax.all_to_all(terms, ALL, split_axis=0, concat_axis=0, tiled=True), axis=0)
    vector_grad = vector_grad.reshape(-1, rows).T
    first_moment = 0.9 * vector_moment + 0.1 * vector_grad
    second = 0.95 * vector_second + 0.05 * vector_grad * vector_grad
    corrected = first_moment / (1.0 - 0.9**STEP)
    normal_second = second / (1.0 - 0.95**STEP)
    next_vectors = vectors - 0.5 * corrected / (jnp.sqrt(normal_second) + 1e-08)
    return (
        output,
        grad_tokens,
        weight_grad,
        new_weights,
        moment_new,
        first_moment,
        second,
        next_vectors,
    )


def solution(mesh):
    dp, sh = mesh.shape["dp"], mesh.shape["shard"]
    tp = math.gcd(dp, 8)
    fine = Mesh(mesh.devices.reshape(dp // tp, tp, sh), ALL)
    two, three = P(ALL, None), P(ALL, None, None)
    return jax.shard_map(
        local,
        mesh=fine,
        in_specs=(two, two, three, three, two, two, two, two),
        out_specs=(two, two, three, three, three, two, two, two),
        check_vma=False,
    )
```

```python
from functools import partial
import math

import jax
import jax.numpy as jnp
from jax import lax
from jax.experimental import pallas as pl
from jax.experimental.pallas import tpu as pltpu
from jax.sharding import Mesh, PartitionSpec as P

HEADS = 16
HEAD = 128
PAIR = 2 * HEAD
NS_ITERS = 5
STEP = 10

COEF_A = 3.4445
COEF_B = -4.775
COEF_C = 2.0315
BF = jnp.bfloat16
F32 = jnp.float32
ALL = ("hi", "tp", "shard")
FS = ("hi", "shard")


MESH = pl.DeviceIdType.MESH
WIDE = 256


def rem(a, b):
    return lax.rem(a, jnp.int32(b))


def div(a, b):
    return lax.div(a, jnp.int32(b))


def spots():
    me = lax.axis_index("tp")
    c, x, y = rem(me, 2), rem(div(me, 2), 2), div(me, 4)
    return me, c, x, y, me + 1 - 2 * c, me + 2 - 4 * x, me + 4 - 8 * y


def meet(peers):
    barrier = pltpu.get_barrier_semaphore()
    for peer in peers:
        pl.semaphore_signal(barrier, inc=1, device_id={"tp": peer}, device_id_type=MESH)
    pl.semaphore_wait(barrier, len(peers))


def remote(src, dst, send, recv, peer):
    return pltpu.make_async_remote_copy(
        src_ref=src, dst_ref=dst, send_sem=send, recv_sem=recv, device_id={"tp": peer}, device_id_type=MESH
    )


def sum_scratch(rows, width):
    count = width // WIDE
    return [
        pltpu.VMEM((count, 2, 2, 2, rows, WIDE), BF),
        pltpu.VMEM((count, 2, 2, rows, WIDE), BF),
        pltpu.VMEM((count, 2, rows, WIDE), BF),
        pltpu.VMEM((count, rows, WIDE), BF),
        pltpu.SemaphoreType.DMA((3, count)),
        pltpu.SemaphoreType.DMA((3, count)),
    ]


class Summing:
    def __init__(self, left, right, total, scratch):
        self.left, self.right, self.total = left, right, total
        self.part, self.from_c, self.from_1, self.from_2, self.send, self.recv = scratch
        self.count = self.part.shape[0]
        self.rows = self.part.shape[4]
        self.copies = {}

    def fill(self, k):
        right = self.right[k * WIDE : (k + 1) * WIDE, :]

        def one(dest, carry):
            rows = self.left[pl.ds(pl.multiple_of(dest * self.rows, self.rows), self.rows), :]
            made = lax.dot_general(rows, right, (((1,), (1,)), ((), ())), preferred_element_type=F32)
            self.part[k, div(dest, 4), rem(div(dest, 2), 2), rem(dest, 2)] = made.astype(BF)
            return carry

        lax.fori_loop(0, 8, one, 0)

    def begin(self, stage, k, src, dst, peer):
        copy = remote(src, dst, self.send.at[stage, k], self.recv.at[stage, k], peer)
        copy.start()
        self.copies[stage, k] = copy

    def run(self):
        self.first()
        self.second()
        self.third()

    def first(self):
        me, c, x, y, pc, px, py = spots()
        oc, ox, oy = 1 - c, 1 - x, 1 - y
        part = self.part

        def core_stage(k):
            self.copies[0, k].wait_recv()
            for i in range(4):
                a, b = i // 2, i % 2
                part[k, a, b, c] = (part[k, a, b, c].astype(F32) + self.from_c[k, a, b].astype(F32)).astype(BF)
            if k % 2 == 0:
                self.begin(1, k, part.at[k, :, ox, c], self.from_1.at[k], px)
            else:
                self.begin(1, k, part.at[k, oy, :, c], self.from_1.at[k], py)

        for k in range(self.count):
            self.fill(k)
            self.begin(0, k, part.at[k, :, :, oc], self.from_c.at[k], pc)
            if k:
                core_stage(k - 1)
        core_stage(self.count - 1)

    def second(self):
        me, c, x, y, pc, px, py = spots()
        ox, oy = 1 - x, 1 - y
        part = self.part
        for k in range(self.count):
            self.copies[1, k].wait_recv()
            for i in range(2):
                if k % 2 == 0:
                    part[k, i, x, c] = (part[k, i, x, c].astype(F32) + self.from_1[k, i].astype(F32)).astype(BF)
                else:
                    part[k, y, i, c] = (part[k, y, i, c].astype(F32) + self.from_1[k, i].astype(F32)).astype(BF)
            if k % 2 == 0:
                self.begin(2, k, part.at[k, oy, x, c], self.from_2.at[k], py)
            else:
                self.begin(2, k, part.at[k, y, ox, c], self.from_2.at[k], px)

    def third(self):
        me, c, x, y, pc, px, py = spots()
        for k in range(self.count):
            self.copies[2, k].wait_recv()
            self.total[:, k * WIDE : (k + 1) * WIDE] = self.part[k, y, x, c].astype(F32) + self.from_2[k].astype(F32)

    def end(self):
        for copy in self.copies.values():
            copy.wait_send()


class Gathering:
    def __init__(self, own, out, send, recv, local):
        self.own, self.out, self.send, self.recv, self.local = own, out, send, recv, local
        self.copies = []

    def begin(self, src, dst, peer):
        n = len(self.copies)
        copy = remote(src, dst, self.send.at[n], self.recv.at[n], peer)
        copy.start()
        self.copies.append(copy)
        return copy

    def start(self):
        me, c, x, y, pc, px, py = spots()
        self.spots = me, px, py, pc
        own, out = self.own, self.out
        half = own.shape[-1] // 2
        self.low, self.high = pl.ds(0, half), pl.ds(half, half)
        low, high = self.low, self.high
        self.px_high = self.begin(own.at[:, high], out.at[me, :, high], px)
        self.py_low = self.begin(own.at[:, low], out.at[me, :, low], py)
        self.begin(own, out.at[me], pc)
        self.px_low = self.begin(own.at[:, low], out.at[me, :, low], px)
        self.py_high = self.begin(own.at[:, high], out.at[me, :, high], py)
        self.kept = pltpu.make_async_copy(own, out.at[me], self.local)
        self.kept.start()

    def forward(self):
        me, px, py, pc = self.spots
        out, low, high = self.out, self.low, self.high
        across = px + py - me
        self.px_high.wait_recv()
        a = self.begin(out.at[px, :, high], out.at[px, :, high], py)
        self.begin(out.at[px, :, high], out.at[px, :, high], pc)
        self.py_low.wait_recv()
        b = self.begin(out.at[py, :, low], out.at[py, :, low], px)
        self.begin(out.at[py, :, low], out.at[py, :, low], pc)
        self.px_low.wait_recv()
        self.begin(out.at[px, :, low], out.at[px, :, low], pc)
        self.py_high.wait_recv()
        self.begin(out.at[py, :, high], out.at[py, :, high], pc)
        a.wait_recv()
        self.begin(out.at[across, :, high], out.at[across, :, high], pc)
        b.wait_recv()
        self.begin(out.at[across, :, low], out.at[across, :, low], pc)
        self.seen = (0, 1, 3, 4, 5, 7)

    def end(self):
        for n, copy in enumerate(self.copies):
            if n not in self.seen:
                copy.wait_recv()
            copy.wait_send()
        self.kept.wait()


def gather_scratch():
    return [pltpu.SemaphoreType.DMA((13,)), pltpu.SemaphoreType.DMA((13,)), pltpu.SemaphoreType.DMA]


def row_loop(rows, body):
    def one(i, carry):
        body(pl.ds(pl.multiple_of(i * 16, 16), 16))
        return carry

    lax.fori_loop(0, rows // 16, one, 0)


def normalized(values):
    average = jnp.mean(values, axis=-1, keepdims=True)
    centered = values - average
    variance = jnp.mean(centered * centered, axis=-1, keepdims=True)
    scale = lax.rsqrt(variance + 1e-05)
    return centered * scale, scale


def norm_back(values, grad, gain):
    unit, scale = normalized(values)
    weighted = grad * gain
    mean_one = jnp.mean(weighted, axis=-1, keepdims=True)
    mean_two = jnp.mean(weighted * unit, axis=-1, keepdims=True)
    return scale * (weighted - mean_one - unit * mean_two), grad * unit


def fetch_rows(w, first, held, sem, hi, sh):
    rows, width = w.shape[2], held.shape[1]

    def one(f, carry):
        s, t, h = rem(f, sh), rem(div(f, sh), 8), div(f, 8 * sh)
        pltpu.make_async_copy(
            w.at[h * sh + s, t, :, pl.ds(first, width)], held.at[pl.ds(pl.multiple_of(f * rows, rows), rows)], sem
        ).start()
        return carry

    lax.fori_loop(0, 8 * hi * sh, one, 0)


def fetched(held, sem):
    pltpu.make_async_copy(held, held, sem).wait()


def first_kernel(hi, sh, tok, piece, normed_all, vec, lengths, own, pieces, send_p, recv_p, send_q, recv_q, *sems):
    me, c, x, y, pc, px, py = spots()
    groups = hi * sh
    mine = lax.axis_index("hi") * sh + lax.axis_index("shard")
    barrier = pltpu.get_barrier_semaphore()
    across, around = [], []
    for i in range(1, groups):
        there = rem(mine + i, groups)
        across.append({"hi": div(there, sh), "shard": rem(there, sh)})
    for i in range(1, 8):
        around.append({"tp": rem(me + i, 8)})
    for peer in across + around:
        pl.semaphore_signal(barrier, inc=1, device_id=peer, device_id_type=MESH)
    pl.semaphore_wait(barrier, groups + 6)

    pieces[mine, me] = piece[...]
    spot = pieces.at[mine, me]
    first = [
        pltpu.make_async_remote_copy(
            src_ref=spot, dst_ref=spot, send_sem=send_p.at[i], recv_sem=recv_p.at[i], device_id=peer, device_id_type=MESH
        )
        for i, peer in enumerate(across)
    ]
    for copy in first:
        copy.start()
    for copy in first:
        copy.wait_recv()
    column = pieces.at[:, me]
    second = [
        pltpu.make_async_remote_copy(
            src_ref=column, dst_ref=column, send_sem=send_q.at[i], recv_sem=recv_q.at[i], device_id=peer, device_id_type=MESH
        )
        for i, peer in enumerate(around)
    ]
    for copy in second:
        copy.start()
    for copy in second:
        copy.wait_recv()
    width = tok.shape[1]
    parts = 8 * groups * 128 // width
    for q in range(width // 128):
        found = None
        for f in range(q * parts, (q + 1) * parts):
            value = pieces[f // (8 * sh) * sh + f % sh, f // sh % 8].astype(F32)
            found = value if found is None else found + value
        vec[:, q * 128 : (q + 1) * 128] = found
    for t in range(8):
        lengths[t : t + 1, :] = pieces[mine, t].astype(F32)[12:13, :]

    def body(at):
        unit, _ = normalized(tok[at, :].astype(F32))
        own[at, :] = (unit * vec[0:1, :] + vec[1:2, :]).astype(BF)

    row_loop(own.shape[0], body)
    spread = Gathering(own, normed_all, *sems)
    spread.start()
    spread.forward()
    spread.end()
    for copy in first + second:
        copy.wait_send()


def allowed_of(lengths, row, size):
    line = lengths[pl.ds(row, 1), :]
    ends = [line[:, 0:1]]
    for n in range(1, 3):
        ends.append(ends[-1] + line[:, n : n + 1])
    down = lax.broadcasted_iota(jnp.int32, (size, 1), 0)
    along = lax.broadcasted_iota(jnp.int32, (1, size), 1)

    def span(places):
        places = places.astype(F32)
        return sum(jnp.where(places >= end, 1.0, 0.0) for end in ends)

    span_down, span_along = span(down), span(along)
    tail = jnp.where(span_down == 3.0, down, 0)
    return (span_down == span_along) & (along <= down) & (along >= tail)


def probabilities(query, key, allowed):
    scores = lax.dot_general(query, key, (((1,), (1,)), ((), ())), preferred_element_type=F32) * HEAD ** (-0.5)
    scores = jnp.where(allowed, scores, -1e30)
    exponent = jnp.exp(scores - jnp.max(scores, axis=-1, keepdims=True))
    return exponent / jnp.sum(exponent, axis=-1, keepdims=True)


def attention_kernel(
    hi, sh, normed, w_any, lengths, vec, tok, cot, middle, normed_all, cot_all, qkv, att, total, own, w, w_sem, *scratch
):
    me, c, x, y, pc, px, py = spots()
    fetch_rows(w_any, 0, w, w_sem, hi, sh)
    meet((pc, px, py))
    spread_cot = Gathering(cot, cot_all, *scratch[9:])
    spread_cot.start()
    size = own.shape[0]
    hc = att.shape[1]
    fetched(w, w_sem)

    def one_row(r, carry):
        joined = jnp.dot(normed[r], w[:, : 3 * hc], preferred_element_type=F32)
        here = pl.ds(pl.multiple_of(me * hc, 128), hc)
        queries = (joined[:, :hc] + vec[4:5, here]).astype(BF)
        keys = joined[:, hc : 2 * hc].astype(BF)
        values = (joined[:, 2 * hc :] + vec[5:6, here]).astype(BF)
        qkv[r, :, :hc] = queries
        qkv[r, :, hc : 2 * hc] = keys
        qkv[r, :, 2 * hc :] = values
        allowed = allowed_of(lengths, r, size)
        rows = pl.ds(pl.multiple_of(r * size, size), size)
        for h in range(hc // HEAD):
            at = slice(h * HEAD, (h + 1) * HEAD)
            low = probabilities(queries[:, at], keys[:, at], allowed).astype(BF)
            att[rows, at] = jnp.dot(low, values[:, at], preferred_element_type=F32).astype(BF)
        return carry

    lax.fori_loop(0, 8, one_row, 0)
    sums = Summing(att, w.at[:, 3 * hc :], total, scratch[:6])
    sums.first()
    spread_cot.forward()
    sums.second()
    sums.third()

    def body(at):
        values = tok[at, :].astype(F32) + total[at, :] + vec[6:7, :]
        middle[at, :] = values
        unit, _ = normalized(values)
        own[at, :] = (unit * vec[2:3, :] + vec[3:4, :]).astype(BF)

    row_loop(own.shape[0], body)
    spread = Gathering(own, normed_all, *scratch[6:9])
    spread.start()
    spread.forward()
    sums.end()
    spread_cot.end()
    spread.end()


GELU_A = math.sqrt(2.0 / math.pi)


def mlp_kernel(hi, sh, normed, cot, w_any, vec, mom, activated, grad_before, mom_out, w_up, w_down, sems, *scratch):
    width = w_up.shape[1]
    swapped = Swapping(mom, mom_out, *scratch)

    @pl.when(pl.program_id(0) == 0)
    def _():
        fetch_rows(w_any, 0, w_up, sems.at[0], hi, sh)
        fetch_rows(w_any, width, w_down, sems.at[1], hi, sh)
        meet_all(group_peers())
        swapped.start()
        fetched(w_up, sems.at[0])
        fetched(w_down, sems.at[1])

    me = lax.axis_index("tp")
    each = vec.shape[1] // width
    for j in range(width // 256):
        at = slice(j * 256, (j + 1) * 256)
        bias = vec[pl.ds(8 + div(me, each), 1), pl.ds(pl.multiple_of(rem(me, each) * width + j * 256, 256), 256)]
        before = jnp.dot(normed[0], w_up[:, at], preferred_element_type=F32) + bias
        grad = jnp.dot(cot[0], w_down[:, at], preferred_element_type=F32)
        square = before * before
        slope = jnp.tanh(before * (GELU_A + GELU_A * 0.044715 * square))
        half = 0.5 * (1.0 + slope)
        activated[:, at] = (before * half).astype(BF)
        inner = GELU_A + 3.0 * GELU_A * 0.044715 * square
        grad_before[:, at] = (grad * (half + 0.5 * before * (1.0 - slope * slope) * inner)).astype(BF)

    @pl.when(pl.program_id(0) == pl.num_programs(0) - 1)
    def _():
        swapped.end()


def attention_back_kernel(hi, sh, branch, w_any, qkv, lengths, mom, grad_joined, mom_out, w, sem, *scratch):
    swapped = Swapping(mom, mom_out, *scratch)
    hc = w.shape[1]
    size = branch.shape[1]
    r = pl.program_id(0)

    @pl.when(r == 0)
    def _():
        fetch_rows(w_any, 3 * hc, w, sem, hi, sh)
        meet_all(group_peers())
        swapped.start()
        fetched(w, sem)

    grad_att = jnp.dot(branch[0], w[...], preferred_element_type=F32).astype(BF)
    allowed = allowed_of(lengths, r, size)
    scale = HEAD ** (-0.5)
    for h in range(hc // HEAD):
        at = slice(h * HEAD, (h + 1) * HEAD)
        query, key, value = (qkv[0, :, n * hc + h * HEAD : n * hc + (h + 1) * HEAD] for n in range(3))
        probability = probabilities(query, key, allowed)
        low = probability.astype(BF)
        grad = grad_att[:, at]
        grad_prob = lax.dot_general(grad, value, (((1,), (1,)), ((), ())), preferred_element_type=F32)
        row_total = jnp.sum(probability * grad_prob, axis=-1, keepdims=True)
        grad_scores = (probability * (grad_prob - row_total)).astype(BF)
        made = (
            jnp.dot(grad_scores, key, preferred_element_type=F32) * scale,
            lax.dot_general(grad_scores, query, (((0,), (0,)), ((), ())), preferred_element_type=F32) * scale,
            lax.dot_general(low, grad, (((0,), (0,)), ((), ())), preferred_element_type=F32),
        )
        for n in range(3):
            grad_joined[:, n * hc + h * HEAD : n * hc + (h + 1) * HEAD] = made[n].astype(BF)

    @pl.when(r == pl.num_programs(0) - 1)
    def _():
        swapped.end()


def branch_kernel(
    hi, sh, grad_before, activated, w_any, middle, cot, vec, grad_middle, sums_out, branch_all, output, total, own,
    w_up, w_down, w_sem, *scratch
):
    me, c, x, y, pc, px, py = spots()
    fetch_rows(w_any, 0, w_up, w_sem.at[0], hi, sh)
    fetch_rows(w_any, w_up.shape[1], w_down, w_sem.at[1], hi, sh)
    meet((pc, px, py))
    fetched(w_up, w_sem.at[0])
    sums = Summing(grad_before, w_up, total, scratch[:6])
    sums.run()
    sums_out[...] = jnp.zeros_like(sums_out)

    def body(at):
        grad = total[at, :]
        part, for_gain = norm_back(middle[at, :], grad, vec[2:3, :])
        back = cot[at, :].astype(F32)
        whole = back + part
        grad_middle[at, :] = whole
        low = whole.astype(BF)
        own[at, :] = low
        low = low.astype(F32)
        for n, values in enumerate((for_gain, grad, low, back)):
            sums_out[n] += values[:8] + values[8:]

    row_loop(own.shape[0], body)
    spread = Gathering(own, branch_all, *scratch[6:9])
    spread.start()
    fetched(w_down, w_sem.at[1])
    more = Summing(activated, w_down, total, scratch[9:])
    more.first()
    spread.forward()
    more.second()
    more.third()

    def body_two(at):
        output[at, :] = (middle[at, :] + total[at, :] + vec[7:8, :]).astype(BF)

    row_loop(own.shape[0], body_two)
    sums.end()
    more.end()
    spread.end()


def last_kernel(
    hi, sh, grad_joined, w_attn, tok, grad_middle, vec, mom, grad, grad_tokens, sums_out, grad_back, ortho_back, total,
    w_qkv, w_sem, ortho, *scratch
):
    fetch_rows(w_attn, 0, w_qkv, w_sem, hi, sh)
    meet_all(group_peers() + [peer for _, peer in row_peers(hi, sh)])
    work = Orthogonal(hi, sh, mom, grad, ortho, scratch[6:13])
    grads = Swapping(grad, grad_back, *scratch[13:16])
    orthos = Swapping(ortho, ortho_back, *scratch[16:19])
    sums = Summing(grad_joined, w_qkv, total, scratch[:6])
    work.grams()
    fetched(w_qkv, w_sem)
    sums.first()
    grads.start()
    work.iterate()
    sums.second()
    work.finish()
    orthos.start()
    sums.third()
    sums_out[...] = jnp.zeros_like(sums_out)

    def body(at):
        there = total[at, :]
        part, for_gain = norm_back(tok[at, :].astype(F32), there, vec[0:1, :])
        grad_tokens[at, :] = grad_middle[at, :] + part
        for n, values in enumerate((for_gain, there)):
            sums_out[n] += values[:8] + values[8:]

    row_loop(total.shape[0], body)
    sums.end()
    grads.end()
    work.end()
    orthos.end()


def call(body, ins, outs, scratch, number, microseconds, name, grid=None):
    def spec(how):
        if how is True:
            return pl.BlockSpec(memory_space=pl.ANY)
        return pl.BlockSpec(memory_space=pltpu.VMEM) if how is False else pl.BlockSpec(*how)

    remote_params = {} if number is None else {"collective_id": number, "has_side_effects": True}
    return pl.pallas_call(
        body,
        out_shape=[jax.ShapeDtypeStruct(s.shape, s.dtype) for s, _ in outs],
        in_specs=[spec(how) for _, how in ins],
        out_specs=[spec(how) for _, how in outs],
        scratch_shapes=scratch,
        compiler_params=pltpu.CompilerParams(vmem_limit_bytes=60 * 2**20, **remote_params),
        cost_estimate=pl.CostEstimate(flops=0, transcendentals=0, bytes_accessed=int(microseconds * 3.0e6)),
        name=name,
        **({} if grid is None else {"grid": grid}),
    )(*[a for a, _ in ins])


class Swapping:
    def __init__(self, own, out, send, recv, local):
        me = lax.axis_index("tp")
        self.copies = []
        for i in range(1, 8):
            peer = rem(me + i, 8)
            self.copies.append(remote(own.at[peer], out.at[me], send.at[i - 1], recv.at[i - 1], peer))
        self.kept = pltpu.make_async_copy(own.at[me], out.at[me], local)

    def start(self):
        for copy in self.copies:
            copy.start()
        self.kept.start()

    def end(self):
        for copy in self.copies:
            copy.wait_recv()
        for copy in self.copies:
            copy.wait_send()
        self.kept.wait()


def swap_scratch():
    return [pltpu.SemaphoreType.DMA((7,)), pltpu.SemaphoreType.DMA((7,)), pltpu.SemaphoreType.DMA]


def group_peers():
    me = lax.axis_index("tp")
    return [{"tp": rem(me + i, 8)} for i in range(1, 8)]


def row_peers(hi, sh):
    mine = lax.axis_index("hi") * sh + lax.axis_index("shard")
    theres = [rem(mine + i, hi * sh) for i in range(1, hi * sh)]
    return [(there, {"hi": div(there, sh), "shard": rem(there, sh)}) for there in theres]


def meet_all(peers):
    barrier = pltpu.get_barrier_semaphore()
    for peer in peers:
        pl.semaphore_signal(barrier, inc=1, device_id=peer, device_id_type=MESH)
    pl.semaphore_wait(barrier, len(peers))


class Orthogonal:
    def __init__(self, hi, sh, mom, grad, out, scratch):
        self.mom, self.grad, self.out = mom, grad, out
        self.gram, self.arrived, self.power, self.send_a, self.recv_a, self.send_b, self.recv_b = scratch
        self.mine = lax.axis_index("hi") * sh + lax.axis_index("shard")
        self.peers = row_peers(hi, sh)
        self.count = out.shape[2] // PAIR
        self.per = self.gram.shape[0] // (hi * sh)

    def block(self, k):
        at = pl.ds(pl.multiple_of(k * PAIR, PAIR), PAIR)
        values = 0.95 * self.mom[:, :, at].astype(F32) + self.grad[:, :, at].astype(F32)
        return values.reshape(-1, PAIR).astype(BF), at

    def copy(self, i, src, dst, send, recv):
        return pltpu.make_async_remote_copy(
            src_ref=src, dst_ref=dst, send_sem=send.at[i], recv_sem=recv.at[i],
            device_id=self.peers[i][1], device_id_type=MESH,
        )

    def grams(self):
        one, two = slice(0, HEAD), slice(HEAD, PAIR)

        def one_gram(k, carry):
            values, _ = self.block(k)
            made = lax.dot_general(values, values, (((0,), (0,)), ((), ())), preferred_element_type=F32)
            self.gram[k, 0] = made[one, one].astype(BF)
            self.gram[k, 1] = made[two, two].astype(BF)
            return carry

        lax.fori_loop(0, self.count, one_gram, 0)
        for k in range(self.count, self.gram.shape[0]):
            self.gram[k] = jnp.zeros((2, HEAD, HEAD), BF)
        self.first = [
            self.copy(i, self.gram.at[pl.ds(there * self.per, self.per)], self.arrived.at[i], self.send_a, self.recv_a)
            for i, (there, _) in enumerate(self.peers)
        ]
        for copy in self.first:
            copy.start()

    def iterate(self):
        gram, arrived, per, mine = self.gram, self.arrived, self.per, self.mine
        one, two = slice(0, HEAD), slice(HEAD, PAIR)
        rows = lax.broadcasted_iota(jnp.int32, (PAIR, PAIR), 0)
        columns = lax.broadcasted_iota(jnp.int32, (PAIR, PAIR), 1)
        unit = jnp.where(rows == columns, 1.0, 0.0)
        upper = (rows < HEAD) & (rows == columns)
        lower = (rows >= HEAD) & (rows == columns)

        def product(a, b):
            a_high, b_high = a.astype(BF), b.astype(BF)
            a_low, b_low = (a - a_high.astype(F32)).astype(BF), (b - b_high.astype(F32)).astype(BF)
            made = jnp.dot(a_high, b_low, preferred_element_type=F32) + jnp.dot(a_low, b_high, preferred_element_type=F32)
            return made + jnp.dot(a_high, b_high, preferred_element_type=F32)

        for copy in self.first:
            copy.wait_recv()
        grams, wholes = [], []
        for j in range(per):
            halves = []
            for n in range(2):
                half = gram[mine * per + j, n].astype(F32)
                for i in range(len(self.peers)):
                    half = half + arrived[i, j, n].astype(F32)
                halves.append(half)
            empty = jnp.zeros((HEAD, HEAD), F32)
            total = jnp.concatenate(
                [jnp.concatenate([halves[0], empty], axis=1), jnp.concatenate([empty, halves[1]], axis=1)], axis=0
            )

            def scaling_of(chosen):
                trace = jnp.sum(jnp.sum(jnp.where(chosen, total, 0.0), axis=1, keepdims=True), axis=0, keepdims=True)
                return 1.0 / (jnp.sqrt(trace) + 1e-07)

            scaling = jnp.where(rows < HEAD, scaling_of(upper), scaling_of(lower))
            grams.append(total * (scaling * scaling))
            wholes.append(scaling)
        for number in range(NS_ITERS):
            squares = [product(a, a) for a in grams]
            steps = [COEF_A * unit + COEF_B * a + COEF_C * s for a, s in zip(grams, squares)]
            wholes = [product(w, p) for w, p in zip(wholes, steps)] if number else [w * p for w, p in zip(wholes, steps)]
            if number < NS_ITERS - 1:
                grams = [product(product(a, p), p) for a, p in zip(grams, steps)]
        for j in range(per):
            self.power[mine * per + j, 0] = wholes[j][one, one].astype(BF)
            self.power[mine * per + j, 1] = wholes[j][two, two].astype(BF)
        own = self.power.at[pl.ds(mine * per, per)]
        self.second = [self.copy(i, own, own, self.send_b, self.recv_b) for i in range(len(self.peers))]
        for copy in self.second:
            copy.start()

    def finish(self):
        one, two = slice(0, HEAD), slice(HEAD, PAIR)
        for copy in self.second:
            copy.wait_recv()

        def last(k, carry):
            values, at = self.block(k)
            made = [
                jnp.dot(values[:, side], self.power[k, n], preferred_element_type=F32) for n, side in enumerate((one, two))
            ]
            made = jnp.concatenate(made, axis=1).astype(BF)
            self.out[:, :, at] = made.reshape(self.out.shape[0], self.out.shape[1], PAIR)
            return carry

        lax.fori_loop(0, self.count, last, 0)

    def end(self):
        for copy in self.first + self.second:
            copy.wait_send()


def ortho_scratch(groups, columns):
    per = -(-(columns // PAIR) // groups)
    return [
        pltpu.VMEM((groups * per, 2, HEAD, HEAD), BF),
        pltpu.VMEM((groups - 1, per, 2, HEAD, HEAD), BF),
        pltpu.VMEM((groups * per, 2, HEAD, HEAD), BF),
    ] + [pltpu.SemaphoreType.DMA((groups - 1,))] * 4


def ortho_kernel(hi, sh, mom, grad, grad_back, ortho_back, ortho, *scratch):
    meet_all(group_peers() + [peer for _, peer in row_peers(hi, sh)])
    work = Orthogonal(hi, sh, mom, grad, ortho, scratch[:7])
    grads = Swapping(grad, grad_back, *scratch[7:10])
    orthos = Swapping(ortho, ortho_back, *scratch[10:13])
    work.grams()
    grads.start()
    work.iterate()
    work.finish()
    orthos.start()
    grads.end()
    work.end()
    orthos.end()


def dot(spec, a, b, **kw):
    return jnp.einsum(spec, a, b, preferred_element_type=F32, **kw)


def local(tokens, doc_lengths, weights, momentum, vectors, vector_moment, vector_second, cotangent):
    hi, tp, sh = (lax.axis_size(a) for a in ALL)
    groups, world = hi * sh, hi * tp * sh
    rows, blocks, head = weights.shape
    row_tokens, d = tokens.shape
    heads = HEADS // tp
    inner_all = (blocks - 4 * HEADS) // 2
    inner = inner_all // tp
    attn_blocks = 4 * heads
    me = lax.axis_index("tp")
    t_all = tp * row_tokens

    def arrange(array):
        attn = array[:, : 4 * HEADS].reshape(rows, 4, tp, heads, head).transpose(2, 0, 1, 3, 4).reshape(tp, rows, attn_blocks * head)
        mlp = array[:, 4 * HEADS :].reshape(rows, 2, tp, inner, head).transpose(2, 0, 1, 3, 4).reshape(tp, rows, 2 * inner * head)
        return attn, mlp

    def restore(attn, mlp):
        attn = attn.reshape(tp, rows, 4, heads, head).transpose(1, 2, 0, 3, 4).reshape(rows, 4 * HEADS, head)
        mlp = mlp.reshape(tp, rows, 2, inner, head).transpose(1, 2, 0, 3, 4).reshape(rows, 2 * inner_all, head)
        return jnp.concatenate([attn, mlp], axis=1)

    def swap(array):
        return lax.all_to_all(array, "tp", split_axis=0, concat_axis=0, tiled=True)

    attn_send, mlp_send = arrange(weights.astype(BF))

    def spread(array):
        return lax.all_gather(array, FS, axis=0, tiled=False)

    w_attn = spread(swap(attn_send))
    mlp_swapped, tokens = lax.optimization_barrier((swap(mlp_send), tokens))
    w_mlp = spread(mlp_swapped)

    flat = (lax.axis_index("hi") * tp + me) * sh + lax.axis_index("shard")
    lanes = 128 // rows
    spot = lax.broadcasted_iota(jnp.int32, (1, 128), 1) // rows == flat % lanes
    piece = jnp.where(spot, jnp.tile(vectors.T, (1, lanes)), 0.0)
    count = vectors.shape[1]
    spans = jnp.pad(doc_lengths.astype(F32), ((0, 15 - count), (0, 128 - doc_lengths.shape[1])))
    piece = jnp.concatenate([piece, spans], axis=0).astype(BF)

    gathered = jax.ShapeDtypeStruct((tp, row_tokens, d), BF)
    own_f32 = jax.ShapeDtypeStruct((row_tokens, d), F32)
    own_bf = jax.ShapeDtypeStruct((row_tokens, d), BF)
    own_scratch = [pltpu.VMEM(own_f32.shape, F32), pltpu.VMEM(own_f32.shape, BF)]
    small = [pltpu.SemaphoreType.DMA((groups,))] * 2 + [pltpu.SemaphoreType.DMA((8,))] * 2
    normed_one, vec_rows, lengths = call(
        partial(first_kernel, hi, sh),
        [(tokens, False), (piece, False)],
        [
            (gathered, True),
            (jax.ShapeDtypeStruct((16, d), F32), False),
            (jax.ShapeDtypeStruct((8, 128), F32), False),
        ],
        [own_scratch[1], pltpu.VMEM((groups, 8, 16, 128), BF)] + small + gather_scratch(),
        1,
        50,
        "first_norm",
    )

    hc = heads * head
    units = inner * head
    middle, normed_two, cot_all, qkv, attended = call(
        partial(attention_kernel, hi, sh),
        [(normed_one, False), (w_attn, True), (lengths, False), (vec_rows, False), (tokens, False), (cotangent, True)],
        [
            (own_f32, False),
            (gathered, True),
            (gathered, True),
            (jax.ShapeDtypeStruct((tp, row_tokens, 3 * hc), BF), False),
            (jax.ShapeDtypeStruct((t_all, hc), BF), False),
        ],
        own_scratch
        + [pltpu.VMEM((d, 4 * hc), BF), pltpu.SemaphoreType.DMA]
        + sum_scratch(row_tokens, d)
        + gather_scratch() * 2,
        2,
        110,
        "attention",
    )

    normed_two, momentum_now = lax.optimization_barrier((normed_two, momentum))
    send_attn, send_mlp = lax.optimization_barrier(arrange(momentum_now.astype(BF)))

    def rows_of(width):
        return (row_tokens, width), lambda r: (r, 0)

    def row_of(width):
        return (1, row_tokens, width), lambda r: (r, 0, 0)

    def fixed(array):
        return array.shape, lambda r: (0,) * array.ndim

    activated, grad_before, mom_mlp = call(
        partial(mlp_kernel, hi, sh),
        [(normed_two, row_of(d)), (cot_all, row_of(d)), (w_mlp, True), (vec_rows, fixed(vec_rows)), (send_mlp, True)],
        [(jax.ShapeDtypeStruct((t_all, units), BF), rows_of(units))] * 2 + [(send_mlp, True)],
        [pltpu.VMEM((d, units), BF)] * 2 + [pltpu.SemaphoreType.DMA((2,))] + swap_scratch(),
        7,
        30,
        "hidden_units",
        grid=(tp,),
    )
    flat_one, flat_two, flat_cot = (a.reshape(t_all, d) for a in (normed_one, normed_two, cot_all))

    def summed(left_right):
        parts = [dot("td,tn->dn", a, b).astype(BF) for a, b in left_right]
        part = parts[0] if len(parts) == 1 else jnp.concatenate(parts, axis=1)
        stacked = part.reshape(hi, tp, sh, rows, -1).transpose(0, 2, 1, 3, 4).reshape(groups, tp * rows, -1)
        return stacked

    def sent(stacked):
        return lax.psum_scatter(stacked, FS, scatter_dimension=0, tiled=False)

    s_down = summed([(flat_cot, activated)])
    s_up = summed([(flat_two, grad_before)])
    grad_before, s_down, s_up = lax.optimization_barrier((grad_before, s_down, s_up))
    g_down, g_up = sent(s_down), sent(s_up)

    grad_middle, sums_two, grad_branch, output = call(
        partial(branch_kernel, hi, sh),
        [(grad_before, False), (activated, False), (w_mlp, True), (middle, False), (cotangent, False), (vec_rows, False)],
        [(own_f32, False), (jax.ShapeDtypeStruct((4, 8, d), F32), False), (gathered, True), (own_bf, False)],
        own_scratch
        + [pltpu.VMEM((d, units), BF)] * 2
        + [pltpu.SemaphoreType.DMA((2,))]
        + sum_scratch(row_tokens, d)
        + gather_scratch()
        + sum_scratch(row_tokens, d),
        3,
        115,
        "second_norm_backward",
    )
    grad_branch, g_down = lax.optimization_barrier((grad_branch, g_down))
    grad_joined, mom_attn = call(
        partial(attention_back_kernel, hi, sh),
        [(grad_branch, row_of(d)), (w_attn, True), (qkv, row_of(3 * hc)), (lengths, fixed(lengths)), (send_attn, True)],
        [(jax.ShapeDtypeStruct((t_all, 3 * hc), BF), rows_of(3 * hc)), (send_attn, True)],
        [pltpu.VMEM((d, hc), BF), pltpu.SemaphoreType.DMA] + swap_scratch(),
        8,
        25,
        "attention_backward",
        grid=(tp,),
    )
    grad_branch = grad_branch.reshape(t_all, d)
    s_attn = summed([(flat_one, grad_joined), (grad_branch, attended)])
    grad_joined, s_attn = lax.optimization_barrier((grad_joined, s_attn))
    g_attn = sent(s_attn).reshape(send_attn.shape)
    g_mlp = jnp.concatenate([g_up, g_down], axis=1).reshape(send_mlp.shape)
    grad_tokens, sums_one, back_mlp, ortho_mlp = call(
        partial(last_kernel, hi, sh),
        [(grad_joined, False), (w_attn, True), (tokens, False), (grad_middle, False), (vec_rows, False)]
        + [(mom_mlp, False), (g_mlp, False)],
        [(own_f32, False), (jax.ShapeDtypeStruct((2, 8, d), F32), False), (send_mlp, True), (send_mlp, True)],
        own_scratch[:1]
        + [pltpu.VMEM((d, 3 * hc), BF), pltpu.SemaphoreType.DMA, pltpu.VMEM(send_mlp.shape, BF)]
        + sum_scratch(row_tokens, d)
        + ortho_scratch(groups, send_mlp.shape[2])
        + swap_scratch() * 2,
        4,
        75,
        "first_norm_backward",
    )
    grad_tokens, g_attn = lax.optimization_barrier((grad_tokens, g_attn))

    back_attn, ortho_attn = call(
        partial(ortho_kernel, hi, sh),
        [(mom_attn, False), (g_attn, False)],
        [(send_attn, True), (send_attn, True)],
        [pltpu.VMEM(send_attn.shape, BF)] + ortho_scratch(groups, send_attn.shape[2]) + swap_scratch() * 2,
        6,
        30,
        "orthogonalize_attention",
    )
    weight_grad = restore(back_attn, back_mlp).astype(F32)
    moment_new = 0.95 * momentum + weight_grad
    orthogonal_rows = restore(ortho_attn, ortho_mlp).astype(F32)
    new_weights = weights * (1.0 - 0.15 * 0.1) - 0.15 * 0.2 * math.sqrt(d) * orthogonal_rows

    sums_one, sums_two = jnp.sum(sums_one, axis=1), jnp.sum(sums_two, axis=1)
    plain = jnp.stack(
        [
            sums_one[0],
            sums_one[1],
            sums_two[0],
            sums_two[1],
            jnp.zeros((d,), F32),
            jnp.zeros((d,), F32),
            sums_two[2],
            sums_two[3],
        ],
        axis=0,
    )
    plain = lax.dynamic_update_slice(plain, jnp.sum(grad_joined[:, :hc], axis=0, dtype=F32)[None], (4, me * hc))
    plain = lax.dynamic_update_slice(plain, jnp.sum(grad_joined[:, 2 * hc :], axis=0, dtype=F32)[None], (5, me * hc))
    hidden = jnp.zeros((inner_all * head,), F32)
    hidden = lax.dynamic_update_slice(hidden, jnp.sum(grad_before, axis=0, dtype=F32), (me * inner * head,))
    terms = jnp.concatenate([plain, hidden.reshape(-1, d)], axis=0)
    terms = terms.reshape(-1, world, rows).transpose(1, 0, 2).reshape(world, -1)
    vector_grad = jnp.sum(lax.all_to_all(terms, ALL, split_axis=0, concat_axis=0, tiled=True), axis=0)
    vector_grad = vector_grad.reshape(-1, rows).T
    first_moment = 0.9 * vector_moment + 0.1 * vector_grad
    second = 0.95 * vector_second + 0.05 * vector_grad * vector_grad
    corrected = first_moment / (1.0 - 0.9**STEP)
    normal_second = second / (1.0 - 0.95**STEP)
    next_vectors = vectors - 0.5 * corrected / (jnp.sqrt(normal_second) + 1e-08)
    return (
        output,
        grad_tokens,
        weight_grad,
        new_weights,
        moment_new,
        first_moment,
        second,
        next_vectors,
    )


def solution(mesh):
    dp, sh = mesh.shape["dp"], mesh.shape["shard"]
    tp = math.gcd(dp, 8)
    fine = Mesh(mesh.devices.reshape(dp // tp, tp, sh), ALL)
    two, three = P(ALL, None), P(ALL, None, None)
    return jax.shard_map(
        local,
        mesh=fine,
        in_specs=(two, two, three, three, two, two, two, two),
        out_specs=(two, two, three, three, three, two, two, two),
        check_vma=False,
    )
```

```python
from functools import partial
import math

import jax
import jax.numpy as jnp
from jax import lax
from jax.experimental import pallas as pl
from jax.experimental.pallas import tpu as pltpu
from jax.sharding import Mesh, PartitionSpec as P

HEADS = 16
HEAD = 128
PAIR = 2 * HEAD
NS_ITERS = 5
STEP = 10

COEF_A = 3.4445
COEF_B = -4.775
COEF_C = 2.0315
BF = jnp.bfloat16
F32 = jnp.float32
ALL = ("hi", "tp", "shard")
FS = ("hi", "shard")


MESH = pl.DeviceIdType.MESH
WIDE = 256


def rem(a, b):
    return lax.rem(a, jnp.int32(b))


def div(a, b):
    return lax.div(a, jnp.int32(b))


def spots():
    me = lax.axis_index("tp")
    c, x, y = rem(me, 2), rem(div(me, 2), 2), div(me, 4)
    return me, c, x, y, me + 1 - 2 * c, me + 2 - 4 * x, me + 4 - 8 * y


def meet(peers):
    barrier = pltpu.get_barrier_semaphore()
    for peer in peers:
        pl.semaphore_signal(barrier, inc=1, device_id={"tp": peer}, device_id_type=MESH)
    pl.semaphore_wait(barrier, len(peers))


def remote(src, dst, send, recv, peer):
    return pltpu.make_async_remote_copy(
        src_ref=src, dst_ref=dst, send_sem=send, recv_sem=recv, device_id={"tp": peer}, device_id_type=MESH
    )


def sum_scratch(rows, width):
    count = width // WIDE
    return [
        pltpu.VMEM((count, 2, 2, 2, rows, WIDE), BF),
        pltpu.VMEM((count, 2, 2, rows, WIDE), BF),
        pltpu.VMEM((count, 2, rows, WIDE), BF),
        pltpu.VMEM((count, rows, WIDE), BF),
        pltpu.SemaphoreType.DMA((3, count)),
        pltpu.SemaphoreType.DMA((3, count)),
    ]


class Summing:
    def __init__(self, left, right, total, scratch):
        self.left, self.right, self.total = left, right, total
        self.part, self.from_c, self.from_1, self.from_2, self.send, self.recv = scratch
        self.count = self.part.shape[0]
        self.rows = self.part.shape[4]

    def fill(self, k):
        right = self.right[k * WIDE : (k + 1) * WIDE, :]

        def one(dest, carry):
            rows = self.left[pl.ds(pl.multiple_of(dest * self.rows, self.rows), self.rows), :]
            made = lax.dot_general(rows, right, (((1,), (1,)), ((), ())), preferred_element_type=F32)
            self.part[k, div(dest, 4), rem(div(dest, 2), 2), rem(dest, 2)] = made.astype(BF)
            return carry

        lax.fori_loop(0, 8, one, 0)

    def copy(self, stage, k, at):
        me, c, x, y, pc, px, py = at
        even = k % 2 == 0
        if stage == 0:
            src, dst, peer = self.part.at[k, :, :, 1 - c], self.from_c.at[k], pc
        elif stage == 1:
            src = self.part.at[k, :, 1 - x, c] if even else self.part.at[k, 1 - y, :, c]
            dst, peer = self.from_1.at[k], px if even else py
        else:
            src = self.part.at[k, 1 - y, x, c] if even else self.part.at[k, y, 1 - x, c]
            dst, peer = self.from_2.at[k], py if even else px
        return remote(src, dst, self.send.at[stage, k], self.recv.at[stage, k], peer)

    def run(self):
        self.first()
        self.second()
        self.third()

    def first(self):
        at = spots()
        c = at[1]
        part = self.part

        def core_stage(k):
            self.copy(0, k, at).wait_recv()
            for i in range(4):
                a, b = i // 2, i % 2
                part[k, a, b, c] = (part[k, a, b, c].astype(F32) + self.from_c[k, a, b].astype(F32)).astype(BF)
            self.copy(1, k, at).start()

        for k in range(self.count):
            self.fill(k)
            self.copy(0, k, at).start()
            if k:
                core_stage(k - 1)
        core_stage(self.count - 1)

    def second(self):
        at = spots()
        _, c, x, y = at[:4]
        part = self.part
        for k in range(self.count):
            self.copy(1, k, at).wait_recv()
            for i in range(2):
                if k % 2 == 0:
                    part[k, i, x, c] = (part[k, i, x, c].astype(F32) + self.from_1[k, i].astype(F32)).astype(BF)
                else:
                    part[k, y, i, c] = (part[k, y, i, c].astype(F32) + self.from_1[k, i].astype(F32)).astype(BF)
            self.copy(2, k, at).start()

    def third(self):
        at = spots()
        _, c, x, y = at[:4]
        for k in range(self.count):
            self.copy(2, k, at).wait_recv()
            self.total[:, k * WIDE : (k + 1) * WIDE] = self.part[k, y, x, c].astype(F32) + self.from_2[k].astype(F32)

    def end(self):
        at = spots()
        for stage in range(3):
            for k in range(self.count):
                self.copy(stage, k, at).wait_send()


class Gathering:
    def __init__(self, own, out, send, recv, local):
        self.own, self.out, self.send, self.recv, self.local = own, out, send, recv, local
        self.copies = []

    def begin(self, src, dst, peer):
        n = len(self.copies)
        copy = remote(src, dst, self.send.at[n], self.recv.at[n], peer)
        copy.start()
        self.copies.append(copy)
        return copy

    def start(self):
        me, c, x, y, pc, px, py = spots()
        self.spots = me, px, py, pc
        own, out = self.own, self.out
        half = own.shape[-1] // 2
        self.low, self.high = pl.ds(0, half), pl.ds(half, half)
        low, high = self.low, self.high
        self.px_high = self.begin(own.at[:, high], out.at[me, :, high], px)
        self.py_low = self.begin(own.at[:, low], out.at[me, :, low], py)
        self.begin(own, out.at[me], pc)
        self.px_low = self.begin(own.at[:, low], out.at[me, :, low], px)
        self.py_high = self.begin(own.at[:, high], out.at[me, :, high], py)
        self.kept = pltpu.make_async_copy(own, out.at[me], self.local)
        self.kept.start()

    def forward(self):
        me, px, py, pc = self.spots
        out, low, high = self.out, self.low, self.high
        across = px + py - me
        self.px_high.wait_recv()
        a = self.begin(out.at[px, :, high], out.at[px, :, high], py)
        self.begin(out.at[px, :, high], out.at[px, :, high], pc)
        self.py_low.wait_recv()
        b = self.begin(out.at[py, :, low], out.at[py, :, low], px)
        self.begin(out.at[py, :, low], out.at[py, :, low], pc)
        self.px_low.wait_recv()
        self.begin(out.at[px, :, low], out.at[px, :, low], pc)
        self.py_high.wait_recv()
        self.begin(out.at[py, :, high], out.at[py, :, high], pc)
        a.wait_recv()
        self.begin(out.at[across, :, high], out.at[across, :, high], pc)
        b.wait_recv()
        self.begin(out.at[across, :, low], out.at[across, :, low], pc)
        self.seen = (0, 1, 3, 4, 5, 7)

    def end(self):
        for n, copy in enumerate(self.copies):
            if n not in self.seen:
                copy.wait_recv()
            copy.wait_send()
        self.kept.wait()


def gather_scratch():
    return [pltpu.SemaphoreType.DMA((13,)), pltpu.SemaphoreType.DMA((13,)), pltpu.SemaphoreType.DMA]


def row_loop(rows, body):
    def one(i, carry):
        body(pl.ds(pl.multiple_of(i * 16, 16), 16))
        return carry

    lax.fori_loop(0, rows // 16, one, 0)


def normalized(values):
    average = jnp.mean(values, axis=-1, keepdims=True)
    centered = values - average
    variance = jnp.mean(centered * centered, axis=-1, keepdims=True)
    scale = lax.rsqrt(variance + 1e-05)
    return centered * scale, scale


def norm_back(values, grad, gain):
    unit, scale = normalized(values)
    weighted = grad * gain
    mean_one = jnp.mean(weighted, axis=-1, keepdims=True)
    mean_two = jnp.mean(weighted * unit, axis=-1, keepdims=True)
    return scale * (weighted - mean_one - unit * mean_two), grad * unit


def fetch_rows(w, first, held, sem, hi, sh):
    rows, width = w.shape[2], held.shape[1]

    def one(f, carry):
        s, t, h = rem(f, sh), rem(div(f, sh), 8), div(f, 8 * sh)
        pltpu.make_async_copy(
            w.at[h * sh + s, t, :, pl.ds(first, width)], held.at[pl.ds(pl.multiple_of(f * rows, rows), rows)], sem
        ).start()
        return carry

    lax.fori_loop(0, 8 * hi * sh, one, 0)


def fetched(held, sem):
    pltpu.make_async_copy(held, held, sem).wait()


def first_kernel(hi, sh, tok, piece, normed_all, vec, lengths, own, pieces, send_p, recv_p, send_q, recv_q, *sems):
    me, c, x, y, pc, px, py = spots()
    groups = hi * sh
    mine = lax.axis_index("hi") * sh + lax.axis_index("shard")
    barrier = pltpu.get_barrier_semaphore()
    across, around = [], []
    for i in range(1, groups):
        there = rem(mine + i, groups)
        across.append({"hi": div(there, sh), "shard": rem(there, sh)})
    for i in range(1, 8):
        around.append({"tp": rem(me + i, 8)})
    for peer in across + around:
        pl.semaphore_signal(barrier, inc=1, device_id=peer, device_id_type=MESH)
    pl.semaphore_wait(barrier, groups + 6)

    pieces[mine, me] = piece[...]
    spot = pieces.at[mine, me]
    first = [
        pltpu.make_async_remote_copy(
            src_ref=spot, dst_ref=spot, send_sem=send_p.at[i], recv_sem=recv_p.at[i], device_id=peer, device_id_type=MESH
        )
        for i, peer in enumerate(across)
    ]
    for copy in first:
        copy.start()
    for copy in first:
        copy.wait_recv()
    column = pieces.at[:, me]
    second = [
        pltpu.make_async_remote_copy(
            src_ref=column, dst_ref=column, send_sem=send_q.at[i], recv_sem=recv_q.at[i], device_id=peer, device_id_type=MESH
        )
        for i, peer in enumerate(around)
    ]
    for copy in second:
        copy.start()
    for copy in second:
        copy.wait_recv()
    width = tok.shape[1]
    parts = 8 * groups * 128 // width
    for q in range(width // 128):
        found = None
        for f in range(q * parts, (q + 1) * parts):
            value = pieces[f // (8 * sh) * sh + f % sh, f // sh % 8].astype(F32)
            found = value if found is None else found + value
        vec[:, q * 128 : (q + 1) * 128] = found
    for t in range(8):
        lengths[t : t + 1, :] = pieces[mine, t].astype(F32)[12:13, :]

    def body(at):
        unit, _ = normalized(tok[at, :].astype(F32))
        own[at, :] = (unit * vec[0:1, :] + vec[1:2, :]).astype(BF)

    row_loop(own.shape[0], body)
    spread = Gathering(own, normed_all, *sems)
    spread.start()
    spread.forward()
    spread.end()
    for copy in first + second:
        copy.wait_send()


def allowed_of(lengths, row, size):
    line = lengths[pl.ds(row, 1), :]
    ends = [line[:, 0:1]]
    for n in range(1, 3):
        ends.append(ends[-1] + line[:, n : n + 1])
    down = lax.broadcasted_iota(jnp.int32, (size, 1), 0)
    along = lax.broadcasted_iota(jnp.int32, (1, size), 1)

    def span(places):
        places = places.astype(F32)
        return sum(jnp.where(places >= end, 1.0, 0.0) for end in ends)

    span_down, span_along = span(down), span(along)
    tail = jnp.where(span_down == 3.0, down, 0)
    return (span_down == span_along) & (along <= down) & (along >= tail)


def probabilities(query, key, allowed):
    scores = lax.dot_general(query, key, (((1,), (1,)), ((), ())), preferred_element_type=F32) * HEAD ** (-0.5)
    scores = jnp.where(allowed, scores, -1e30)
    exponent = jnp.exp(scores - jnp.max(scores, axis=-1, keepdims=True))
    return exponent / jnp.sum(exponent, axis=-1, keepdims=True)


def attention_kernel(
    hi, sh, normed, w_any, lengths, vec, tok, cot, mom, middle, normed_all, cot_all, qkv, att, mom_out, total, own, w,
    w_sem, *scratch
):
    me, c, x, y, pc, px, py = spots()
    fetch_rows(w_any, 0, w, w_sem, hi, sh)
    meet_all(group_peers())
    spread_cot = Gathering(cot, cot_all, *scratch[9:12])
    spread_cot.start()
    swapped = Swapping(mom, mom_out, *scratch[12:])
    size = own.shape[0]
    hc = att.shape[1]
    fetched(w, w_sem)

    def one_row(r, carry):
        joined = jnp.dot(normed[r], w[:, : 3 * hc], preferred_element_type=F32)
        here = pl.ds(pl.multiple_of(me * hc, 128), hc)
        queries = (joined[:, :hc] + vec[4:5, here]).astype(BF)
        keys = joined[:, hc : 2 * hc].astype(BF)
        values = (joined[:, 2 * hc :] + vec[5:6, here]).astype(BF)
        qkv[r, :, :hc] = queries
        qkv[r, :, hc : 2 * hc] = keys
        qkv[r, :, 2 * hc :] = values
        allowed = allowed_of(lengths, r, size)
        rows = pl.ds(pl.multiple_of(r * size, size), size)
        for h in range(hc // HEAD):
            at = slice(h * HEAD, (h + 1) * HEAD)
            low = probabilities(queries[:, at], keys[:, at], allowed).astype(BF)
            att[rows, at] = jnp.dot(low, values[:, at], preferred_element_type=F32).astype(BF)
        return carry

    lax.fori_loop(0, 8, one_row, 0)
    sums = Summing(att, w.at[:, 3 * hc :], total, scratch[:6])
    sums.first()
    spread_cot.forward()
    swapped.start()
    sums.second()
    sums.third()

    def body(at):
        values = tok[at, :].astype(F32) + total[at, :] + vec[6:7, :]
        middle[at, :] = values
        unit, _ = normalized(values)
        own[at, :] = (unit * vec[2:3, :] + vec[3:4, :]).astype(BF)

    row_loop(own.shape[0], body)
    spread = Gathering(own, normed_all, *scratch[6:9])
    spread.start()
    spread.forward()
    sums.end()
    spread_cot.end()
    spread.end()
    swapped.end()


GELU_A = math.sqrt(2.0 / math.pi)


def mlp_kernel(hi, sh, normed, cot, w_any, vec, mom, activated, grad_before, mom_out, w_up, w_down, sems, *scratch):
    width = w_up.shape[1]
    swapped = Swapping(mom, mom_out, *scratch)

    @pl.when(pl.program_id(0) == 0)
    def _():
        fetch_rows(w_any, 0, w_up, sems.at[0], hi, sh)
        fetch_rows(w_any, width, w_down, sems.at[1], hi, sh)
        meet_all(group_peers())
        swapped.start()
        fetched(w_up, sems.at[0])
        fetched(w_down, sems.at[1])

    me = lax.axis_index("tp")
    each = vec.shape[1] // width
    for j in range(width // 256):
        at = slice(j * 256, (j + 1) * 256)
        bias = vec[pl.ds(8 + div(me, each), 1), pl.ds(pl.multiple_of(rem(me, each) * width + j * 256, 256), 256)]
        before = jnp.dot(normed[0], w_up[:, at], preferred_element_type=F32) + bias
        grad = jnp.dot(cot[0], w_down[:, at], preferred_element_type=F32)
        square = before * before
        slope = jnp.tanh(before * (GELU_A + GELU_A * 0.044715 * square))
        half = 0.5 * (1.0 + slope)
        activated[:, at] = (before * half).astype(BF)
        inner = GELU_A + 3.0 * GELU_A * 0.044715 * square
        grad_before[:, at] = (grad * (half + 0.5 * before * (1.0 - slope * slope) * inner)).astype(BF)

    @pl.when(pl.program_id(0) == pl.num_programs(0) - 1)
    def _():
        swapped.end()


def attention_back_kernel(
    hi, sh, branch, w_any, qkv, lengths, grad_down, grad_joined, back_down, w, sem, *scratch
):
    swapped = Swapping(grad_down, back_down, *scratch)
    hc = w.shape[1]
    size = branch.shape[1]
    r = pl.program_id(0)

    @pl.when(r == 0)
    def _():
        fetch_rows(w_any, 3 * hc, w, sem, hi, sh)
        meet_all(group_peers())
        swapped.start()
        fetched(w, sem)

    grad_att = jnp.dot(branch[0], w[...], preferred_element_type=F32).astype(BF)
    allowed = allowed_of(lengths, r, size)
    scale = HEAD ** (-0.5)
    for h in range(hc // HEAD):
        at = slice(h * HEAD, (h + 1) * HEAD)
        query, key, value = (qkv[0, :, n * hc + h * HEAD : n * hc + (h + 1) * HEAD] for n in range(3))
        probability = probabilities(query, key, allowed)
        low = probability.astype(BF)
        grad = grad_att[:, at]
        grad_prob = lax.dot_general(grad, value, (((1,), (1,)), ((), ())), preferred_element_type=F32)
        row_total = jnp.sum(probability * grad_prob, axis=-1, keepdims=True)
        grad_scores = (probability * (grad_prob - row_total)).astype(BF)
        made = (
            jnp.dot(grad_scores, key, preferred_element_type=F32) * scale,
            lax.dot_general(grad_scores, query, (((0,), (0,)), ((), ())), preferred_element_type=F32) * scale,
            lax.dot_general(low, grad, (((0,), (0,)), ((), ())), preferred_element_type=F32),
        )
        for n in range(3):
            grad_joined[:, n * hc + h * HEAD : n * hc + (h + 1) * HEAD] = made[n].astype(BF)

    @pl.when(r == pl.num_programs(0) - 1)
    def _():
        swapped.end()


def branch_kernel(
    hi, sh, grad_before, activated, w_any, middle, cot, vec, grad_middle, sums_out, branch_all, output, total, own,
    w_up, w_down, w_sem, *scratch
):
    me, c, x, y, pc, px, py = spots()
    fetch_rows(w_any, 0, w_up, w_sem.at[0], hi, sh)
    fetch_rows(w_any, w_up.shape[1], w_down, w_sem.at[1], hi, sh)
    meet((pc, px, py))
    fetched(w_up, w_sem.at[0])
    sums = Summing(grad_before, w_up, total, scratch[:6])
    sums.run()
    sums_out[...] = jnp.zeros_like(sums_out)

    def body(at):
        grad = total[at, :]
        part, for_gain = norm_back(middle[at, :], grad, vec[2:3, :])
        back = cot[at, :].astype(F32)
        whole = back + part
        grad_middle[at, :] = whole
        low = whole.astype(BF)
        own[at, :] = low
        low = low.astype(F32)
        for n, values in enumerate((for_gain, grad, low, back)):
            sums_out[n] += values[:8] + values[8:]

    row_loop(own.shape[0], body)
    spread = Gathering(own, branch_all, *scratch[6:9])
    spread.start()
    fetched(w_down, w_sem.at[1])
    more = Summing(activated, w_down, total, scratch[9:])
    more.first()
    spread.forward()
    more.second()
    more.third()

    def body_two(at):
        output[at, :] = (middle[at, :] + total[at, :] + vec[7:8, :]).astype(BF)

    row_loop(own.shape[0], body_two)
    sums.end()
    more.end()
    spread.end()


def last_kernel(
    hi, sh, grad_joined, w_attn, tok, grad_middle, vec, mom, grad_up, grad_down, grad_tokens, sums_out, back_up, ortho_back,
    total, w_qkv, w_sem, grad, grad_sems, ortho, *scratch
):
    fetch_rows(w_attn, 0, w_qkv, w_sem, hi, sh)
    width = grad_up.shape[2]
    loads = [
        pltpu.make_async_copy(part, grad.at[:, :, pl.ds(n * width, width)], grad_sems.at[n])
        for n, part in enumerate((grad_up, grad_down))
    ]
    for load in loads:
        load.start()
    meet_all(group_peers() + [peer for _, peer in row_peers(hi, sh)])
    work = Orthogonal(hi, sh, mom, grad, ortho, scratch[6:13])
    ups = Swapping(grad_up, back_up, *scratch[13:16])
    orthos = Swapping(ortho, ortho_back, *scratch[16:19])
    sums = Summing(grad_joined, w_qkv, total, scratch[:6])
    fetched(w_qkv, w_sem)
    for load in loads:
        load.wait()
    work.grams()
    sums.first()
    ups.start()
    work.iterate()
    sums.second()
    work.finish()
    orthos.start()
    sums.third()
    sums_out[...] = jnp.zeros_like(sums_out)

    def body(at):
        there = total[at, :]
        part, for_gain = norm_back(tok[at, :].astype(F32), there, vec[0:1, :])
        grad_tokens[at, :] = grad_middle[at, :] + part
        for n, values in enumerate((for_gain, there)):
            sums_out[n] += values[:8] + values[8:]

    row_loop(total.shape[0], body)
    sums.end()
    ups.end()
    work.end()
    orthos.end()


def outer_kernel(*refs):
    *pairs, out = refs
    _, sh, some, rows, _ = out.shape
    first = 0
    for left, right in zip(pairs[::2], pairs[1::2]):
        made = lax.dot_general(
            left[...].reshape(-1, left.shape[-1]), right[...], (((0,), (0,)), ((), ())), preferred_element_type=F32
        ).astype(BF)
        n = right.shape[1]
        for a in range(some):
            for s in range(sh):
                at = (a * sh + s) * rows
                out[0, s, a, :, first : first + n] = made[at : at + rows]
        first += n


def outer(pairs, hi, sh, name):
    tp, tokens, d = pairs[0][0].shape
    n = sum(right.shape[1] for _, right in pairs)
    rows = d // (hi * tp * sh)
    some = 256 // (sh * rows)
    turns = tp // some
    ins = []
    for left, right in pairs:
        ins += [(left, ((tp, tokens, 256), lambda i: (0, 0, i))), (right, (right.shape, lambda i: (0, 0)))]
    (made,) = call(
        outer_kernel,
        ins,
        [
            (
                jax.ShapeDtypeStruct((hi, sh, tp, rows, n), BF),
                ((1, sh, some, rows, n), lambda i: (i // turns, 0, i % turns, 0, 0)),
            )
        ],
        [],
        None,
        n / 70,
        name,
        grid=(d // 256,),
    )
    return made.reshape(hi * sh, tp * rows, n)


def call(body, ins, outs, scratch, number, microseconds, name, grid=None):
    def spec(how):
        if how is True:
            return pl.BlockSpec(memory_space=pl.ANY)
        return pl.BlockSpec(memory_space=pltpu.VMEM) if how is False else pl.BlockSpec(*how)

    remote_params = {} if number is None else {"collective_id": number, "has_side_effects": True}
    return pl.pallas_call(
        body,
        out_shape=[jax.ShapeDtypeStruct(s.shape, s.dtype) for s, _ in outs],
        in_specs=[spec(how) for _, how in ins],
        out_specs=[spec(how) for _, how in outs],
        scratch_shapes=scratch,
        compiler_params=pltpu.CompilerParams(vmem_limit_bytes=60 * 2**20, **remote_params),
        cost_estimate=pl.CostEstimate(flops=0, transcendentals=0, bytes_accessed=int(microseconds * 3.0e6)),
        name=name,
        **({} if grid is None else {"grid": grid}),
    )(*[a for a, _ in ins])


class Swapping:
    def __init__(self, own, out, send, recv, local):
        me = lax.axis_index("tp")
        self.copies = []
        for i in range(1, 8):
            peer = rem(me + i, 8)
            self.copies.append(remote(own.at[peer], out.at[me], send.at[i - 1], recv.at[i - 1], peer))
        self.kept = pltpu.make_async_copy(own.at[me], out.at[me], local)

    def start(self):
        for copy in self.copies:
            copy.start()
        self.kept.start()

    def end(self):
        for copy in self.copies:
            copy.wait_recv()
        for copy in self.copies:
            copy.wait_send()
        self.kept.wait()


def swap_scratch():
    return [pltpu.SemaphoreType.DMA((7,)), pltpu.SemaphoreType.DMA((7,)), pltpu.SemaphoreType.DMA]


def group_peers():
    me = lax.axis_index("tp")
    return [{"tp": rem(me + i, 8)} for i in range(1, 8)]


def row_peers(hi, sh):
    mine = lax.axis_index("hi") * sh + lax.axis_index("shard")
    theres = [rem(mine + i, hi * sh) for i in range(1, hi * sh)]
    return [(there, {"hi": div(there, sh), "shard": rem(there, sh)}) for there in theres]


def meet_all(peers):
    barrier = pltpu.get_barrier_semaphore()
    for peer in peers:
        pl.semaphore_signal(barrier, inc=1, device_id=peer, device_id_type=MESH)
    pl.semaphore_wait(barrier, len(peers))


class Orthogonal:
    def __init__(self, hi, sh, mom, grad, out, scratch):
        self.mom, self.grad, self.out = mom, grad, out
        self.gram, self.arrived, self.power, self.send_a, self.recv_a, self.send_b, self.recv_b = scratch
        self.mine = lax.axis_index("hi") * sh + lax.axis_index("shard")
        self.peers = row_peers(hi, sh)
        self.count = out.shape[2] // PAIR
        self.per = self.gram.shape[0] // (hi * sh)

    def block(self, k):
        at = pl.ds(pl.multiple_of(k * PAIR, PAIR), PAIR)
        values = 0.95 * self.mom[:, :, at].astype(F32) + self.grad[:, :, at].astype(F32)
        return values.reshape(-1, PAIR).astype(BF), at

    def copy(self, i, src, dst, send, recv):
        return pltpu.make_async_remote_copy(
            src_ref=src, dst_ref=dst, send_sem=send.at[i], recv_sem=recv.at[i],
            device_id=self.peers[i][1], device_id_type=MESH,
        )

    def grams(self):
        one, two = slice(0, HEAD), slice(HEAD, PAIR)

        def one_gram(k, carry):
            values, _ = self.block(k)
            made = lax.dot_general(values, values, (((0,), (0,)), ((), ())), preferred_element_type=F32)
            self.gram[k, 0] = made[one, one].astype(BF)
            self.gram[k, 1] = made[two, two].astype(BF)
            return carry

        lax.fori_loop(0, self.count, one_gram, 0)
        for k in range(self.count, self.gram.shape[0]):
            self.gram[k] = jnp.zeros((2, HEAD, HEAD), BF)
        self.first = [
            self.copy(i, self.gram.at[pl.ds(there * self.per, self.per)], self.arrived.at[i], self.send_a, self.recv_a)
            for i, (there, _) in enumerate(self.peers)
        ]
        for copy in self.first:
            copy.start()

    def iterate(self):
        gram, arrived, per, mine = self.gram, self.arrived, self.per, self.mine
        one, two = slice(0, HEAD), slice(HEAD, PAIR)
        rows = lax.broadcasted_iota(jnp.int32, (PAIR, PAIR), 0)
        columns = lax.broadcasted_iota(jnp.int32, (PAIR, PAIR), 1)
        unit = jnp.where(rows == columns, 1.0, 0.0)
        upper = (rows < HEAD) & (rows == columns)
        lower = (rows >= HEAD) & (rows == columns)

        def product(a, b):
            a_high, b_high = a.astype(BF), b.astype(BF)
            a_low, b_low = (a - a_high.astype(F32)).astype(BF), (b - b_high.astype(F32)).astype(BF)
            made = jnp.dot(a_high, b_low, preferred_element_type=F32) + jnp.dot(a_low, b_high, preferred_element_type=F32)
            return made + jnp.dot(a_high, b_high, preferred_element_type=F32)

        for copy in self.first:
            copy.wait_recv()
        grams, wholes = [], []
        for j in range(per):
            halves = []
            for n in range(2):
                half = gram[mine * per + j, n].astype(F32)
                for i in range(len(self.peers)):
                    half = half + arrived[i, j, n].astype(F32)
                halves.append(half)
            empty = jnp.zeros((HEAD, HEAD), F32)
            total = jnp.concatenate(
                [jnp.concatenate([halves[0], empty], axis=1), jnp.concatenate([empty, halves[1]], axis=1)], axis=0
            )

            def scaling_of(chosen):
                trace = jnp.sum(jnp.sum(jnp.where(chosen, total, 0.0), axis=1, keepdims=True), axis=0, keepdims=True)
                return 1.0 / (jnp.sqrt(trace) + 1e-07)

            scaling = jnp.where(rows < HEAD, scaling_of(upper), scaling_of(lower))
            grams.append(total * (scaling * scaling))
            wholes.append(scaling)
        for number in range(NS_ITERS):
            squares = [product(a, a) for a in grams]
            steps = [COEF_A * unit + COEF_B * a + COEF_C * s for a, s in zip(grams, squares)]
            wholes = [product(w, p) for w, p in zip(wholes, steps)] if number else [w * p for w, p in zip(wholes, steps)]
            if number < NS_ITERS - 1:
                grams = [product(product(a, p), p) for a, p in zip(grams, steps)]
        for j in range(per):
            self.power[mine * per + j, 0] = wholes[j][one, one].astype(BF)
            self.power[mine * per + j, 1] = wholes[j][two, two].astype(BF)
        own = self.power.at[pl.ds(mine * per, per)]
        self.second = [self.copy(i, own, own, self.send_b, self.recv_b) for i in range(len(self.peers))]
        for copy in self.second:
            copy.start()

    def finish(self):
        one, two = slice(0, HEAD), slice(HEAD, PAIR)
        for copy in self.second:
            copy.wait_recv()

        def last(k, carry):
            values, at = self.block(k)
            made = [
                jnp.dot(values[:, side], self.power[k, n], preferred_element_type=F32) for n, side in enumerate((one, two))
            ]
            made = jnp.concatenate(made, axis=1).astype(BF)
            self.out[:, :, at] = made.reshape(self.out.shape[0], self.out.shape[1], PAIR)
            return carry

        lax.fori_loop(0, self.count, last, 0)

    def end(self):
        for copy in self.first + self.second:
            copy.wait_send()


def ortho_scratch(groups, columns):
    per = -(-(columns // PAIR) // groups)
    return [
        pltpu.VMEM((groups * per, 2, HEAD, HEAD), BF),
        pltpu.VMEM((groups - 1, per, 2, HEAD, HEAD), BF),
        pltpu.VMEM((groups * per, 2, HEAD, HEAD), BF),
    ] + [pltpu.SemaphoreType.DMA((groups - 1,))] * 4


class Terms:
    def __init__(self, hi, sh, terms, got_a, summed, got_b, send_a, recv_a, send_b, recv_b):
        self.hi, self.sh, self.terms, self.got_a, self.summed, self.got_b = hi, sh, terms, got_a, summed, got_b
        self.sems = send_a, recv_a, send_b, recv_b
        self.rows = terms.shape[1] // (8 * hi * sh)
        self.wide = summed.shape[2]

    def columns(self, h, t):
        start = (h * 8 + t) * self.sh * self.rows // 128 * 128
        return pl.ds(pl.multiple_of(start, 128), self.wide)

    def start(self):
        me = lax.axis_index("tp")
        self.first = []
        for i in range(1, 8):
            peer = rem(me + i, 8)
            for h in range(self.hi):
                n = (i - 1) * self.hi + h
                self.first.append(
                    remote(
                        self.terms.at[:, self.columns(h, peer)], self.got_a.at[i - 1, h],
                        self.sems[0].at[n], self.sems[1].at[n], peer,
                    )
                )
        for copy in self.first:
            copy.start()

    def middle(self):
        me = lax.axis_index("tp")
        for copy in self.first:
            copy.wait_recv()
        for h in range(self.hi):
            value = self.terms[:, self.columns(h, me)]
            for i in range(7):
                value = value + self.got_a[i, h]
            self.summed[h] = value
        self.second = []
        for j, (there, peer) in enumerate(row_peers(self.hi, self.sh)):
            self.second.append(
                pltpu.make_async_remote_copy(
                    src_ref=self.part(there), dst_ref=self.got_b.at[j], send_sem=self.sems[2].at[j],
                    recv_sem=self.sems[3].at[j], device_id=peer, device_id_type=MESH,
                )
            )
        for copy in self.second:
            copy.start()

    def part(self, there):
        at = pl.multiple_of(div(rem(there, self.sh) * self.rows, 128) * 128, 128)
        return self.summed.at[div(there, self.sh), :, pl.ds(at, 128)]

    def end(self, out):
        mine = lax.axis_index("hi") * self.sh + lax.axis_index("shard")
        for copy in self.second:
            copy.wait_recv()
        value = self.part(mine)[...]
        for j in range(len(self.second)):
            value = value + self.got_b[j]
        out[...] = value
        for copy in self.first + self.second:
            copy.wait_send()


def terms_scratch(hi, sh, d):
    groups = hi * sh
    wide = max(128, d // 8 // hi)
    return [
        pltpu.VMEM((16, d), F32),
        pltpu.VMEM((7, hi, 16, wide), F32),
        pltpu.VMEM((hi, 16, wide), F32),
        pltpu.VMEM((groups - 1, 16, 128), F32),
    ] + [pltpu.SemaphoreType.DMA((7 * hi,))] * 2 + [pltpu.SemaphoreType.DMA((groups - 1,))] * 2


def ortho_kernel(hi, sh, mom, grad, early, sums_one, grad_back, ortho_back, vector_grad, ortho, *scratch):
    meet_all(group_peers() + [peer for _, peer in row_peers(hi, sh)])
    work = Orthogonal(hi, sh, mom, grad, ortho, scratch[:7])
    grads = Swapping(grad, grad_back, *scratch[7:10])
    orthos = Swapping(ortho, ortho_back, *scratch[10:13])
    terms = Terms(hi, sh, *scratch[13:])
    work.grams()
    terms.terms[...] = early[...]
    for n in range(2):
        terms.terms[n : n + 1, :] = jnp.sum(sums_one[n], axis=0, keepdims=True)
    terms.start()
    grads.start()
    work.iterate()
    terms.middle()
    work.finish()
    orthos.start()
    terms.end(vector_grad)
    grads.end()
    work.end()
    orthos.end()


def update_kernel(
    weights, momentum, back_attn, ortho_attn, back_up, back_down, ortho_up, ortho_down, weight_grad, new_weights, new_momentum
):
    rows, each, _ = weights.shape
    flat = [ref.reshape(rows * each, HEAD) for ref in (weights, momentum, weight_grad, new_weights, new_momentum)]
    step = 0.15 * 0.2 * math.sqrt(2048)
    i = pl.program_id(0)

    def blocks(back, ortho):
        inside = back.shape[2] // HEAD
        for b in range(each):
            to = pl.ds(b, rows, each)
            at = slice(b % inside * HEAD, (b % inside + 1) * HEAD)
            grad = back[b // inside, :, at].astype(F32)
            flat[2][to, :] = grad
            flat[4][to, :] = 0.95 * flat[1][to, :] + grad
            flat[3][to, :] = flat[0][to, :] * (1.0 - 0.15 * 0.1) - step * ortho[b // inside, :, at].astype(F32)

    @pl.when(i < 4)
    def _():
        blocks(back_attn, ortho_attn)

    @pl.when((i >= 4) & (i < 8))
    def _():
        blocks(back_up, ortho_up)

    @pl.when(i >= 8)
    def _():
        blocks(back_down, ortho_down)


def update(weights, momentum, back_attn, ortho_attn, back_up, back_down, ortho_mlp):
    rows, blocks, head = weights.shape
    tp = back_attn.shape[0]
    width = back_attn.shape[2] // 4
    units = back_up.shape[2]
    some = HEADS * head // units
    whole = (weights, ((rows, HEADS, head), lambda i: (0, i, 0)))
    attn = ((tp, rows, width), lambda i: (0, 0, jnp.minimum(i, 3)))
    ups = ((some, rows, units), lambda i: (jnp.clip(i - 4, 0, 3), 0, 0))
    downs = ((some, rows, units), lambda i: (jnp.maximum(i - 8, 0), 0, 0))
    ortho_downs = ((some, rows, units), lambda i: (jnp.maximum(i - 8, 0), 0, 1))
    return call(
        update_kernel,
        [whole, (momentum, whole[1]), (back_attn, attn), (ortho_attn, attn)]
        + [(back_up, ups), (back_down, downs), (ortho_mlp, ups), (ortho_mlp, ortho_downs)],
        [whole] * 3,
        [],
        None,
        15,
        "update",
        grid=(blocks // HEADS,),
    )


def local(tokens, doc_lengths, weights, momentum, vectors, vector_moment, vector_second, cotangent):
    hi, tp, sh = (lax.axis_size(a) for a in ALL)
    groups, world = hi * sh, hi * tp * sh
    rows, blocks, head = weights.shape
    row_tokens, d = tokens.shape
    heads = HEADS // tp
    inner_all = (blocks - 4 * HEADS) // 2
    inner = inner_all // tp
    attn_blocks = 4 * heads
    me = lax.axis_index("tp")
    t_all = tp * row_tokens

    def arrange(array):
        attn = array[:, : 4 * HEADS].astype(BF).reshape(rows, 4, tp, heads, head).transpose(2, 0, 1, 3, 4).reshape(tp, rows, attn_blocks * head)
        mlp = array[:, 4 * HEADS :].astype(BF).reshape(rows, 2, tp, inner, head).transpose(2, 0, 1, 3, 4).reshape(tp, rows, 2 * inner * head)
        return attn, mlp

    def swap(array):
        return lax.all_to_all(array, "tp", split_axis=0, concat_axis=0, tiled=True)

    attn_send, mlp_send = arrange(weights)

    def spread(array):
        return lax.all_gather(array, FS, axis=0, tiled=False)

    w_attn = spread(swap(attn_send))
    mlp_swapped, tokens = lax.optimization_barrier((swap(mlp_send), tokens))
    w_mlp = spread(mlp_swapped)

    flat = (lax.axis_index("hi") * tp + me) * sh + lax.axis_index("shard")
    lanes = 128 // rows
    spot = lax.broadcasted_iota(jnp.int32, (1, 128), 1) // rows == flat % lanes
    piece = jnp.where(spot, jnp.tile(vectors.T, (1, lanes)), 0.0)
    count = vectors.shape[1]
    spans = jnp.pad(doc_lengths.astype(F32), ((0, 15 - count), (0, 128 - doc_lengths.shape[1])))
    piece = jnp.concatenate([piece, spans], axis=0).astype(BF)

    gathered = jax.ShapeDtypeStruct((tp, row_tokens, d), BF)
    own_f32 = jax.ShapeDtypeStruct((row_tokens, d), F32)
    own_bf = jax.ShapeDtypeStruct((row_tokens, d), BF)
    own_scratch = [pltpu.VMEM(own_f32.shape, F32), pltpu.VMEM(own_f32.shape, BF)]
    small = [pltpu.SemaphoreType.DMA((groups,))] * 2 + [pltpu.SemaphoreType.DMA((8,))] * 2
    normed_one, vec_rows, lengths = call(
        partial(first_kernel, hi, sh),
        [(tokens, False), (piece, False)],
        [
            (gathered, True),
            (jax.ShapeDtypeStruct((16, d), F32), False),
            (jax.ShapeDtypeStruct((8, 128), F32), False),
        ],
        [own_scratch[1], pltpu.VMEM((groups, 8, 16, 128), BF)] + small + gather_scratch(),
        1,
        50,
        "first_norm",
    )

    hc = heads * head
    units = inner * head
    normed_one, momentum_now = lax.optimization_barrier((normed_one, momentum))
    send_attn, send_mlp = arrange(momentum_now)
    middle, normed_two, cot_all, qkv, attended, mom_attn = call(
        partial(attention_kernel, hi, sh),
        [(normed_one, False), (w_attn, True), (lengths, False), (vec_rows, False), (tokens, False), (cotangent, True)]
        + [(send_attn, True)],
        [
            (own_f32, False),
            (gathered, True),
            (gathered, True),
            (jax.ShapeDtypeStruct((tp, row_tokens, 3 * hc), BF), False),
            (jax.ShapeDtypeStruct((t_all, hc), BF), False),
            (send_attn, True),
        ],
        own_scratch
        + [pltpu.VMEM((d, 4 * hc), BF), pltpu.SemaphoreType.DMA]
        + sum_scratch(row_tokens, d)
        + gather_scratch() * 2
        + swap_scratch(),
        2,
        120,
        "attention",
    )

    def rows_of(width):
        return (row_tokens, width), lambda r: (r, 0)

    def row_of(width):
        return (1, row_tokens, width), lambda r: (r, 0, 0)

    def fixed(array):
        return array.shape, lambda r: (0,) * array.ndim

    activated, grad_before, mom_mlp = call(
        partial(mlp_kernel, hi, sh),
        [(normed_two, row_of(d)), (cot_all, row_of(d)), (w_mlp, True), (vec_rows, fixed(vec_rows)), (send_mlp, True)],
        [(jax.ShapeDtypeStruct((t_all, units), BF), rows_of(units))] * 2 + [(send_mlp, True)],
        [pltpu.VMEM((d, units), BF)] * 2 + [pltpu.SemaphoreType.DMA((2,))] + swap_scratch(),
        7,
        30,
        "hidden_units",
        grid=(tp,),
    )

    def sent(stacked):
        return lax.psum_scatter(stacked, FS, scatter_dimension=0, tiled=False)

    s_down = outer([(cot_all, activated)], hi, sh, "grad_down")
    grad_before, s_down = lax.optimization_barrier((grad_before, s_down))
    s_up = outer([(normed_two, grad_before)], hi, sh, "grad_up")
    grad_before, s_down, s_up = lax.optimization_barrier((grad_before, s_down, s_up))
    g_down, g_up = sent(s_down), sent(s_up)

    grad_middle, sums_two, grad_branch, output = call(
        partial(branch_kernel, hi, sh),
        [(grad_before, False), (activated, False), (w_mlp, True), (middle, False), (cotangent, False), (vec_rows, False)],
        [(own_f32, False), (jax.ShapeDtypeStruct((4, 8, d), F32), False), (gathered, True), (own_bf, False)],
        own_scratch
        + [pltpu.VMEM((d, units), BF)] * 2
        + [pltpu.SemaphoreType.DMA((2,))]
        + sum_scratch(row_tokens, d)
        + gather_scratch()
        + sum_scratch(row_tokens, d),
        3,
        115,
        "second_norm_backward",
    )
    grad_branch, g_down = lax.optimization_barrier((grad_branch, g_down))
    g_down = g_down.reshape(tp, rows, -1)
    grad_joined, back_down = call(
        partial(attention_back_kernel, hi, sh),
        [(grad_branch, row_of(d)), (w_attn, True), (qkv, row_of(3 * hc)), (lengths, fixed(lengths)), (g_down, True)],
        [(jax.ShapeDtypeStruct((t_all, 3 * hc), BF), rows_of(3 * hc)), (g_down, True)],
        [pltpu.VMEM((d, hc), BF), pltpu.SemaphoreType.DMA] + swap_scratch(),
        8,
        25,
        "attention_backward",
        grid=(tp,),
    )
    s_attn = outer([(normed_one, grad_joined), (grad_branch, attended)], hi, sh, "grad_attention")
    grad_joined, s_attn = lax.optimization_barrier((grad_joined, s_attn))
    g_attn = sent(s_attn).reshape(send_attn.shape)
    g_up = g_up.reshape(tp, rows, -1)
    grad_tokens, sums_one, back_up, ortho_mlp = call(
        partial(last_kernel, hi, sh),
        [(grad_joined, False), (w_attn, True), (tokens, False), (grad_middle, False), (vec_rows, False)]
        + [(mom_mlp, False), (g_up, True), (g_down, True)],
        [(own_f32, False), (jax.ShapeDtypeStruct((2, 8, d), F32), False), (g_up, True), (send_mlp, True)],
        own_scratch[:1]
        + [pltpu.VMEM((d, 3 * hc), BF), pltpu.SemaphoreType.DMA]
        + [pltpu.VMEM(send_mlp.shape, BF), pltpu.SemaphoreType.DMA((2,)), pltpu.VMEM(send_mlp.shape, BF)]
        + sum_scratch(row_tokens, d)
        + ortho_scratch(groups, send_mlp.shape[2])
        + swap_scratch() * 2,
        4,
        85,
        "first_norm_backward",
    )
    grad_tokens, g_attn = lax.optimization_barrier((grad_tokens, g_attn))

    sums_two = jnp.sum(sums_two, axis=1)
    early = jnp.zeros((16, d), F32)
    for row, value in ((2, sums_two[:2]), (6, sums_two[2:])):
        early = lax.dynamic_update_slice(early, value, (row, 0))
    biases = jnp.sum(grad_joined, axis=0, dtype=F32)[None]
    early = lax.dynamic_update_slice(early, biases[:, :hc], (4, me * hc))
    early = lax.dynamic_update_slice(early, biases[:, 2 * hc :], (5, me * hc))
    each = d // units
    hidden = jnp.sum(grad_before, axis=0, dtype=F32)[None]
    early = lax.dynamic_update_slice(early, hidden, (8 + me // each, me % each * units))
    early, sums_one = lax.optimization_barrier((early, sums_one))

    back_attn, ortho_attn, vector_sums = call(
        partial(ortho_kernel, hi, sh),
        [(mom_attn, False), (g_attn, False), (early, False), (sums_one, False)],
        [(send_attn, True), (send_attn, True), (jax.ShapeDtypeStruct((16, 128), F32), False)],
        [pltpu.VMEM(send_attn.shape, BF)]
        + ortho_scratch(groups, send_attn.shape[2])
        + swap_scratch() * 2
        + terms_scratch(hi, sh, d),
        6,
        40,
        "orthogonalize_attention",
    )
    weight_grad, new_weights, moment_new = update(weights, momentum, back_attn, ortho_attn, back_up, back_down, ortho_mlp)

    spot = (flat % lanes) * rows
    vector_grad = lax.dynamic_slice(vector_sums, (0, spot), (16, rows))[:count].T
    first_moment = 0.9 * vector_moment + 0.1 * vector_grad
    second = 0.95 * vector_second + 0.05 * vector_grad * vector_grad
    corrected = first_moment / (1.0 - 0.9**STEP)
    normal_second = second / (1.0 - 0.95**STEP)
    next_vectors = vectors - 0.5 * corrected / (jnp.sqrt(normal_second) + 1e-08)
    return (
        output,
        grad_tokens,
        weight_grad,
        new_weights,
        moment_new,
        first_moment,
        second,
        next_vectors,
    )


def solution(mesh):
    dp, sh = mesh.shape["dp"], mesh.shape["shard"]
    tp = math.gcd(dp, 8)
    fine = Mesh(mesh.devices.reshape(dp // tp, tp, sh), ALL)
    two, three = P(ALL, None), P(ALL, None, None)
    return jax.shard_map(
        local,
        mesh=fine,
        in_specs=(two, two, three, three, two, two, two, two),
        out_specs=(two, two, three, three, three, two, two, two),
        check_vma=False,
    )
```

```python
from functools import partial
import math

import jax
import jax.numpy as jnp
from jax import lax
from jax.experimental import pallas as pl
from jax.experimental.pallas import tpu as pltpu
from jax.sharding import Mesh, PartitionSpec as P

HEADS = 16
HEAD = 128
PAIR = 2 * HEAD
NS_ITERS = 5
STEP = 10

COEF_A = 3.4445
COEF_B = -4.775
COEF_C = 2.0315
BF = jnp.bfloat16
F32 = jnp.float32
ALL = ("hi", "tp", "shard")
FS = ("hi", "shard")


MESH = pl.DeviceIdType.MESH
WIDE = 256


def rem(a, b):
    return lax.rem(a, jnp.int32(b))


def div(a, b):
    return lax.div(a, jnp.int32(b))


def spots():
    me = lax.axis_index("tp")
    c, x, y = rem(me, 2), rem(div(me, 2), 2), div(me, 4)
    return me, c, x, y, me + 1 - 2 * c, me + 2 - 4 * x, me + 4 - 8 * y


def meet(peers):
    barrier = pltpu.get_barrier_semaphore()
    for peer in peers:
        pl.semaphore_signal(barrier, inc=1, device_id={"tp": peer}, device_id_type=MESH)
    pl.semaphore_wait(barrier, len(peers))


def remote(src, dst, send, recv, peer):
    return pltpu.make_async_remote_copy(
        src_ref=src, dst_ref=dst, send_sem=send, recv_sem=recv, device_id={"tp": peer}, device_id_type=MESH
    )


def sum_scratch(rows, width):
    count = width // WIDE
    return [
        pltpu.VMEM((count, 2, 2, 2, rows, WIDE), BF),
        pltpu.VMEM((count, 2, 2, rows, WIDE), BF),
        pltpu.VMEM((count, 2, rows, WIDE), BF),
        pltpu.VMEM((count, rows, WIDE), BF),
        pltpu.SemaphoreType.DMA((3, count)),
        pltpu.SemaphoreType.DMA((3, count)),
    ]


class Summing:
    def __init__(self, left, right, total, scratch):
        self.left, self.right, self.total = left, right, total
        self.part, self.from_c, self.from_1, self.from_2, self.send, self.recv = scratch
        self.count = self.part.shape[0]
        self.rows = self.part.shape[4]

    def fill(self, k):
        right = self.right[k * WIDE : (k + 1) * WIDE, :]

        def one(dest, carry):
            rows = self.left[pl.ds(pl.multiple_of(dest * self.rows, self.rows), self.rows), :]
            made = lax.dot_general(rows, right, (((1,), (1,)), ((), ())), preferred_element_type=F32)
            self.part[k, div(dest, 4), rem(div(dest, 2), 2), rem(dest, 2)] = made.astype(BF)
            return carry

        lax.fori_loop(0, 8, one, 0)

    def copy(self, stage, k, at):
        me, c, x, y, pc, px, py = at
        even = k % 2 == 0
        if stage == 0:
            src, dst, peer = self.part.at[k, :, :, 1 - c], self.from_c.at[k], pc
        elif stage == 1:
            src = self.part.at[k, :, 1 - x, c] if even else self.part.at[k, 1 - y, :, c]
            dst, peer = self.from_1.at[k], px if even else py
        else:
            src = self.part.at[k, 1 - y, x, c] if even else self.part.at[k, y, 1 - x, c]
            dst, peer = self.from_2.at[k], py if even else px
        return remote(src, dst, self.send.at[stage, k], self.recv.at[stage, k], peer)

    def run(self):
        self.first()
        self.second()
        self.third()

    def first(self):
        at = spots()
        c = at[1]
        part = self.part

        def core_stage(k):
            self.copy(0, k, at).wait_recv()
            for i in range(4):
                a, b = i // 2, i % 2
                part[k, a, b, c] = (part[k, a, b, c].astype(F32) + self.from_c[k, a, b].astype(F32)).astype(BF)
            self.copy(1, k, at).start()

        for k in range(self.count):
            self.fill(k)
            self.copy(0, k, at).start()
            if k:
                core_stage(k - 1)
        core_stage(self.count - 1)

    def second(self):
        at = spots()
        _, c, x, y = at[:4]
        part = self.part
        for k in range(self.count):
            self.copy(1, k, at).wait_recv()
            for i in range(2):
                if k % 2 == 0:
                    part[k, i, x, c] = (part[k, i, x, c].astype(F32) + self.from_1[k, i].astype(F32)).astype(BF)
                else:
                    part[k, y, i, c] = (part[k, y, i, c].astype(F32) + self.from_1[k, i].astype(F32)).astype(BF)
            self.copy(2, k, at).start()

    def third(self):
        at = spots()
        _, c, x, y = at[:4]
        for k in range(self.count):
            self.copy(2, k, at).wait_recv()
            self.total[:, k * WIDE : (k + 1) * WIDE] = self.part[k, y, x, c].astype(F32) + self.from_2[k].astype(F32)

    def end(self):
        at = spots()
        for stage in range(3):
            for k in range(self.count):
                self.copy(stage, k, at).wait_send()


class Gathering:
    def __init__(self, own, out, send, recv, local):
        self.own, self.out, self.send, self.recv, self.local = own, out, send, recv, local
        self.copies = []

    def begin(self, src, dst, peer):
        n = len(self.copies)
        copy = remote(src, dst, self.send.at[n], self.recv.at[n], peer)
        copy.start()
        self.copies.append(copy)
        return copy

    def start(self):
        me, c, x, y, pc, px, py = spots()
        self.spots = me, px, py, pc
        own, out = self.own, self.out
        half = own.shape[-1] // 2
        self.low, self.high = pl.ds(0, half), pl.ds(half, half)
        low, high = self.low, self.high
        self.px_high = self.begin(own.at[:, high], out.at[me, :, high], px)
        self.py_low = self.begin(own.at[:, low], out.at[me, :, low], py)
        self.begin(own, out.at[me], pc)
        self.px_low = self.begin(own.at[:, low], out.at[me, :, low], px)
        self.py_high = self.begin(own.at[:, high], out.at[me, :, high], py)
        self.kept = pltpu.make_async_copy(own, out.at[me], self.local)
        self.kept.start()

    def forward(self):
        me, px, py, pc = self.spots
        out, low, high = self.out, self.low, self.high
        across = px + py - me
        self.px_high.wait_recv()
        a = self.begin(out.at[px, :, high], out.at[px, :, high], py)
        self.begin(out.at[px, :, high], out.at[px, :, high], pc)
        self.py_low.wait_recv()
        b = self.begin(out.at[py, :, low], out.at[py, :, low], px)
        self.begin(out.at[py, :, low], out.at[py, :, low], pc)
        self.px_low.wait_recv()
        self.begin(out.at[px, :, low], out.at[px, :, low], pc)
        self.py_high.wait_recv()
        self.begin(out.at[py, :, high], out.at[py, :, high], pc)
        a.wait_recv()
        self.begin(out.at[across, :, high], out.at[across, :, high], pc)
        b.wait_recv()
        self.begin(out.at[across, :, low], out.at[across, :, low], pc)
        self.seen = (0, 1, 3, 4, 5, 7)

    def end(self):
        for n, copy in enumerate(self.copies):
            if n not in self.seen:
                copy.wait_recv()
            copy.wait_send()
        self.kept.wait()


def gather_scratch():
    return [pltpu.SemaphoreType.DMA((13,)), pltpu.SemaphoreType.DMA((13,)), pltpu.SemaphoreType.DMA]


def row_loop(rows, body):
    def one(i, carry):
        body(pl.ds(pl.multiple_of(i * 16, 16), 16))
        return carry

    lax.fori_loop(0, rows // 16, one, 0)


def normalized(values):
    average = jnp.mean(values, axis=-1, keepdims=True)
    centered = values - average
    variance = jnp.mean(centered * centered, axis=-1, keepdims=True)
    scale = lax.rsqrt(variance + 1e-05)
    return centered * scale, scale


def norm_back(values, grad, gain):
    unit, scale = normalized(values)
    weighted = grad * gain
    mean_one = jnp.mean(weighted, axis=-1, keepdims=True)
    mean_two = jnp.mean(weighted * unit, axis=-1, keepdims=True)
    return scale * (weighted - mean_one - unit * mean_two), grad * unit


def fetch_rows(w, first, held, sem, hi, sh):
    rows, width = w.shape[2], held.shape[1]

    def one(f, carry):
        s, t, h = rem(f, sh), rem(div(f, sh), 8), div(f, 8 * sh)
        pltpu.make_async_copy(
            w.at[h * sh + s, t, :, pl.ds(first, width)], held.at[pl.ds(pl.multiple_of(f * rows, rows), rows)], sem
        ).start()
        return carry

    lax.fori_loop(0, 8 * hi * sh, one, 0)


def fetched(held, sem):
    pltpu.make_async_copy(held, held, sem).wait()


def first_kernel(hi, sh, tok, piece, normed_all, vec, lengths, own, pieces, send_p, recv_p, send_q, recv_q, *sems):
    me, c, x, y, pc, px, py = spots()
    groups = hi * sh
    mine = lax.axis_index("hi") * sh + lax.axis_index("shard")
    barrier = pltpu.get_barrier_semaphore()
    across, around = [], []
    for i in range(1, groups):
        there = rem(mine + i, groups)
        across.append({"hi": div(there, sh), "shard": rem(there, sh)})
    for i in range(1, 8):
        around.append({"tp": rem(me + i, 8)})
    for peer in across + around:
        pl.semaphore_signal(barrier, inc=1, device_id=peer, device_id_type=MESH)
    pl.semaphore_wait(barrier, groups + 6)

    pieces[mine, me] = piece[...]
    spot = pieces.at[mine, me]
    first = [
        pltpu.make_async_remote_copy(
            src_ref=spot, dst_ref=spot, send_sem=send_p.at[i], recv_sem=recv_p.at[i], device_id=peer, device_id_type=MESH
        )
        for i, peer in enumerate(across)
    ]
    for copy in first:
        copy.start()
    for copy in first:
        copy.wait_recv()
    column = pieces.at[:, me]
    second = [
        pltpu.make_async_remote_copy(
            src_ref=column, dst_ref=column, send_sem=send_q.at[i], recv_sem=recv_q.at[i], device_id=peer, device_id_type=MESH
        )
        for i, peer in enumerate(around)
    ]
    for copy in second:
        copy.start()
    for copy in second:
        copy.wait_recv()
    width = tok.shape[1]
    parts = 8 * groups * 128 // width
    for q in range(width // 128):
        found = None
        for f in range(q * parts, (q + 1) * parts):
            value = pieces[f // (8 * sh) * sh + f % sh, f // sh % 8].astype(F32)
            found = value if found is None else found + value
        vec[:, q * 128 : (q + 1) * 128] = found
    for t in range(8):
        lengths[t : t + 1, :] = pieces[mine, t].astype(F32)[12:13, :]

    def body(at):
        unit, _ = normalized(tok[at, :].astype(F32))
        own[at, :] = (unit * vec[0:1, :] + vec[1:2, :]).astype(BF)

    row_loop(own.shape[0], body)
    spread = Gathering(own, normed_all, *sems)
    spread.start()
    spread.forward()
    spread.end()
    for copy in first + second:
        copy.wait_send()


def allowed_of(lengths, row, size):
    line = lengths[pl.ds(row, 1), :]
    ends = [line[:, 0:1]]
    for n in range(1, 3):
        ends.append(ends[-1] + line[:, n : n + 1])
    down = lax.broadcasted_iota(jnp.int32, (size, 1), 0)
    along = lax.broadcasted_iota(jnp.int32, (1, size), 1)

    def span(places):
        places = places.astype(F32)
        return sum(jnp.where(places >= end, 1.0, 0.0) for end in ends)

    span_down, span_along = span(down), span(along)
    tail = jnp.where(span_down == 3.0, down, 0)
    return (span_down == span_along) & (along <= down) & (along >= tail)


def probabilities(query, key, allowed):
    scores = lax.dot_general(query, key, (((1,), (1,)), ((), ())), preferred_element_type=F32) * HEAD ** (-0.5)
    scores = jnp.where(allowed, scores, -1e30)
    exponent = jnp.exp(scores - jnp.max(scores, axis=-1, keepdims=True))
    return exponent / jnp.sum(exponent, axis=-1, keepdims=True)


def attention_kernel(
    hi, sh, normed, w_any, lengths, vec, tok, cot, mom, middle, normed_all, cot_all, qkv, att, mom_out, total, own, w,
    w_sem, *scratch
):
    me, c, x, y, pc, px, py = spots()
    fetch_rows(w_any, 0, w, w_sem, hi, sh)
    meet_all(group_peers())
    spread_cot = Gathering(cot, cot_all, *scratch[9:12])
    spread_cot.start()
    swapped = Swapping(mom, mom_out, *scratch[12:])
    size = own.shape[0]
    hc = att.shape[1]
    fetched(w, w_sem)

    def one_row(r, carry):
        joined = jnp.dot(normed[r], w[:, : 3 * hc], preferred_element_type=F32)
        here = pl.ds(pl.multiple_of(me * hc, 128), hc)
        queries = (joined[:, :hc] + vec[4:5, here]).astype(BF)
        keys = joined[:, hc : 2 * hc].astype(BF)
        values = (joined[:, 2 * hc :] + vec[5:6, here]).astype(BF)
        qkv[r, :, :hc] = queries
        qkv[r, :, hc : 2 * hc] = keys
        qkv[r, :, 2 * hc :] = values
        allowed = allowed_of(lengths, r, size)
        rows = pl.ds(pl.multiple_of(r * size, size), size)
        for h in range(hc // HEAD):
            at = slice(h * HEAD, (h + 1) * HEAD)
            low = probabilities(queries[:, at], keys[:, at], allowed).astype(BF)
            att[rows, at] = jnp.dot(low, values[:, at], preferred_element_type=F32).astype(BF)
        return carry

    lax.fori_loop(0, 8, one_row, 0)
    sums = Summing(att, w.at[:, 3 * hc :], total, scratch[:6])
    sums.first()
    spread_cot.forward()
    swapped.start()
    sums.second()
    sums.third()

    def body(at):
        values = tok[at, :].astype(F32) + total[at, :] + vec[6:7, :]
        middle[at, :] = values
        unit, _ = normalized(values)
        own[at, :] = (unit * vec[2:3, :] + vec[3:4, :]).astype(BF)

    row_loop(own.shape[0], body)
    spread = Gathering(own, normed_all, *scratch[6:9])
    spread.start()
    spread.forward()
    sums.end()
    spread_cot.end()
    spread.end()
    swapped.end()


GELU_A = math.sqrt(2.0 / math.pi)


def mlp_kernel(hi, sh, normed, cot, w_any, vec, mom, activated, grad_before, mom_out, w_up, w_down, sems, *scratch):
    width = w_up.shape[1]
    swapped = Swapping(mom, mom_out, *scratch)

    @pl.when(pl.program_id(0) == 0)
    def _():
        fetch_rows(w_any, 0, w_up, sems.at[0], hi, sh)
        fetch_rows(w_any, width, w_down, sems.at[1], hi, sh)
        meet_all(group_peers())
        swapped.start()
        fetched(w_up, sems.at[0])
        fetched(w_down, sems.at[1])

    me = lax.axis_index("tp")
    each = vec.shape[1] // width
    for j in range(width // 256):
        at = slice(j * 256, (j + 1) * 256)
        bias = vec[pl.ds(8 + div(me, each), 1), pl.ds(pl.multiple_of(rem(me, each) * width + j * 256, 256), 256)]
        before = jnp.dot(normed[0], w_up[:, at], preferred_element_type=F32) + bias
        grad = jnp.dot(cot[0], w_down[:, at], preferred_element_type=F32)
        square = before * before
        slope = jnp.tanh(before * (GELU_A + GELU_A * 0.044715 * square))
        half = 0.5 * (1.0 + slope)
        activated[:, at] = (before * half).astype(BF)
        inner = GELU_A + 3.0 * GELU_A * 0.044715 * square
        grad_before[:, at] = (grad * (half + 0.5 * before * (1.0 - slope * slope) * inner)).astype(BF)

    @pl.when(pl.program_id(0) == pl.num_programs(0) - 1)
    def _():
        swapped.end()


def attention_back_kernel(
    hi, sh, branch, w_any, qkv, lengths, grad_down, grad_joined, back_down, w, sem, *scratch
):
    swapped = Swapping(grad_down, back_down, *scratch)
    hc = w.shape[1]
    size = branch.shape[1]
    r = pl.program_id(0)

    @pl.when(r == 0)
    def _():
        fetch_rows(w_any, 3 * hc, w, sem, hi, sh)
        meet_all(group_peers())
        swapped.start()
        fetched(w, sem)

    grad_att = jnp.dot(branch[0], w[...], preferred_element_type=F32).astype(BF)
    allowed = allowed_of(lengths, r, size)
    scale = HEAD ** (-0.5)
    for h in range(hc // HEAD):
        at = slice(h * HEAD, (h + 1) * HEAD)
        query, key, value = (qkv[0, :, n * hc + h * HEAD : n * hc + (h + 1) * HEAD] for n in range(3))
        probability = probabilities(query, key, allowed)
        low = probability.astype(BF)
        grad = grad_att[:, at]
        grad_prob = lax.dot_general(grad, value, (((1,), (1,)), ((), ())), preferred_element_type=F32)
        row_total = jnp.sum(probability * grad_prob, axis=-1, keepdims=True)
        grad_scores = (probability * (grad_prob - row_total)).astype(BF)
        made = (
            jnp.dot(grad_scores, key, preferred_element_type=F32) * scale,
            lax.dot_general(grad_scores, query, (((0,), (0,)), ((), ())), preferred_element_type=F32) * scale,
            lax.dot_general(low, grad, (((0,), (0,)), ((), ())), preferred_element_type=F32),
        )
        for n in range(3):
            grad_joined[:, n * hc + h * HEAD : n * hc + (h + 1) * HEAD] = made[n].astype(BF)

    @pl.when(r == pl.num_programs(0) - 1)
    def _():
        swapped.end()


def branch_kernel(
    hi, sh, grad_before, activated, w_any, middle, cot, vec, grad_middle, sums_out, branch_all, output, total, own,
    w_up, w_down, w_sem, *scratch
):
    me, c, x, y, pc, px, py = spots()
    fetch_rows(w_any, 0, w_up, w_sem.at[0], hi, sh)
    fetch_rows(w_any, w_up.shape[1], w_down, w_sem.at[1], hi, sh)
    meet((pc, px, py))
    fetched(w_up, w_sem.at[0])
    sums = Summing(grad_before, w_up, total, scratch[:6])
    more = Summing(activated, w_down, total, scratch[9:])
    sums.run()
    sums_out[...] = jnp.zeros_like(sums_out)

    def body(at):
        grad = total[at, :]
        part, for_gain = norm_back(middle[at, :], grad, vec[2:3, :])
        back = cot[at, :].astype(F32)
        whole = back + part
        grad_middle[at, :] = whole
        low = whole.astype(BF)
        own[at, :] = low
        low = low.astype(F32)
        for n, values in enumerate((for_gain, grad, low, back)):
            sums_out[n] += values[:8] + values[8:]

    row_loop(own.shape[0], body)
    spread = Gathering(own, branch_all, *scratch[6:9])
    spread.start()
    fetched(w_down, w_sem.at[1])
    more.first()
    spread.forward()
    more.second()
    more.third()

    def body_two(at):
        output[at, :] = (middle[at, :] + total[at, :] + vec[7:8, :]).astype(BF)

    row_loop(own.shape[0], body_two)
    sums.end()
    more.end()
    spread.end()


def last_kernel(
    hi, sh, grad_joined, w_attn, tok, grad_middle, vec, mom, grad_up, grad_down, grad_tokens, sums_out, back_up, ortho_back,
    total, w_qkv, w_sem, grad, grad_sems, ortho, *scratch
):
    fetch_rows(w_attn, 0, w_qkv, w_sem, hi, sh)
    width = grad_up.shape[2]
    loads = [
        pltpu.make_async_copy(part, grad.at[:, :, pl.ds(n * width, width)], grad_sems.at[n])
        for n, part in enumerate((grad_up, grad_down))
    ]
    for load in loads:
        load.start()
    meet_all(group_peers() + [peer for _, peer in row_peers(hi, sh)])
    work = Orthogonal(hi, sh, mom, grad, ortho, scratch[6:13])
    ups = Swapping(grad_up, back_up, *scratch[13:16])
    orthos = Swapping(ortho, ortho_back, *scratch[16:19])
    sums = Summing(grad_joined, w_qkv, total, scratch[:6])
    fetched(w_qkv, w_sem)
    for load in loads:
        load.wait()
    work.grams()
    sums.first()
    ups.start()
    work.iterate()
    sums.second()
    work.finish()
    orthos.start()
    sums.third()
    sums_out[...] = jnp.zeros_like(sums_out)

    def body(at):
        there = total[at, :]
        part, for_gain = norm_back(tok[at, :].astype(F32), there, vec[0:1, :])
        grad_tokens[at, :] = grad_middle[at, :] + part
        for n, values in enumerate((for_gain, there)):
            sums_out[n] += values[:8] + values[8:]

    row_loop(total.shape[0], body)
    sums.end()
    ups.end()
    work.end()
    orthos.end()


def outer_kernel(*refs):
    *pairs, out = refs
    _, sh, some, rows, _ = out.shape
    first = 0
    for left, right in zip(pairs[::2], pairs[1::2]):
        made = lax.dot_general(
            left[...].reshape(-1, left.shape[-1]), right[...], (((0,), (0,)), ((), ())), preferred_element_type=F32
        ).astype(BF)
        n = right.shape[1]
        for a in range(some):
            for s in range(sh):
                at = (a * sh + s) * rows
                out[0, s, a, :, first : first + n] = made[at : at + rows]
        first += n


def outer(pairs, hi, sh, name):
    tp, tokens, d = pairs[0][0].shape
    n = sum(right.shape[1] for _, right in pairs)
    rows = d // (hi * tp * sh)
    some = 256 // (sh * rows)
    turns = tp // some
    ins = []
    for left, right in pairs:
        ins += [(left, ((tp, tokens, 256), lambda i: (0, 0, i))), (right, (right.shape, lambda i: (0, 0)))]
    (made,) = call(
        outer_kernel,
        ins,
        [
            (
                jax.ShapeDtypeStruct((hi, sh, tp, rows, n), BF),
                ((1, sh, some, rows, n), lambda i: (i // turns, 0, i % turns, 0, 0)),
            )
        ],
        [],
        None,
        n / 70,
        name,
        grid=(d // 256,),
    )
    return made.reshape(hi * sh, tp * rows, n)


def call(body, ins, outs, scratch, number, microseconds, name, grid=None):
    def spec(how):
        if how is True:
            return pl.BlockSpec(memory_space=pl.ANY)
        return pl.BlockSpec(memory_space=pltpu.VMEM) if how is False else pl.BlockSpec(*how)

    remote_params = {} if number is None else {"collective_id": number, "has_side_effects": True}
    return pl.pallas_call(
        body,
        out_shape=[jax.ShapeDtypeStruct(s.shape, s.dtype) for s, _ in outs],
        in_specs=[spec(how) for _, how in ins],
        out_specs=[spec(how) for _, how in outs],
        scratch_shapes=scratch,
        compiler_params=pltpu.CompilerParams(vmem_limit_bytes=60 * 2**20, **remote_params),
        cost_estimate=pl.CostEstimate(flops=0, transcendentals=0, bytes_accessed=int(microseconds * 3.0e6)),
        name=name,
        **({} if grid is None else {"grid": grid}),
    )(*[a for a, _ in ins])


class Swapping:
    def __init__(self, own, out, send, recv, local):
        me = lax.axis_index("tp")
        self.copies = []
        for i in range(1, 8):
            peer = rem(me + i, 8)
            self.copies.append(remote(own.at[peer], out.at[me], send.at[i - 1], recv.at[i - 1], peer))
        self.kept = pltpu.make_async_copy(own.at[me], out.at[me], local)

    def start(self):
        for copy in self.copies:
            copy.start()
        self.kept.start()

    def end(self):
        for copy in self.copies:
            copy.wait_recv()
        for copy in self.copies:
            copy.wait_send()
        self.kept.wait()


def swap_scratch():
    return [pltpu.SemaphoreType.DMA((7,)), pltpu.SemaphoreType.DMA((7,)), pltpu.SemaphoreType.DMA]


def group_peers():
    me = lax.axis_index("tp")
    return [{"tp": rem(me + i, 8)} for i in range(1, 8)]


def row_peers(hi, sh):
    mine = lax.axis_index("hi") * sh + lax.axis_index("shard")
    theres = [rem(mine + i, hi * sh) for i in range(1, hi * sh)]
    return [(there, {"hi": div(there, sh), "shard": rem(there, sh)}) for there in theres]


def meet_all(peers):
    barrier = pltpu.get_barrier_semaphore()
    for peer in peers:
        pl.semaphore_signal(barrier, inc=1, device_id=peer, device_id_type=MESH)
    pl.semaphore_wait(barrier, len(peers))


class Orthogonal:
    def __init__(self, hi, sh, mom, grad, out, scratch):
        self.mom, self.grad, self.out = mom, grad, out
        self.gram, self.arrived, self.power, self.send_a, self.recv_a, self.send_b, self.recv_b = scratch
        self.mine = lax.axis_index("hi") * sh + lax.axis_index("shard")
        self.peers = row_peers(hi, sh)
        self.count = out.shape[2] // PAIR
        self.per = self.gram.shape[0] // (hi * sh)

    def block(self, k):
        at = pl.ds(pl.multiple_of(k * PAIR, PAIR), PAIR)
        values = 0.95 * self.mom[:, :, at].astype(F32) + self.grad[:, :, at].astype(F32)
        return values.reshape(-1, PAIR).astype(BF), at

    def copy(self, i, src, dst, send, recv):
        return pltpu.make_async_remote_copy(
            src_ref=src, dst_ref=dst, send_sem=send.at[i], recv_sem=recv.at[i],
            device_id=self.peers[i][1], device_id_type=MESH,
        )

    def grams(self):
        one, two = slice(0, HEAD), slice(HEAD, PAIR)

        def one_gram(k, carry):
            values, _ = self.block(k)
            made = lax.dot_general(values, values, (((0,), (0,)), ((), ())), preferred_element_type=F32)
            self.gram[k, 0] = made[one, one].astype(BF)
            self.gram[k, 1] = made[two, two].astype(BF)
            return carry

        lax.fori_loop(0, self.count, one_gram, 0)
        for k in range(self.count, self.gram.shape[0]):
            self.gram[k] = jnp.zeros((2, HEAD, HEAD), BF)
        self.first = [
            self.copy(i, self.gram.at[pl.ds(there * self.per, self.per)], self.arrived.at[i], self.send_a, self.recv_a)
            for i, (there, _) in enumerate(self.peers)
        ]
        for copy in self.first:
            copy.start()

    def iterate(self):
        gram, arrived, per, mine = self.gram, self.arrived, self.per, self.mine
        one, two = slice(0, HEAD), slice(HEAD, PAIR)
        rows = lax.broadcasted_iota(jnp.int32, (PAIR, PAIR), 0)
        columns = lax.broadcasted_iota(jnp.int32, (PAIR, PAIR), 1)
        unit = jnp.where(rows == columns, 1.0, 0.0)
        upper = (rows < HEAD) & (rows == columns)
        lower = (rows >= HEAD) & (rows == columns)

        def product(a, b):
            a_high, b_high = a.astype(BF), b.astype(BF)
            a_low, b_low = (a - a_high.astype(F32)).astype(BF), (b - b_high.astype(F32)).astype(BF)
            made = jnp.dot(a_high, b_low, preferred_element_type=F32) + jnp.dot(a_low, b_high, preferred_element_type=F32)
            return made + jnp.dot(a_high, b_high, preferred_element_type=F32)

        for copy in self.first:
            copy.wait_recv()
        grams, wholes = [], []
        for j in range(per):
            halves = []
            for n in range(2):
                half = gram[mine * per + j, n].astype(F32)
                for i in range(len(self.peers)):
                    half = half + arrived[i, j, n].astype(F32)
                halves.append(half)
            empty = jnp.zeros((HEAD, HEAD), F32)
            total = jnp.concatenate(
                [jnp.concatenate([halves[0], empty], axis=1), jnp.concatenate([empty, halves[1]], axis=1)], axis=0
            )

            def scaling_of(chosen):
                trace = jnp.sum(jnp.sum(jnp.where(chosen, total, 0.0), axis=1, keepdims=True), axis=0, keepdims=True)
                return 1.0 / (jnp.sqrt(trace) + 1e-07)

            scaling = jnp.where(rows < HEAD, scaling_of(upper), scaling_of(lower))
            grams.append(total * (scaling * scaling))
            wholes.append(scaling)
        for number in range(NS_ITERS):
            squares = [product(a, a) for a in grams]
            steps = [COEF_A * unit + COEF_B * a + COEF_C * s for a, s in zip(grams, squares)]
            wholes = [product(w, p) for w, p in zip(wholes, steps)] if number else [w * p for w, p in zip(wholes, steps)]
            if number < NS_ITERS - 1:
                grams = [product(product(a, p), p) for a, p in zip(grams, steps)]
        for j in range(per):
            self.power[mine * per + j, 0] = wholes[j][one, one].astype(BF)
            self.power[mine * per + j, 1] = wholes[j][two, two].astype(BF)
        own = self.power.at[pl.ds(mine * per, per)]
        self.second = [self.copy(i, own, own, self.send_b, self.recv_b) for i in range(len(self.peers))]
        for copy in self.second:
            copy.start()

    def finish(self):
        one, two = slice(0, HEAD), slice(HEAD, PAIR)
        for copy in self.second:
            copy.wait_recv()

        def last(k, carry):
            values, at = self.block(k)
            made = [
                jnp.dot(values[:, side], self.power[k, n], preferred_element_type=F32) for n, side in enumerate((one, two))
            ]
            made = jnp.concatenate(made, axis=1).astype(BF)
            self.out[:, :, at] = made.reshape(self.out.shape[0], self.out.shape[1], PAIR)
            return carry

        lax.fori_loop(0, self.count, last, 0)

    def end(self):
        for copy in self.first + self.second:
            copy.wait_send()


def ortho_scratch(groups, columns):
    per = -(-(columns // PAIR) // groups)
    return [
        pltpu.VMEM((groups * per, 2, HEAD, HEAD), BF),
        pltpu.VMEM((groups - 1, per, 2, HEAD, HEAD), BF),
        pltpu.VMEM((groups * per, 2, HEAD, HEAD), BF),
    ] + [pltpu.SemaphoreType.DMA((groups - 1,))] * 4


class Terms:
    def __init__(self, hi, sh, terms, got_a, summed, got_b, send_a, recv_a, send_b, recv_b):
        self.hi, self.sh, self.terms, self.got_a, self.summed, self.got_b = hi, sh, terms, got_a, summed, got_b
        self.sems = send_a, recv_a, send_b, recv_b
        self.rows = terms.shape[1] // (8 * hi * sh)
        self.wide = summed.shape[2]

    def columns(self, h, t):
        start = (h * 8 + t) * self.sh * self.rows // 128 * 128
        return pl.ds(pl.multiple_of(start, 128), self.wide)

    def start(self):
        me = lax.axis_index("tp")
        self.first = []
        for i in range(1, 8):
            peer = rem(me + i, 8)
            for h in range(self.hi):
                n = (i - 1) * self.hi + h
                self.first.append(
                    remote(
                        self.terms.at[:, self.columns(h, peer)], self.got_a.at[i - 1, h],
                        self.sems[0].at[n], self.sems[1].at[n], peer,
                    )
                )
        for copy in self.first:
            copy.start()

    def middle(self):
        me = lax.axis_index("tp")
        for copy in self.first:
            copy.wait_recv()
        for h in range(self.hi):
            value = self.terms[:, self.columns(h, me)]
            for i in range(7):
                value = value + self.got_a[i, h]
            self.summed[h] = value
        self.second = []
        for j, (there, peer) in enumerate(row_peers(self.hi, self.sh)):
            self.second.append(
                pltpu.make_async_remote_copy(
                    src_ref=self.part(there), dst_ref=self.got_b.at[j], send_sem=self.sems[2].at[j],
                    recv_sem=self.sems[3].at[j], device_id=peer, device_id_type=MESH,
                )
            )
        for copy in self.second:
            copy.start()

    def part(self, there):
        at = pl.multiple_of(div(rem(there, self.sh) * self.rows, 128) * 128, 128)
        return self.summed.at[div(there, self.sh), :, pl.ds(at, 128)]

    def end(self, out):
        mine = lax.axis_index("hi") * self.sh + lax.axis_index("shard")
        for copy in self.second:
            copy.wait_recv()
        value = self.part(mine)[...]
        for j in range(len(self.second)):
            value = value + self.got_b[j]
        out[...] = value
        for copy in self.first + self.second:
            copy.wait_send()


def terms_scratch(hi, sh, d):
    groups = hi * sh
    wide = max(128, d // 8 // hi)
    return [
        pltpu.VMEM((16, d), F32),
        pltpu.VMEM((7, hi, 16, wide), F32),
        pltpu.VMEM((hi, 16, wide), F32),
        pltpu.VMEM((groups - 1, 16, 128), F32),
    ] + [pltpu.SemaphoreType.DMA((7 * hi,))] * 2 + [pltpu.SemaphoreType.DMA((groups - 1,))] * 2


def ortho_kernel(hi, sh, mom, grad, early, sums_one, grad_back, ortho_back, vector_grad, ortho, *scratch):
    meet_all(group_peers() + [peer for _, peer in row_peers(hi, sh)])
    work = Orthogonal(hi, sh, mom, grad, ortho, scratch[:7])
    grads = Swapping(grad, grad_back, *scratch[7:10])
    orthos = Swapping(ortho, ortho_back, *scratch[10:13])
    terms = Terms(hi, sh, *scratch[13:])
    work.grams()
    terms.terms[...] = early[...]
    for n in range(2):
        terms.terms[n : n + 1, :] = jnp.sum(sums_one[n], axis=0, keepdims=True)
    terms.start()
    grads.start()
    work.iterate()
    terms.middle()
    work.finish()
    orthos.start()
    terms.end(vector_grad)
    grads.end()
    work.end()
    orthos.end()


def update_kernel(
    weights, momentum, back_attn, ortho_attn, back_up, back_down, ortho_up, ortho_down, weight_grad, new_weights, new_momentum
):
    rows, each, _ = weights.shape
    flat = [ref.reshape(rows * each, HEAD) for ref in (weights, momentum, weight_grad, new_weights, new_momentum)]
    step = 0.15 * 0.2 * math.sqrt(2048)
    i = pl.program_id(0)

    def blocks(back, ortho):
        inside = back.shape[2] // HEAD
        for b in range(each):
            to = pl.ds(b, rows, each)
            at = slice(b % inside * HEAD, (b % inside + 1) * HEAD)
            grad = back[b // inside, :, at].astype(F32)
            flat[2][to, :] = grad
            flat[4][to, :] = 0.95 * flat[1][to, :] + grad
            flat[3][to, :] = flat[0][to, :] * (1.0 - 0.15 * 0.1) - step * ortho[b // inside, :, at].astype(F32)

    @pl.when(i < 4)
    def _():
        blocks(back_attn, ortho_attn)

    @pl.when((i >= 4) & (i < 8))
    def _():
        blocks(back_up, ortho_up)

    @pl.when(i >= 8)
    def _():
        blocks(back_down, ortho_down)


def update(weights, momentum, back_attn, ortho_attn, back_up, back_down, ortho_mlp):
    rows, blocks, head = weights.shape
    tp = back_attn.shape[0]
    width = back_attn.shape[2] // 4
    units = back_up.shape[2]
    some = HEADS * head // units
    whole = (weights, ((rows, HEADS, head), lambda i: (0, i, 0)))
    attn = ((tp, rows, width), lambda i: (0, 0, jnp.minimum(i, 3)))
    ups = ((some, rows, units), lambda i: (jnp.clip(i - 4, 0, 3), 0, 0))
    downs = ((some, rows, units), lambda i: (jnp.maximum(i - 8, 0), 0, 0))
    ortho_downs = ((some, rows, units), lambda i: (jnp.maximum(i - 8, 0), 0, 1))
    return call(
        update_kernel,
        [whole, (momentum, whole[1]), (back_attn, attn), (ortho_attn, attn)]
        + [(back_up, ups), (back_down, downs), (ortho_mlp, ups), (ortho_mlp, ortho_downs)],
        [whole] * 3,
        [],
        None,
        15,
        "update",
        grid=(blocks // HEADS,),
    )


def local(tokens, doc_lengths, weights, momentum, vectors, vector_moment, vector_second, cotangent):
    hi, tp, sh = (lax.axis_size(a) for a in ALL)
    groups, world = hi * sh, hi * tp * sh
    rows, blocks, head = weights.shape
    row_tokens, d = tokens.shape
    heads = HEADS // tp
    inner_all = (blocks - 4 * HEADS) // 2
    inner = inner_all // tp
    attn_blocks = 4 * heads
    me = lax.axis_index("tp")
    t_all = tp * row_tokens

    def arrange(array):
        attn = array[:, : 4 * HEADS].astype(BF).reshape(rows, 4, tp, heads, head).transpose(2, 0, 1, 3, 4).reshape(tp, rows, attn_blocks * head)
        mlp = array[:, 4 * HEADS :].astype(BF).reshape(rows, 2, tp, inner, head).transpose(2, 0, 1, 3, 4).reshape(tp, rows, 2 * inner * head)
        return attn, mlp

    def swap(array):
        return lax.all_to_all(array, "tp", split_axis=0, concat_axis=0, tiled=True)

    attn_send = arrange(weights)[0]
    attn_send, weights_later = lax.optimization_barrier((attn_send, weights))
    mlp_send = arrange(weights_later)[1]

    def spread(array):
        return lax.all_gather(array, FS, axis=0, tiled=False)

    w_attn = spread(swap(attn_send))
    mlp_swapped, tokens, send_attn, send_mlp = lax.optimization_barrier((swap(mlp_send), tokens, *arrange(momentum)))
    w_mlp = spread(mlp_swapped)

    flat = (lax.axis_index("hi") * tp + me) * sh + lax.axis_index("shard")
    lanes = 128 // rows
    spot = lax.broadcasted_iota(jnp.int32, (1, 128), 1) // rows == flat % lanes
    piece = jnp.where(spot, jnp.tile(vectors.T, (1, lanes)), 0.0)
    count = vectors.shape[1]
    spans = jnp.pad(doc_lengths.astype(F32), ((0, 15 - count), (0, 128 - doc_lengths.shape[1])))
    piece = jnp.concatenate([piece, spans], axis=0).astype(BF)

    gathered = jax.ShapeDtypeStruct((tp, row_tokens, d), BF)
    own_f32 = jax.ShapeDtypeStruct((row_tokens, d), F32)
    own_bf = jax.ShapeDtypeStruct((row_tokens, d), BF)
    own_scratch = [pltpu.VMEM(own_f32.shape, F32), pltpu.VMEM(own_f32.shape, BF)]
    small = [pltpu.SemaphoreType.DMA((groups,))] * 2 + [pltpu.SemaphoreType.DMA((8,))] * 2
    normed_one, vec_rows, lengths = call(
        partial(first_kernel, hi, sh),
        [(tokens, False), (piece, False)],
        [
            (gathered, True),
            (jax.ShapeDtypeStruct((16, d), F32), False),
            (jax.ShapeDtypeStruct((8, 128), F32), False),
        ],
        [own_scratch[1], pltpu.VMEM((groups, 8, 16, 128), BF)] + small + gather_scratch(),
        1,
        50,
        "first_norm",
    )

    hc = heads * head
    units = inner * head
    middle, normed_two, cot_all, qkv, attended, mom_attn = call(
        partial(attention_kernel, hi, sh),
        [(normed_one, False), (w_attn, True), (lengths, False), (vec_rows, False), (tokens, False), (cotangent, True)]
        + [(send_attn, True)],
        [
            (own_f32, False),
            (gathered, True),
            (gathered, True),
            (jax.ShapeDtypeStruct((tp, row_tokens, 3 * hc), BF), False),
            (jax.ShapeDtypeStruct((t_all, hc), BF), False),
            (send_attn, True),
        ],
        own_scratch
        + [pltpu.VMEM((d, 4 * hc), BF), pltpu.SemaphoreType.DMA]
        + sum_scratch(row_tokens, d)
        + gather_scratch() * 2
        + swap_scratch(),
        2,
        120,
        "attention",
    )

    def rows_of(width):
        return (row_tokens, width), lambda r: (r, 0)

    def row_of(width):
        return (1, row_tokens, width), lambda r: (r, 0, 0)

    def fixed(array):
        return array.shape, lambda r: (0,) * array.ndim

    activated, grad_before, mom_mlp = call(
        partial(mlp_kernel, hi, sh),
        [(normed_two, row_of(d)), (cot_all, row_of(d)), (w_mlp, True), (vec_rows, fixed(vec_rows)), (send_mlp, True)],
        [(jax.ShapeDtypeStruct((t_all, units), BF), rows_of(units))] * 2 + [(send_mlp, True)],
        [pltpu.VMEM((d, units), BF)] * 2 + [pltpu.SemaphoreType.DMA((2,))] + swap_scratch(),
        7,
        30,
        "hidden_units",
        grid=(tp,),
    )

    def sent(stacked):
        return lax.psum_scatter(stacked, FS, scatter_dimension=0, tiled=False)

    s_down = outer([(cot_all, activated)], hi, sh, "grad_down")
    grad_before, s_down = lax.optimization_barrier((grad_before, s_down))
    s_up = outer([(normed_two, grad_before)], hi, sh, "grad_up")
    grad_before, s_down, s_up = lax.optimization_barrier((grad_before, s_down, s_up))
    g_down, g_up = sent(s_down), sent(s_up)

    grad_middle, sums_two, grad_branch, output = call(
        partial(branch_kernel, hi, sh),
        [(grad_before, False), (activated, False), (w_mlp, True), (middle, False), (cotangent, False), (vec_rows, False)],
        [(own_f32, False), (jax.ShapeDtypeStruct((4, 8, d), F32), False), (gathered, True), (own_bf, False)],
        own_scratch
        + [pltpu.VMEM((d, units), BF)] * 2
        + [pltpu.SemaphoreType.DMA((2,))]
        + sum_scratch(row_tokens, d)
        + gather_scratch()
        + sum_scratch(row_tokens, d),
        3,
        115,
        "second_norm_backward",
    )
    grad_branch, g_down = lax.optimization_barrier((grad_branch, g_down))
    g_down = g_down.reshape(tp, rows, -1)
    grad_joined, back_down = call(
        partial(attention_back_kernel, hi, sh),
        [(grad_branch, row_of(d)), (w_attn, True), (qkv, row_of(3 * hc)), (lengths, fixed(lengths)), (g_down, True)],
        [(jax.ShapeDtypeStruct((t_all, 3 * hc), BF), rows_of(3 * hc)), (g_down, True)],
        [pltpu.VMEM((d, hc), BF), pltpu.SemaphoreType.DMA] + swap_scratch(),
        8,
        25,
        "attention_backward",
        grid=(tp,),
    )
    s_attn = outer([(normed_one, grad_joined), (grad_branch, attended)], hi, sh, "grad_attention")
    grad_joined, s_attn = lax.optimization_barrier((grad_joined, s_attn))
    g_attn = sent(s_attn).reshape(send_attn.shape)
    g_up = g_up.reshape(tp, rows, -1)
    grad_tokens, sums_one, back_up, ortho_mlp = call(
        partial(last_kernel, hi, sh),
        [(grad_joined, False), (w_attn, True), (tokens, False), (grad_middle, False), (vec_rows, False)]
        + [(mom_mlp, False), (g_up, True), (g_down, True)],
        [(own_f32, False), (jax.ShapeDtypeStruct((2, 8, d), F32), False), (g_up, True), (send_mlp, True)],
        own_scratch[:1]
        + [pltpu.VMEM((d, 3 * hc), BF), pltpu.SemaphoreType.DMA]
        + [pltpu.VMEM(send_mlp.shape, BF), pltpu.SemaphoreType.DMA((2,)), pltpu.VMEM(send_mlp.shape, BF)]
        + sum_scratch(row_tokens, d)
        + ortho_scratch(groups, send_mlp.shape[2])
        + swap_scratch() * 2,
        4,
        85,
        "first_norm_backward",
    )
    grad_tokens, g_attn = lax.optimization_barrier((grad_tokens, g_attn))

    sums_two = jnp.sum(sums_two, axis=1)
    early = jnp.zeros((16, d), F32)
    for row, value in ((2, sums_two[:2]), (6, sums_two[2:])):
        early = lax.dynamic_update_slice(early, value, (row, 0))
    biases = jnp.sum(grad_joined, axis=0, dtype=F32)[None]
    early = lax.dynamic_update_slice(early, biases[:, :hc], (4, me * hc))
    early = lax.dynamic_update_slice(early, biases[:, 2 * hc :], (5, me * hc))
    each = d // units
    hidden = jnp.sum(grad_before, axis=0, dtype=F32)[None]
    early = lax.dynamic_update_slice(early, hidden, (8 + me // each, me % each * units))
    early, sums_one = lax.optimization_barrier((early, sums_one))

    back_attn, ortho_attn, vector_sums = call(
        partial(ortho_kernel, hi, sh),
        [(mom_attn, False), (g_attn, False), (early, False), (sums_one, False)],
        [(send_attn, True), (send_attn, True), (jax.ShapeDtypeStruct((16, 128), F32), False)],
        [pltpu.VMEM(send_attn.shape, BF)]
        + ortho_scratch(groups, send_attn.shape[2])
        + swap_scratch() * 2
        + terms_scratch(hi, sh, d),
        6,
        40,
        "orthogonalize_attention",
    )
    weight_grad, new_weights, moment_new = update(weights, momentum, back_attn, ortho_attn, back_up, back_down, ortho_mlp)

    spot = (flat % lanes) * rows
    vector_grad = lax.dynamic_slice(vector_sums, (0, spot), (16, rows))[:count].T
    first_moment = 0.9 * vector_moment + 0.1 * vector_grad
    second = 0.95 * vector_second + 0.05 * vector_grad * vector_grad
    corrected = first_moment / (1.0 - 0.9**STEP)
    normal_second = second / (1.0 - 0.95**STEP)
    next_vectors = vectors - 0.5 * corrected / (jnp.sqrt(normal_second) + 1e-08)
    return (
        output,
        grad_tokens,
        weight_grad,
        new_weights,
        moment_new,
        first_moment,
        second,
        next_vectors,
    )


def solution(mesh):
    dp, sh = mesh.shape["dp"], mesh.shape["shard"]
    tp = math.gcd(dp, 8)
    fine = Mesh(mesh.devices.reshape(dp // tp, tp, sh), ALL)
    two, three = P(ALL, None), P(ALL, None, None)
    return jax.shard_map(
        local,
        mesh=fine,
        in_specs=(two, two, three, three, two, two, two, two),
        out_specs=(two, two, three, three, three, two, two, two),
        check_vma=False,
    )
```

```python
from functools import partial
import math

import jax
import jax.numpy as jnp
from jax import lax
from jax.experimental import pallas as pl
from jax.experimental.pallas import tpu as pltpu
from jax.sharding import Mesh, PartitionSpec as P

HEADS = 16
HEAD = 128
PAIR = 2 * HEAD
NS_ITERS = 5
STEP = 10

COEF_A = 3.4445
COEF_B = -4.775
COEF_C = 2.0315
BF = jnp.bfloat16
F32 = jnp.float32
ALL = ("hi", "tp", "shard")
FS = ("hi", "shard")


MESH = pl.DeviceIdType.MESH
WIDE = 256


def rem(a, b):
    return lax.rem(a, jnp.int32(b))


def div(a, b):
    return lax.div(a, jnp.int32(b))


def spots():
    me = lax.axis_index("tp")
    c, x, y = rem(me, 2), rem(div(me, 2), 2), div(me, 4)
    return me, c, x, y, me + 1 - 2 * c, me + 2 - 4 * x, me + 4 - 8 * y


def meet(peers):
    barrier = pltpu.get_barrier_semaphore()
    for peer in peers:
        pl.semaphore_signal(barrier, inc=1, device_id={"tp": peer}, device_id_type=MESH)
    pl.semaphore_wait(barrier, len(peers))


def remote(src, dst, send, recv, peer):
    return pltpu.make_async_remote_copy(
        src_ref=src, dst_ref=dst, send_sem=send, recv_sem=recv, device_id={"tp": peer}, device_id_type=MESH
    )


def sum_scratch(rows, width):
    count = width // WIDE
    return [
        pltpu.VMEM((count, 2, 2, 2, rows, WIDE), BF),
        pltpu.VMEM((count, 2, 2, rows, WIDE), BF),
        pltpu.VMEM((count, 2, rows, WIDE), BF),
        pltpu.VMEM((count, rows, WIDE), BF),
        pltpu.SemaphoreType.DMA((3, count)),
        pltpu.SemaphoreType.DMA((3, count)),
    ]


class Summing:
    def __init__(self, left, right, total, scratch):
        self.left, self.right, self.total = left, right, total
        self.part, self.from_c, self.from_1, self.from_2, self.send, self.recv = scratch
        self.count = self.part.shape[0]
        self.rows = self.part.shape[4]

    def fill(self, k):
        right = self.right[k * WIDE : (k + 1) * WIDE, :]

        def one(y, carry):
            rows = self.left[pl.ds(pl.multiple_of(y * 4 * self.rows, 4 * self.rows), 4 * self.rows), :]
            made = lax.dot_general(rows, right, (((1,), (1,)), ((), ())), preferred_element_type=F32)
            self.part[k, y] = made.astype(BF).reshape(2, 2, self.rows, WIDE)
            return carry

        lax.fori_loop(0, 2, one, 0)

    def copy(self, stage, k, at):
        me, c, x, y, pc, px, py = at
        even = k % 2 == 0
        if stage == 0:
            src, dst, peer = self.part.at[k, :, :, 1 - c], self.from_c.at[k], pc
        elif stage == 1:
            src = self.part.at[k, :, 1 - x, c] if even else self.part.at[k, 1 - y, :, c]
            dst, peer = self.from_1.at[k], px if even else py
        else:
            src = self.part.at[k, 1 - y, x, c] if even else self.part.at[k, y, 1 - x, c]
            dst, peer = self.from_2.at[k], py if even else px
        return remote(src, dst, self.send.at[stage, k], self.recv.at[stage, k], peer)

    def run(self):
        self.first()
        self.second()
        self.third()

    def first(self):
        at = spots()
        c = at[1]
        part = self.part

        def core_stage(k):
            self.copy(0, k, at).wait_recv()
            for i in range(4):
                a, b = i // 2, i % 2
                part[k, a, b, c] = (part[k, a, b, c].astype(F32) + self.from_c[k, a, b].astype(F32)).astype(BF)
            self.copy(1, k, at).start()

        for k in range(self.count):
            self.fill(k)
            self.copy(0, k, at).start()
            if k:
                core_stage(k - 1)
        core_stage(self.count - 1)

    def second(self):
        at = spots()
        _, c, x, y = at[:4]
        part = self.part
        for k in range(self.count):
            self.copy(1, k, at).wait_recv()
            for i in range(2):
                if k % 2 == 0:
                    part[k, i, x, c] = (part[k, i, x, c].astype(F32) + self.from_1[k, i].astype(F32)).astype(BF)
                else:
                    part[k, y, i, c] = (part[k, y, i, c].astype(F32) + self.from_1[k, i].astype(F32)).astype(BF)
            self.copy(2, k, at).start()

    def third(self):
        at = spots()
        _, c, x, y = at[:4]
        for k in range(self.count):
            self.copy(2, k, at).wait_recv()
            self.total[:, k * WIDE : (k + 1) * WIDE] = self.part[k, y, x, c].astype(F32) + self.from_2[k].astype(F32)

    def end(self):
        at = spots()
        for stage in range(3):
            for k in range(self.count):
                self.copy(stage, k, at).wait_send()


class Gathering:
    def __init__(self, own, out, send, recv, local):
        self.own, self.out, self.send, self.recv, self.local = own, out, send, recv, local
        self.copies = []

    def begin(self, src, dst, peer):
        n = len(self.copies)
        copy = remote(src, dst, self.send.at[n], self.recv.at[n], peer)
        copy.start()
        self.copies.append(copy)
        return copy

    def start(self):
        me, c, x, y, pc, px, py = spots()
        self.spots = me, px, py, pc
        own, out = self.own, self.out
        half = own.shape[-1] // 2
        self.low, self.high = pl.ds(0, half), pl.ds(half, half)
        low, high = self.low, self.high
        self.px_high = self.begin(own.at[:, high], out.at[me, :, high], px)
        self.py_low = self.begin(own.at[:, low], out.at[me, :, low], py)
        self.begin(own, out.at[me], pc)
        self.px_low = self.begin(own.at[:, low], out.at[me, :, low], px)
        self.py_high = self.begin(own.at[:, high], out.at[me, :, high], py)
        self.kept = pltpu.make_async_copy(own, out.at[me], self.local)
        self.kept.start()

    def forward(self):
        me, px, py, pc = self.spots
        out, low, high = self.out, self.low, self.high
        across = px + py - me
        self.px_high.wait_recv()
        a = self.begin(out.at[px, :, high], out.at[px, :, high], py)
        self.begin(out.at[px, :, high], out.at[px, :, high], pc)
        self.py_low.wait_recv()
        b = self.begin(out.at[py, :, low], out.at[py, :, low], px)
        self.begin(out.at[py, :, low], out.at[py, :, low], pc)
        self.px_low.wait_recv()
        self.begin(out.at[px, :, low], out.at[px, :, low], pc)
        self.py_high.wait_recv()
        self.begin(out.at[py, :, high], out.at[py, :, high], pc)
        a.wait_recv()
        self.begin(out.at[across, :, high], out.at[across, :, high], pc)
        b.wait_recv()
        self.begin(out.at[across, :, low], out.at[across, :, low], pc)
        self.seen = (0, 1, 3, 4, 5, 7)

    def end(self):
        for n, copy in enumerate(self.copies):
            if n not in self.seen:
                copy.wait_recv()
            copy.wait_send()
        self.kept.wait()


def gather_scratch():
    return [pltpu.SemaphoreType.DMA((13,)), pltpu.SemaphoreType.DMA((13,)), pltpu.SemaphoreType.DMA]


def row_loop(rows, body):
    def one(i, carry):
        body(pl.ds(pl.multiple_of(i * 16, 16), 16))
        return carry

    lax.fori_loop(0, rows // 16, one, 0)


def normalized(values):
    average = jnp.mean(values, axis=-1, keepdims=True)
    centered = values - average
    variance = jnp.mean(centered * centered, axis=-1, keepdims=True)
    scale = lax.rsqrt(variance + 1e-05)
    return centered * scale, scale


def norm_back(values, grad, gain):
    unit, scale = normalized(values)
    weighted = grad * gain
    mean_one = jnp.mean(weighted, axis=-1, keepdims=True)
    mean_two = jnp.mean(weighted * unit, axis=-1, keepdims=True)
    return scale * (weighted - mean_one - unit * mean_two), grad * unit


def fetch_rows(w, first, held, sem, hi, sh):
    rows, width = w.shape[2], held.shape[1]

    def one(f, carry):
        s, t, h = rem(f, sh), rem(div(f, sh), 8), div(f, 8 * sh)
        pltpu.make_async_copy(
            w.at[h * sh + s, t, :, pl.ds(first, width)], held.at[pl.ds(pl.multiple_of(f * rows, rows), rows)], sem
        ).start()
        return carry

    lax.fori_loop(0, 8 * hi * sh, one, 0)


def fetched(held, sem):
    pltpu.make_async_copy(held, held, sem).wait()


def first_kernel(hi, sh, tok, piece, normed_all, vec, lengths, own, pieces, send_p, recv_p, send_q, recv_q, *sems):
    me, c, x, y, pc, px, py = spots()
    groups = hi * sh
    mine = lax.axis_index("hi") * sh + lax.axis_index("shard")
    barrier = pltpu.get_barrier_semaphore()
    across, around = [], []
    for i in range(1, groups):
        there = rem(mine + i, groups)
        across.append({"hi": div(there, sh), "shard": rem(there, sh)})
    for i in range(1, 8):
        around.append({"tp": rem(me + i, 8)})
    for peer in across + around:
        pl.semaphore_signal(barrier, inc=1, device_id=peer, device_id_type=MESH)
    pl.semaphore_wait(barrier, groups + 6)

    pieces[mine, me] = piece[...]
    spot = pieces.at[mine, me]
    first = [
        pltpu.make_async_remote_copy(
            src_ref=spot, dst_ref=spot, send_sem=send_p.at[i], recv_sem=recv_p.at[i], device_id=peer, device_id_type=MESH
        )
        for i, peer in enumerate(across)
    ]
    for copy in first:
        copy.start()
    for copy in first:
        copy.wait_recv()
    column = pieces.at[:, me]
    second = [
        pltpu.make_async_remote_copy(
            src_ref=column, dst_ref=column, send_sem=send_q.at[i], recv_sem=recv_q.at[i], device_id=peer, device_id_type=MESH
        )
        for i, peer in enumerate(around)
    ]
    for copy in second:
        copy.start()
    for copy in second:
        copy.wait_recv()
    width = tok.shape[1]
    parts = 8 * groups * 128 // width
    for q in range(width // 128):
        found = None
        for f in range(q * parts, (q + 1) * parts):
            value = pieces[f // (8 * sh) * sh + f % sh, f // sh % 8].astype(F32)
            found = value if found is None else found + value
        vec[:, q * 128 : (q + 1) * 128] = found
    for t in range(8):
        lengths[t : t + 1, :] = pieces[mine, t].astype(F32)[12:13, :]

    def body(at):
        unit, _ = normalized(tok[at, :].astype(F32))
        own[at, :] = (unit * vec[0:1, :] + vec[1:2, :]).astype(BF)

    row_loop(own.shape[0], body)
    spread = Gathering(own, normed_all, *sems)
    spread.start()
    spread.forward()
    spread.end()
    for copy in first + second:
        copy.wait_send()


def allowed_of(lengths, row, size):
    line = lengths[pl.ds(row, 1), :]
    ends = [line[:, 0:1]]
    for n in range(1, 3):
        ends.append(ends[-1] + line[:, n : n + 1])
    down = lax.broadcasted_iota(jnp.int32, (size, 1), 0)
    along = lax.broadcasted_iota(jnp.int32, (1, size), 1)

    def span(places):
        places = places.astype(F32)
        return sum(jnp.where(places >= end, 1.0, 0.0) for end in ends)

    span_down, span_along = span(down), span(along)
    tail = jnp.where(span_down == 3.0, down, 0)
    return (span_down == span_along) & (along <= down) & (along >= tail)


def probabilities(query, key, allowed):
    scores = lax.dot_general(query, key, (((1,), (1,)), ((), ())), preferred_element_type=F32) * HEAD ** (-0.5)
    scores = jnp.where(allowed, scores, -1e30)
    exponent = jnp.exp(scores - jnp.max(scores, axis=-1, keepdims=True))
    return exponent / jnp.sum(exponent, axis=-1, keepdims=True)


def attention_kernel(
    hi, sh, normed, w_any, lengths, vec, tok, cot, mom, middle, normed_all, cot_all, qkv, att, mom_out, total, own, w,
    w_sem, *scratch
):
    me, c, x, y, pc, px, py = spots()
    fetch_rows(w_any, 0, w, w_sem, hi, sh)
    meet_all(group_peers())
    spread_cot = Gathering(cot, cot_all, *scratch[9:12])
    spread_cot.start()
    swapped = Swapping(mom, mom_out, *scratch[12:])
    size = own.shape[0]
    hc = att.shape[1]
    fetched(w, w_sem)

    def one_row(r, carry):
        joined = jnp.dot(normed[r], w[:, : 3 * hc], preferred_element_type=F32)
        here = pl.ds(pl.multiple_of(me * hc, 128), hc)
        queries = (joined[:, :hc] + vec[4:5, here]).astype(BF)
        keys = joined[:, hc : 2 * hc].astype(BF)
        values = (joined[:, 2 * hc :] + vec[5:6, here]).astype(BF)
        qkv[r, :, :hc] = queries
        qkv[r, :, hc : 2 * hc] = keys
        qkv[r, :, 2 * hc :] = values
        allowed = allowed_of(lengths, r, size)
        rows = pl.ds(pl.multiple_of(r * size, size), size)
        for h in range(hc // HEAD):
            at = slice(h * HEAD, (h + 1) * HEAD)
            low = probabilities(queries[:, at], keys[:, at], allowed).astype(BF)
            att[rows, at] = jnp.dot(low, values[:, at], preferred_element_type=F32).astype(BF)
        return carry

    lax.fori_loop(0, 8, one_row, 0)
    sums = Summing(att, w.at[:, 3 * hc :], total, scratch[:6])
    sums.first()
    spread_cot.forward()
    swapped.start()
    sums.second()
    sums.third()

    def body(at):
        values = tok[at, :].astype(F32) + total[at, :] + vec[6:7, :]
        middle[at, :] = values
        unit, _ = normalized(values)
        own[at, :] = (unit * vec[2:3, :] + vec[3:4, :]).astype(BF)

    row_loop(own.shape[0], body)
    spread = Gathering(own, normed_all, *scratch[6:9])
    spread.start()
    spread.forward()
    sums.end()
    spread_cot.end()
    spread.end()
    swapped.end()


GELU_A = math.sqrt(2.0 / math.pi)


def mlp_kernel(hi, sh, normed, cot, w_any, vec, mom, activated, grad_before, mom_out, w_up, w_down, sems, *scratch):
    width = w_up.shape[1]
    swapped = Swapping(mom, mom_out, *scratch)

    @pl.when(pl.program_id(0) == 0)
    def _():
        fetch_rows(w_any, 0, w_up, sems.at[0], hi, sh)
        fetch_rows(w_any, width, w_down, sems.at[1], hi, sh)
        meet_all(group_peers())
        swapped.start()
        fetched(w_up, sems.at[0])
        fetched(w_down, sems.at[1])

    me = lax.axis_index("tp")
    each = vec.shape[1] // width
    for j in range(width // 256):
        at = slice(j * 256, (j + 1) * 256)
        bias = vec[pl.ds(8 + div(me, each), 1), pl.ds(pl.multiple_of(rem(me, each) * width + j * 256, 256), 256)]
        before = jnp.dot(normed[0], w_up[:, at], preferred_element_type=F32) + bias
        grad = jnp.dot(cot[0], w_down[:, at], preferred_element_type=F32)
        square = before * before
        slope = jnp.tanh(before * (GELU_A + GELU_A * 0.044715 * square))
        half = 0.5 * (1.0 + slope)
        activated[:, at] = (before * half).astype(BF)
        inner = GELU_A + 3.0 * GELU_A * 0.044715 * square
        grad_before[:, at] = (grad * (half + 0.5 * before * (1.0 - slope * slope) * inner)).astype(BF)

    @pl.when(pl.program_id(0) == pl.num_programs(0) - 1)
    def _():
        swapped.end()


def attention_back_kernel(
    hi, sh, branch, w_any, qkv, lengths, grad_down, grad_joined, back_down, w, sem, *scratch
):
    swapped = Swapping(grad_down, back_down, *scratch)
    hc = w.shape[1]
    size = branch.shape[1]
    r = pl.program_id(0)

    @pl.when(r == 0)
    def _():
        fetch_rows(w_any, 3 * hc, w, sem, hi, sh)
        meet_all(group_peers())
        swapped.start()
        fetched(w, sem)

    grad_att = jnp.dot(branch[0], w[...], preferred_element_type=F32).astype(BF)
    allowed = allowed_of(lengths, r, size)
    scale = HEAD ** (-0.5)
    for h in range(hc // HEAD):
        at = slice(h * HEAD, (h + 1) * HEAD)
        query, key, value = (qkv[0, :, n * hc + h * HEAD : n * hc + (h + 1) * HEAD] for n in range(3))
        probability = probabilities(query, key, allowed)
        low = probability.astype(BF)
        grad = grad_att[:, at]
        grad_prob = lax.dot_general(grad, value, (((1,), (1,)), ((), ())), preferred_element_type=F32)
        row_total = jnp.sum(probability * grad_prob, axis=-1, keepdims=True)
        grad_scores = (probability * (grad_prob - row_total)).astype(BF)
        made = (
            jnp.dot(grad_scores, key, preferred_element_type=F32) * scale,
            lax.dot_general(grad_scores, query, (((0,), (0,)), ((), ())), preferred_element_type=F32) * scale,
            lax.dot_general(low, grad, (((0,), (0,)), ((), ())), preferred_element_type=F32),
        )
        for n in range(3):
            grad_joined[:, n * hc + h * HEAD : n * hc + (h + 1) * HEAD] = made[n].astype(BF)

    @pl.when(r == pl.num_programs(0) - 1)
    def _():
        swapped.end()


def branch_kernel(
    hi, sh, grad_before, activated, w_any, middle, cot, vec, grad_middle, sums_out, branch_all, output, total, own,
    w_up, w_down, w_sem, *scratch
):
    me, c, x, y, pc, px, py = spots()
    fetch_rows(w_any, 0, w_up, w_sem.at[0], hi, sh)
    fetch_rows(w_any, w_up.shape[1], w_down, w_sem.at[1], hi, sh)
    meet((pc, px, py))
    fetched(w_up, w_sem.at[0])
    sums = Summing(grad_before, w_up, total, scratch[:6])
    more = Summing(activated, w_down, total, scratch[9:])
    sums.run()
    sums_out[...] = jnp.zeros_like(sums_out)

    def body(at):
        grad = total[at, :]
        part, for_gain = norm_back(middle[at, :], grad, vec[2:3, :])
        back = cot[at, :].astype(F32)
        whole = back + part
        grad_middle[at, :] = whole
        low = whole.astype(BF)
        own[at, :] = low
        low = low.astype(F32)
        for n, values in enumerate((for_gain, grad, low, back)):
            sums_out[n] += values[:8] + values[8:]

    row_loop(own.shape[0], body)
    spread = Gathering(own, branch_all, *scratch[6:9])
    spread.start()
    fetched(w_down, w_sem.at[1])
    more.first()
    spread.forward()
    more.second()
    more.third()

    def body_two(at):
        output[at, :] = (middle[at, :] + total[at, :] + vec[7:8, :]).astype(BF)

    row_loop(own.shape[0], body_two)
    sums.end()
    more.end()
    spread.end()


def last_kernel(
    hi, sh, grad_joined, w_attn, tok, grad_middle, vec, mom, grad_up, grad_down, grad_tokens, sums_out, back_up, ortho_back,
    total, w_qkv, w_sem, grad, grad_sems, ortho, *scratch
):
    fetch_rows(w_attn, 0, w_qkv, w_sem, hi, sh)
    width = grad_up.shape[2]
    loads = [
        pltpu.make_async_copy(part, grad.at[:, :, pl.ds(n * width, width)], grad_sems.at[n])
        for n, part in enumerate((grad_up, grad_down))
    ]
    for load in loads:
        load.start()
    meet_all(group_peers() + [peer for _, peer in row_peers(hi, sh)])
    work = Orthogonal(hi, sh, mom, grad, ortho, scratch[6:13])
    ups = Swapping(grad_up, back_up, *scratch[13:16])
    orthos = Swapping(ortho, ortho_back, *scratch[16:19])
    sums = Summing(grad_joined, w_qkv, total, scratch[:6])
    fetched(w_qkv, w_sem)
    for load in loads:
        load.wait()
    work.grams()
    sums.first()
    ups.start()
    work.iterate()
    sums.second()
    work.finish()
    orthos.start()
    sums.third()
    sums_out[...] = jnp.zeros_like(sums_out)

    def body(at):
        there = total[at, :]
        part, for_gain = norm_back(tok[at, :].astype(F32), there, vec[0:1, :])
        grad_tokens[at, :] = grad_middle[at, :] + part
        for n, values in enumerate((for_gain, there)):
            sums_out[n] += values[:8] + values[8:]

    row_loop(total.shape[0], body)
    sums.end()
    ups.end()
    work.end()
    orthos.end()


def outer_kernel(*refs):
    *pairs, out = refs
    _, sh, some, rows, _ = out.shape
    first = 0
    for left, right in zip(pairs[::2], pairs[1::2]):
        made = lax.dot_general(
            left[...].reshape(-1, left.shape[-1]), right[...], (((0,), (0,)), ((), ())), preferred_element_type=F32
        ).astype(BF)
        n = right.shape[1]
        for a in range(some):
            for s in range(sh):
                at = (a * sh + s) * rows
                out[0, s, a, :, first : first + n] = made[at : at + rows]
        first += n


def outer(pairs, hi, sh, name):
    tp, tokens, d = pairs[0][0].shape
    n = sum(right.shape[1] for _, right in pairs)
    rows = d // (hi * tp * sh)
    some = 256 // (sh * rows)
    turns = tp // some
    ins = []
    for left, right in pairs:
        ins += [(left, ((tp, tokens, 256), lambda i: (0, 0, i))), (right, (right.shape, lambda i: (0, 0)))]
    (made,) = call(
        outer_kernel,
        ins,
        [
            (
                jax.ShapeDtypeStruct((hi, sh, tp, rows, n), BF),
                ((1, sh, some, rows, n), lambda i: (i // turns, 0, i % turns, 0, 0)),
            )
        ],
        [],
        None,
        n / 70,
        name,
        grid=(d // 256,),
    )
    return made.reshape(hi * sh, tp * rows, n)


def call(body, ins, outs, scratch, number, microseconds, name, grid=None):
    def spec(how):
        if how is True:
            return pl.BlockSpec(memory_space=pl.ANY)
        return pl.BlockSpec(memory_space=pltpu.VMEM) if how is False else pl.BlockSpec(*how)

    remote_params = {} if number is None else {"collective_id": number, "has_side_effects": True}
    return pl.pallas_call(
        body,
        out_shape=[jax.ShapeDtypeStruct(s.shape, s.dtype) for s, _ in outs],
        in_specs=[spec(how) for _, how in ins],
        out_specs=[spec(how) for _, how in outs],
        scratch_shapes=scratch,
        compiler_params=pltpu.CompilerParams(vmem_limit_bytes=60 * 2**20, **remote_params),
        cost_estimate=pl.CostEstimate(flops=0, transcendentals=0, bytes_accessed=int(microseconds * 3.0e6)),
        name=name,
        **({} if grid is None else {"grid": grid}),
    )(*[a for a, _ in ins])


class Swapping:
    def __init__(self, own, out, send, recv, local):
        me = lax.axis_index("tp")
        self.copies = []
        for i in range(1, 8):
            peer = rem(me + i, 8)
            self.copies.append(remote(own.at[peer], out.at[me], send.at[i - 1], recv.at[i - 1], peer))
        self.kept = pltpu.make_async_copy(own.at[me], out.at[me], local)

    def start(self):
        for copy in self.copies:
            copy.start()
        self.kept.start()

    def end(self):
        for copy in self.copies:
            copy.wait_recv()
        for copy in self.copies:
            copy.wait_send()
        self.kept.wait()


def swap_scratch():
    return [pltpu.SemaphoreType.DMA((7,)), pltpu.SemaphoreType.DMA((7,)), pltpu.SemaphoreType.DMA]


def group_peers():
    me = lax.axis_index("tp")
    return [{"tp": rem(me + i, 8)} for i in range(1, 8)]


def row_peers(hi, sh):
    mine = lax.axis_index("hi") * sh + lax.axis_index("shard")
    theres = [rem(mine + i, hi * sh) for i in range(1, hi * sh)]
    return [(there, {"hi": div(there, sh), "shard": rem(there, sh)}) for there in theres]


def meet_all(peers):
    barrier = pltpu.get_barrier_semaphore()
    for peer in peers:
        pl.semaphore_signal(barrier, inc=1, device_id=peer, device_id_type=MESH)
    pl.semaphore_wait(barrier, len(peers))


class Orthogonal:
    def __init__(self, hi, sh, mom, grad, out, scratch):
        self.mom, self.grad, self.out = mom, grad, out
        self.gram, self.arrived, self.power, self.send_a, self.recv_a, self.send_b, self.recv_b = scratch
        self.mine = lax.axis_index("hi") * sh + lax.axis_index("shard")
        self.peers = row_peers(hi, sh)
        self.count = out.shape[2] // PAIR
        self.per = self.gram.shape[0] // (hi * sh)

    def block(self, k):
        at = pl.ds(pl.multiple_of(k * PAIR, PAIR), PAIR)
        values = 0.95 * self.mom[:, :, at].astype(F32) + self.grad[:, :, at].astype(F32)
        return values.reshape(-1, PAIR).astype(BF), at

    def copy(self, i, src, dst, send, recv):
        return pltpu.make_async_remote_copy(
            src_ref=src, dst_ref=dst, send_sem=send.at[i], recv_sem=recv.at[i],
            device_id=self.peers[i][1], device_id_type=MESH,
        )

    def grams(self):
        one, two = slice(0, HEAD), slice(HEAD, PAIR)

        def one_gram(k, carry):
            values, _ = self.block(k)
            made = lax.dot_general(values, values, (((0,), (0,)), ((), ())), preferred_element_type=F32)
            self.gram[k, 0] = made[one, one].astype(BF)
            self.gram[k, 1] = made[two, two].astype(BF)
            return carry

        lax.fori_loop(0, self.count, one_gram, 0)
        for k in range(self.count, self.gram.shape[0]):
            self.gram[k] = jnp.zeros((2, HEAD, HEAD), BF)
        self.first = [
            self.copy(i, self.gram.at[pl.ds(there * self.per, self.per)], self.arrived.at[i], self.send_a, self.recv_a)
            for i, (there, _) in enumerate(self.peers)
        ]
        for copy in self.first:
            copy.start()

    def iterate(self):
        gram, arrived, per, mine = self.gram, self.arrived, self.per, self.mine
        one, two = slice(0, HEAD), slice(HEAD, PAIR)
        rows = lax.broadcasted_iota(jnp.int32, (PAIR, PAIR), 0)
        columns = lax.broadcasted_iota(jnp.int32, (PAIR, PAIR), 1)
        unit = jnp.where(rows == columns, 1.0, 0.0)
        upper = (rows < HEAD) & (rows == columns)
        lower = (rows >= HEAD) & (rows == columns)

        def product(a, b):
            a_high, b_high = a.astype(BF), b.astype(BF)
            a_low, b_low = (a - a_high.astype(F32)).astype(BF), (b - b_high.astype(F32)).astype(BF)
            made = jnp.dot(a_high, b_low, preferred_element_type=F32) + jnp.dot(a_low, b_high, preferred_element_type=F32)
            return made + jnp.dot(a_high, b_high, preferred_element_type=F32)

        for copy in self.first:
            copy.wait_recv()
        grams, wholes = [], []
        for j in range(per):
            halves = []
            for n in range(2):
                half = gram[mine * per + j, n].astype(F32)
                for i in range(len(self.peers)):
                    half = half + arrived[i, j, n].astype(F32)
                halves.append(half)
            empty = jnp.zeros((HEAD, HEAD), F32)
            total = jnp.concatenate(
                [jnp.concatenate([halves[0], empty], axis=1), jnp.concatenate([empty, halves[1]], axis=1)], axis=0
            )

            def scaling_of(chosen):
                trace = jnp.sum(jnp.sum(jnp.where(chosen, total, 0.0), axis=1, keepdims=True), axis=0, keepdims=True)
                return 1.0 / (jnp.sqrt(trace) + 1e-07)

            scaling = jnp.where(rows < HEAD, scaling_of(upper), scaling_of(lower))
            grams.append(total * (scaling * scaling))
            wholes.append(scaling)
        for number in range(NS_ITERS):
            squares = [product(a, a) for a in grams]
            steps = [COEF_A * unit + COEF_B * a + COEF_C * s for a, s in zip(grams, squares)]
            wholes = [product(w, p) for w, p in zip(wholes, steps)] if number else [w * p for w, p in zip(wholes, steps)]
            if number < NS_ITERS - 1:
                grams = [product(product(a, p), p) for a, p in zip(grams, steps)]
        for j in range(per):
            self.power[mine * per + j, 0] = wholes[j][one, one].astype(BF)
            self.power[mine * per + j, 1] = wholes[j][two, two].astype(BF)
        own = self.power.at[pl.ds(mine * per, per)]
        self.second = [self.copy(i, own, own, self.send_b, self.recv_b) for i in range(len(self.peers))]
        for copy in self.second:
            copy.start()

    def finish(self):
        one, two = slice(0, HEAD), slice(HEAD, PAIR)
        for copy in self.second:
            copy.wait_recv()

        def last(k, carry):
            values, at = self.block(k)
            made = [
                jnp.dot(values[:, side], self.power[k, n], preferred_element_type=F32) for n, side in enumerate((one, two))
            ]
            made = jnp.concatenate(made, axis=1).astype(BF)
            self.out[:, :, at] = made.reshape(self.out.shape[0], self.out.shape[1], PAIR)
            return carry

        lax.fori_loop(0, self.count, last, 0)

    def end(self):
        for copy in self.first + self.second:
            copy.wait_send()


def ortho_scratch(groups, columns):
    per = -(-(columns // PAIR) // groups)
    return [
        pltpu.VMEM((groups * per, 2, HEAD, HEAD), BF),
        pltpu.VMEM((groups - 1, per, 2, HEAD, HEAD), BF),
        pltpu.VMEM((groups * per, 2, HEAD, HEAD), BF),
    ] + [pltpu.SemaphoreType.DMA((groups - 1,))] * 4


class Terms:
    def __init__(self, hi, sh, terms, got_a, summed, got_b, send_a, recv_a, send_b, recv_b):
        self.hi, self.sh, self.terms, self.got_a, self.summed, self.got_b = hi, sh, terms, got_a, summed, got_b
        self.sems = send_a, recv_a, send_b, recv_b
        self.rows = terms.shape[1] // (8 * hi * sh)
        self.wide = summed.shape[2]

    def columns(self, h, t):
        start = (h * 8 + t) * self.sh * self.rows // 128 * 128
        return pl.ds(pl.multiple_of(start, 128), self.wide)

    def start(self):
        me = lax.axis_index("tp")
        self.first = []
        for i in range(1, 8):
            peer = rem(me + i, 8)
            for h in range(self.hi):
                n = (i - 1) * self.hi + h
                self.first.append(
                    remote(
                        self.terms.at[:, self.columns(h, peer)], self.got_a.at[i - 1, h],
                        self.sems[0].at[n], self.sems[1].at[n], peer,
                    )
                )
        for copy in self.first:
            copy.start()

    def middle(self):
        me = lax.axis_index("tp")
        for copy in self.first:
            copy.wait_recv()
        for h in range(self.hi):
            value = self.terms[:, self.columns(h, me)]
            for i in range(7):
                value = value + self.got_a[i, h]
            self.summed[h] = value
        self.second = []
        for j, (there, peer) in enumerate(row_peers(self.hi, self.sh)):
            self.second.append(
                pltpu.make_async_remote_copy(
                    src_ref=self.part(there), dst_ref=self.got_b.at[j], send_sem=self.sems[2].at[j],
                    recv_sem=self.sems[3].at[j], device_id=peer, device_id_type=MESH,
                )
            )
        for copy in self.second:
            copy.start()

    def part(self, there):
        at = pl.multiple_of(div(rem(there, self.sh) * self.rows, 128) * 128, 128)
        return self.summed.at[div(there, self.sh), :, pl.ds(at, 128)]

    def end(self, out):
        mine = lax.axis_index("hi") * self.sh + lax.axis_index("shard")
        for copy in self.second:
            copy.wait_recv()
        value = self.part(mine)[...]
        for j in range(len(self.second)):
            value = value + self.got_b[j]
        out[...] = value
        for copy in self.first + self.second:
            copy.wait_send()


def terms_scratch(hi, sh, d):
    groups = hi * sh
    wide = max(128, d // 8 // hi)
    return [
        pltpu.VMEM((16, d), F32),
        pltpu.VMEM((7, hi, 16, wide), F32),
        pltpu.VMEM((hi, 16, wide), F32),
        pltpu.VMEM((groups - 1, 16, 128), F32),
    ] + [pltpu.SemaphoreType.DMA((7 * hi,))] * 2 + [pltpu.SemaphoreType.DMA((groups - 1,))] * 2


def ortho_kernel(hi, sh, mom, grad, early, sums_one, grad_back, ortho_back, vector_grad, ortho, *scratch):
    meet_all(group_peers() + [peer for _, peer in row_peers(hi, sh)])
    work = Orthogonal(hi, sh, mom, grad, ortho, scratch[:7])
    grads = Swapping(grad, grad_back, *scratch[7:10])
    orthos = Swapping(ortho, ortho_back, *scratch[10:13])
    terms = Terms(hi, sh, *scratch[13:])
    work.grams()
    terms.terms[...] = early[...]
    for n in range(2):
        terms.terms[n : n + 1, :] = jnp.sum(sums_one[n], axis=0, keepdims=True)
    terms.start()
    grads.start()
    work.iterate()
    terms.middle()
    work.finish()
    orthos.start()
    terms.end(vector_grad)
    grads.end()
    work.end()
    orthos.end()


def update_kernel(
    weights, momentum, back_attn, ortho_attn, back_up, back_down, ortho_up, ortho_down, weight_grad, new_weights, new_momentum
):
    rows, each, _ = weights.shape
    flat = [ref.reshape(rows * each, HEAD) for ref in (weights, momentum, weight_grad, new_weights, new_momentum)]
    step = 0.15 * 0.2 * math.sqrt(2048)
    i = pl.program_id(0)

    def blocks(back, ortho):
        inside = back.shape[2] // HEAD
        for b in range(each):
            to = pl.ds(b, rows, each)
            at = slice(b % inside * HEAD, (b % inside + 1) * HEAD)
            grad = back[b // inside, :, at].astype(F32)
            flat[2][to, :] = grad
            flat[4][to, :] = 0.95 * flat[1][to, :] + grad
            flat[3][to, :] = flat[0][to, :] * (1.0 - 0.15 * 0.1) - step * ortho[b // inside, :, at].astype(F32)

    @pl.when(i < 4)
    def _():
        blocks(back_attn, ortho_attn)

    @pl.when((i >= 4) & (i < 8))
    def _():
        blocks(back_up, ortho_up)

    @pl.when(i >= 8)
    def _():
        blocks(back_down, ortho_down)


def update(weights, momentum, back_attn, ortho_attn, back_up, back_down, ortho_mlp):
    rows, blocks, head = weights.shape
    tp = back_attn.shape[0]
    width = back_attn.shape[2] // 4
    units = back_up.shape[2]
    some = HEADS * head // units
    whole = (weights, ((rows, HEADS, head), lambda i: (0, i, 0)))
    attn = ((tp, rows, width), lambda i: (0, 0, jnp.minimum(i, 3)))
    ups = ((some, rows, units), lambda i: (jnp.clip(i - 4, 0, 3), 0, 0))
    downs = ((some, rows, units), lambda i: (jnp.maximum(i - 8, 0), 0, 0))
    ortho_downs = ((some, rows, units), lambda i: (jnp.maximum(i - 8, 0), 0, 1))
    return call(
        update_kernel,
        [whole, (momentum, whole[1]), (back_attn, attn), (ortho_attn, attn)]
        + [(back_up, ups), (back_down, downs), (ortho_mlp, ups), (ortho_mlp, ortho_downs)],
        [whole] * 3,
        [],
        None,
        15,
        "update",
        grid=(blocks // HEADS,),
    )


def local(tokens, doc_lengths, weights, momentum, vectors, vector_moment, vector_second, cotangent):
    hi, tp, sh = (lax.axis_size(a) for a in ALL)
    groups, world = hi * sh, hi * tp * sh
    rows, blocks, head = weights.shape
    row_tokens, d = tokens.shape
    heads = HEADS // tp
    inner_all = (blocks - 4 * HEADS) // 2
    inner = inner_all // tp
    attn_blocks = 4 * heads
    me = lax.axis_index("tp")
    t_all = tp * row_tokens

    def arrange(array):
        attn = array[:, : 4 * HEADS].astype(BF).reshape(rows, 4, tp, heads, head).transpose(2, 0, 1, 3, 4).reshape(tp, rows, attn_blocks * head)
        mlp = array[:, 4 * HEADS :].astype(BF).reshape(rows, 2, tp, inner, head).transpose(2, 0, 1, 3, 4).reshape(tp, rows, 2 * inner * head)
        return attn, mlp

    def swap(array):
        return lax.all_to_all(array, "tp", split_axis=0, concat_axis=0, tiled=True)

    attn_send = arrange(weights)[0]
    attn_send, weights_later = lax.optimization_barrier((attn_send, weights))
    mlp_send = arrange(weights_later)[1]

    def spread(array):
        return lax.all_gather(array, FS, axis=0, tiled=False)

    w_attn = spread(swap(attn_send))
    mlp_swapped, tokens, send_attn, send_mlp = lax.optimization_barrier((swap(mlp_send), tokens, *arrange(momentum)))
    w_mlp = spread(mlp_swapped)

    flat = (lax.axis_index("hi") * tp + me) * sh + lax.axis_index("shard")
    lanes = 128 // rows
    spot = lax.broadcasted_iota(jnp.int32, (1, 128), 1) // rows == flat % lanes
    piece = jnp.where(spot, jnp.tile(vectors.T, (1, lanes)), 0.0)
    count = vectors.shape[1]
    spans = jnp.pad(doc_lengths.astype(F32), ((0, 15 - count), (0, 128 - doc_lengths.shape[1])))
    piece = jnp.concatenate([piece, spans], axis=0).astype(BF)

    gathered = jax.ShapeDtypeStruct((tp, row_tokens, d), BF)
    own_f32 = jax.ShapeDtypeStruct((row_tokens, d), F32)
    own_bf = jax.ShapeDtypeStruct((row_tokens, d), BF)
    own_scratch = [pltpu.VMEM(own_f32.shape, F32), pltpu.VMEM(own_f32.shape, BF)]
    small = [pltpu.SemaphoreType.DMA((groups,))] * 2 + [pltpu.SemaphoreType.DMA((8,))] * 2
    normed_one, vec_rows, lengths = call(
        partial(first_kernel, hi, sh),
        [(tokens, False), (piece, False)],
        [
            (gathered, True),
            (jax.ShapeDtypeStruct((16, d), F32), False),
            (jax.ShapeDtypeStruct((8, 128), F32), False),
        ],
        [own_scratch[1], pltpu.VMEM((groups, 8, 16, 128), BF)] + small + gather_scratch(),
        1,
        50,
        "first_norm",
    )

    hc = heads * head
    units = inner * head
    middle, normed_two, cot_all, qkv, attended, mom_attn = call(
        partial(attention_kernel, hi, sh),
        [(normed_one, False), (w_attn, True), (lengths, False), (vec_rows, False), (tokens, False), (cotangent, True)]
        + [(send_attn, True)],
        [
            (own_f32, False),
            (gathered, True),
            (gathered, True),
            (jax.ShapeDtypeStruct((tp, row_tokens, 3 * hc), BF), False),
            (jax.ShapeDtypeStruct((t_all, hc), BF), False),
            (send_attn, True),
        ],
        own_scratch
        + [pltpu.VMEM((d, 4 * hc), BF), pltpu.SemaphoreType.DMA]
        + sum_scratch(row_tokens, d)
        + gather_scratch() * 2
        + swap_scratch(),
        2,
        120,
        "attention",
    )

    def rows_of(width):
        return (row_tokens, width), lambda r: (r, 0)

    def row_of(width):
        return (1, row_tokens, width), lambda r: (r, 0, 0)

    def fixed(array):
        return array.shape, lambda r: (0,) * array.ndim

    activated, grad_before, mom_mlp = call(
        partial(mlp_kernel, hi, sh),
        [(normed_two, row_of(d)), (cot_all, row_of(d)), (w_mlp, True), (vec_rows, fixed(vec_rows)), (send_mlp, True)],
        [(jax.ShapeDtypeStruct((t_all, units), BF), rows_of(units))] * 2 + [(send_mlp, True)],
        [pltpu.VMEM((d, units), BF)] * 2 + [pltpu.SemaphoreType.DMA((2,))] + swap_scratch(),
        7,
        30,
        "hidden_units",
        grid=(tp,),
    )

    def sent(stacked):
        return lax.psum_scatter(stacked, FS, scatter_dimension=0, tiled=False)

    s_down = outer([(cot_all, activated)], hi, sh, "grad_down")
    grad_before, s_down = lax.optimization_barrier((grad_before, s_down))
    s_up = outer([(normed_two, grad_before)], hi, sh, "grad_up")
    grad_before, s_down, s_up = lax.optimization_barrier((grad_before, s_down, s_up))
    g_down, g_up = sent(s_down), sent(s_up)

    grad_middle, sums_two, grad_branch, output = call(
        partial(branch_kernel, hi, sh),
        [(grad_before, False), (activated, False), (w_mlp, True), (middle, False), (cotangent, False), (vec_rows, False)],
        [(own_f32, False), (jax.ShapeDtypeStruct((4, 8, d), F32), False), (gathered, True), (own_bf, False)],
        own_scratch
        + [pltpu.VMEM((d, units), BF)] * 2
        + [pltpu.SemaphoreType.DMA((2,))]
        + sum_scratch(row_tokens, d)
        + gather_scratch()
        + sum_scratch(row_tokens, d),
        3,
        115,
        "second_norm_backward",
    )
    grad_branch, g_down = lax.optimization_barrier((grad_branch, g_down))
    g_down = g_down.reshape(tp, rows, -1)
    grad_joined, back_down = call(
        partial(attention_back_kernel, hi, sh),
        [(grad_branch, row_of(d)), (w_attn, True), (qkv, row_of(3 * hc)), (lengths, fixed(lengths)), (g_down, True)],
        [(jax.ShapeDtypeStruct((t_all, 3 * hc), BF), rows_of(3 * hc)), (g_down, True)],
        [pltpu.VMEM((d, hc), BF), pltpu.SemaphoreType.DMA] + swap_scratch(),
        8,
        25,
        "attention_backward",
        grid=(tp,),
    )
    s_attn = outer([(normed_one, grad_joined), (grad_branch, attended)], hi, sh, "grad_attention")
    grad_joined, s_attn = lax.optimization_barrier((grad_joined, s_attn))
    g_attn = sent(s_attn).reshape(send_attn.shape)
    g_up = g_up.reshape(tp, rows, -1)
    grad_tokens, sums_one, back_up, ortho_mlp = call(
        partial(last_kernel, hi, sh),
        [(grad_joined, False), (w_attn, True), (tokens, False), (grad_middle, False), (vec_rows, False)]
        + [(mom_mlp, False), (g_up, True), (g_down, True)],
        [(own_f32, False), (jax.ShapeDtypeStruct((2, 8, d), F32), False), (g_up, True), (send_mlp, True)],
        own_scratch[:1]
        + [pltpu.VMEM((d, 3 * hc), BF), pltpu.SemaphoreType.DMA]
        + [pltpu.VMEM(send_mlp.shape, BF), pltpu.SemaphoreType.DMA((2,)), pltpu.VMEM(send_mlp.shape, BF)]
        + sum_scratch(row_tokens, d)
        + ortho_scratch(groups, send_mlp.shape[2])
        + swap_scratch() * 2,
        4,
        85,
        "first_norm_backward",
    )
    grad_tokens, g_attn = lax.optimization_barrier((grad_tokens, g_attn))

    sums_two = jnp.sum(sums_two, axis=1)
    early = jnp.zeros((16, d), F32)
    for row, value in ((2, sums_two[:2]), (6, sums_two[2:])):
        early = lax.dynamic_update_slice(early, value, (row, 0))
    biases = jnp.sum(grad_joined, axis=0, dtype=F32)[None]
    early = lax.dynamic_update_slice(early, biases[:, :hc], (4, me * hc))
    early = lax.dynamic_update_slice(early, biases[:, 2 * hc :], (5, me * hc))
    each = d // units
    hidden = jnp.sum(grad_before, axis=0, dtype=F32)[None]
    early = lax.dynamic_update_slice(early, hidden, (8 + me // each, me % each * units))
    early, sums_one = lax.optimization_barrier((early, sums_one))

    back_attn, ortho_attn, vector_sums = call(
        partial(ortho_kernel, hi, sh),
        [(mom_attn, False), (g_attn, False), (early, False), (sums_one, False)],
        [(send_attn, True), (send_attn, True), (jax.ShapeDtypeStruct((16, 128), F32), False)],
        [pltpu.VMEM(send_attn.shape, BF)]
        + ortho_scratch(groups, send_attn.shape[2])
        + swap_scratch() * 2
        + terms_scratch(hi, sh, d),
        6,
        40,
        "orthogonalize_attention",
    )
    weight_grad, new_weights, moment_new = update(weights, momentum, back_attn, ortho_attn, back_up, back_down, ortho_mlp)

    spot = (flat % lanes) * rows
    vector_grad = lax.dynamic_slice(vector_sums, (0, spot), (16, rows))[:count].T
    first_moment = 0.9 * vector_moment + 0.1 * vector_grad
    second = 0.95 * vector_second + 0.05 * vector_grad * vector_grad
    corrected = first_moment / (1.0 - 0.9**STEP)
    normal_second = second / (1.0 - 0.95**STEP)
    next_vectors = vectors - 0.5 * corrected / (jnp.sqrt(normal_second) + 1e-08)
    return (
        output,
        grad_tokens,
        weight_grad,
        new_weights,
        moment_new,
        first_moment,
        second,
        next_vectors,
    )


def solution(mesh):
    dp, sh = mesh.shape["dp"], mesh.shape["shard"]
    tp = math.gcd(dp, 8)
    fine = Mesh(mesh.devices.reshape(dp // tp, tp, sh), ALL)
    two, three = P(ALL, None), P(ALL, None, None)
    return jax.shard_map(
        local,
        mesh=fine,
        in_specs=(two, two, three, three, two, two, two, two),
        out_specs=(two, two, three, three, three, two, two, two),
        check_vma=False,
    )
```
